32 devices in a mesh: dom: 8 (over y, x, core), pert: 4 (over z).
Axes of the slice: x: 2, y: 2, z: 4, core: 2. Of those that a mesh axis runs over, the one named last changes fastest.
Arguments:
- probes: float32 [64, 1024], P('pert', 'dom'), may hold values from -6 to 6
- melt_shape: float32 [65536], P('dom'), may hold values from 0.5 to 1.5
- obs_weight: float32 [65536], P('dom'), may hold values from 0.1 to 1
- diag_inverse: bfloat16 [1024, 64, 64], P('dom'), as said below
- coupling: bfloat16 [1024, 64, 256], P('dom'), may hold values from -0.25 to 0.25
- columns: int32 [1024, 4], P('dom'), may hold values from 0 to 191, as said below
- send_list: int32 [8, 4, 16], P('dom'), may hold values from -1 to 127, as said below
- patch_of_block: int32 [1024], P('dom'), may hold values from 0 to 1023, each once
Outputs:
- tangent: float32 [64, 65536], P('pert', 'dom')
- hessian_probe: float32 [64, 1024], P('pert', 'dom')
- hessian_diagonal: float32 [1024], P('dom')
The draws below stay inside these ranges and needn't reach their ends.
Inputs may be any that keep to these rules, and one draw needn't show every extreme that they name: send_list[d, j] lists distinct block numbers of partition d that it sends to partition d + o, o = (-2, -1, 1, 2)[j], in its first slots, and -1 in the others; a group whose target lies outside the partitions is empty, every other group fills at least half of its 16 slots, and some group fills all of them. `columns`: an entry below 128 names a block of the same partition; an entry at or above it names a filled interface slot as in the first step. `patch_of_block`: every parameter patch belongs to exactly one block row. `diag_inverse`: the inverse of the diagonal block of each block row.
All inputs are finite; a program needn't handle non-finite values.
Results may differ from the reference program's by a relative error of at most 0.0075.
Values may be sent and summed in bfloat16 or wider, within the bound.
No kernel may reach another device: no remote copies, remote signals or barrier semaphores. Data moves between devices by JAX's collectives and lax.ppermute only.
A program may use at most 64 MiB of HBM per device.

```python
import math
import jax
import jax.numpy as jnp
from jax import lax

BLOCK_ROWS = 64
OFF_BLOCKS = 4
CAPACITY = 16
SWEEPS = 4
LOCAL_BLOCKS = 128
PERT_LOCAL = 16
PARTITIONS = 8
BLOCKS_ALL = 1024
ROWS_ALL = 65536
PERTURBATIONS = 64


OFFSET_LIST = (-2, -1, 1, 2)


def interface_counts(key):
    base_key = jax.random.fold_in(key, 11)
    drawn = jax.random.randint(base_key, (PARTITIONS, 4), (CAPACITY + 1) // 2, CAPACITY + 1)
    drawn = drawn.at[0, 2].set(CAPACITY)
    drawn = drawn.at[0, 3].set(CAPACITY)
    sender = jnp.arange(PARTITIONS, dtype=jnp.int32)[:, None]
    target = sender + jnp.array(OFFSET_LIST, dtype=jnp.int32)[None, :]
    inside = (target >= 0) & (target < PARTITIONS)
    return jnp.where(inside, drawn, 0).astype(jnp.int32)


def draw_send_list(key, part):
    counts = interface_counts(key)
    order_key = jax.random.fold_in(key, 12)

    def one_list(list_index):
        shuffled = jax.random.permutation(jax.random.fold_in(order_key, list_index), LOCAL_BLOCKS)
        moved = (shuffled + (LOCAL_BLOCKS - 1 - shuffled[0])) % LOCAL_BLOCKS
        chosen = jnp.where(list_index == 2, moved, shuffled)
        return chosen[:CAPACITY]
    orders = jax.vmap(one_list)(jnp.arange(PARTITIONS * 4)).reshape(PARTITIONS, 4, CAPACITY)
    slot_ids = jnp.arange(CAPACITY, dtype=jnp.int32)[None, None, :]
    return jnp.where(slot_ids < counts[:, :, None], orders, -1).astype(jnp.int32)


def draw_columns(key, part):
    counts = interface_counts(key)
    offsets = jnp.array(OFFSET_LIST, dtype=jnp.int32)
    receiver = jnp.arange(PARTITIONS, dtype=jnp.int32)[:, None]
    source = receiver - offsets[None, :]
    inside = (source >= 0) & (source < PARTITIONS)
    group_ids = jnp.arange(4, dtype=jnp.int32)[None, :]
    ghost_counts = jnp.where(inside, counts[jnp.clip(source, 0, PARTITIONS - 1), group_ids], 0)
    slot_live = (jnp.arange(CAPACITY, dtype=jnp.int32)[None, None, :] < ghost_counts[:, :, None]).reshape(PARTITIONS, 4 * CAPACITY)
    local_pick = jax.random.randint(jax.random.fold_in(key, 13), (PARTITIONS, LOCAL_BLOCKS, OFF_BLOCKS), 0, LOCAL_BLOCKS)
    order_key = jax.random.fold_in(key, 14)

    def one_order(slot_index):
        return jax.random.permutation(jax.random.fold_in(order_key, slot_index), 4 * CAPACITY)
    slot_order = jax.vmap(one_order)(jnp.arange(PARTITIONS))
    half_cols = OFF_BLOCKS // 2
    remote_count = OFF_BLOCKS - half_cols
    row_ids = jnp.arange(LOCAL_BLOCKS, dtype=jnp.int32)
    columns_out = []
    for column_num in range(OFF_BLOCKS):
        if column_num < half_cols:
            columns_out.append(local_pick[:, :, column_num])
        else:
            position = (row_ids * remote_count + column_num - half_cols) % (4 * CAPACITY)
            slot_ids = slot_order[:, position]
            live_mask = jnp.take_along_axis(slot_live, slot_ids, axis=1)
            columns_out.append(jnp.where(live_mask, LOCAL_BLOCKS + slot_ids, local_pick[:, :, column_num]))
    return jnp.stack(columns_out, axis=2).reshape(BLOCKS_ALL, OFF_BLOCKS).astype(jnp.int32)


def draw_diag_inverse(key, part):
    noise = jax.random.normal(key, (BLOCKS_ALL, BLOCK_ROWS, BLOCK_ROWS), jnp.float32)
    row_ids = jnp.arange(BLOCK_ROWS)[:, None]
    col_ids = jnp.arange(BLOCK_ROWS)[None, :]
    identity = (row_ids == col_ids).astype(jnp.float32)
    return (0.6 * identity[None] + 0.6 / math.sqrt(BLOCK_ROWS) * noise).astype(jnp.bfloat16)


def shard_levels(own_key, extent, pieces, low, largest):
    def one(dim, parts):
        draws = jax.random.uniform(jax.random.fold_in(jax.random.fold_in(own_key, 6), dim), (parts,), jnp.float32, low / len(pieces), largest / len(pieces))
        return jnp.repeat(jnp.exp(draws), extent[dim] // parts).reshape((-1,) + (1,) * (len(extent) - dim - 1))

    gain = one(*pieces[0])
    for cut in pieces[1:]:
        gain = gain * one(*cut)
    return gain


def bell_draw(rng, dims, scale, most, pieces=(), kind=jnp.bfloat16):
    entries = scale * jax.random.normal(rng, dims, jnp.float32)
    if pieces:
        entries = entries * shard_levels(rng, dims, pieces, -0.22, 0.18)
    return jnp.clip(entries, -most, most).astype(kind)


def setup_inputs(seed: int = 0) -> dict:
    streams_of = jax.random.split(jax.random.key(seed), 9)
    return {
        "probes": bell_draw(streams_of[0], (PERTURBATIONS, BLOCKS_ALL), 1.0, 6.0, ((0, 4), (1, 8)), jnp.float32),
        "melt_shape": jnp.clip(0.5 + 1.0 * jax.random.uniform(streams_of[1], (ROWS_ALL,), jnp.float32) ** shard_levels(streams_of[1], (ROWS_ALL,), ((0, 8),), -0.2, 0.2), 0.5, 1.5),
        "obs_weight": jnp.clip(jnp.exp(math.log(1.0) - 2.3025851 * jax.random.uniform(streams_of[2], (ROWS_ALL,), jnp.float32) ** shard_levels(streams_of[2], (ROWS_ALL,), ((0, 8),), -0.2, 0.2)), 0.1, 1.0),
        "diag_inverse": draw_diag_inverse(jax.random.fold_in(streams_of[8], 71), 0),
        "coupling": bell_draw(streams_of[4], (BLOCKS_ALL, BLOCK_ROWS, OFF_BLOCKS * BLOCK_ROWS), (2 * OFF_BLOCKS * BLOCK_ROWS) ** -0.5, 0.25, ((0, 8),)),
        "columns": draw_columns(jax.random.fold_in(streams_of[8], 71), 0),
        "send_list": draw_send_list(jax.random.fold_in(streams_of[8], 71), 0),
        "patch_of_block": jax.random.permutation(streams_of[7], BLOCKS_ALL).astype(jnp.int32),
    }


OFFSET_LIST = (-2, -1, 1, 2)


def global_columns(columns, send_list):
    block_ids = jnp.arange(BLOCKS_ALL, dtype=jnp.int32)
    owner = block_ids // LOCAL_BLOCKS
    remote_slot = jnp.maximum(columns - LOCAL_BLOCKS, 0)
    group_ids = remote_slot // CAPACITY
    slot_pos = remote_slot % CAPACITY
    offsets = jnp.array(OFFSET_LIST, dtype=jnp.int32)
    source = jnp.clip(owner[:, None] - offsets[group_ids], 0, PARTITIONS - 1).astype(jnp.int32)
    entry = jnp.clip(send_list[source, group_ids, slot_pos], 0, LOCAL_BLOCKS - 1)
    remote = source * LOCAL_BLOCKS + entry
    local = owner[:, None] * LOCAL_BLOCKS + columns
    return jnp.where(columns < LOCAL_BLOCKS, local, remote).astype(jnp.int32)


def round_trip(values):
    return lax.optimization_barrier(values.astype(jnp.bfloat16)).astype(jnp.float32)


def reference(probes, melt_shape, obs_weight, diag_inverse, coupling, columns, send_list, patch_of_block):
    table = global_columns(columns, send_list).reshape(-1)
    couple_f = coupling.astype(jnp.float32)
    inverse_f = diag_inverse.astype(jnp.float32)
    melt = melt_shape.reshape(BLOCKS_ALL, BLOCK_ROWS)
    weight_obs = obs_weight.reshape(BLOCKS_ALL, BLOCK_ROWS)

    def one_slab(slab):
        forcing = melt[None] * slab[:, patch_of_block][:, :, None]
        tangent = jnp.zeros((PERT_LOCAL, BLOCKS_ALL, BLOCK_ROWS), jnp.float32)
        for sweep_num in range(SWEEPS):
            rounded = round_trip(tangent)
            gathered = rounded[:, table, :].reshape(PERT_LOCAL, BLOCKS_ALL, OFF_BLOCKS * BLOCK_ROWS)
            coupled = jnp.einsum("gik,pgk->pgi", couple_f, gathered)
            residual = round_trip(forcing - coupled)
            tangent = jnp.einsum("gij,pgj->pgi", inverse_f, residual)
        target = weight_obs[None] * tangent
        adjoint = jnp.zeros((PERT_LOCAL, BLOCKS_ALL, BLOCK_ROWS), jnp.float32)
        for sweep_num in range(SWEEPS):
            rounded = round_trip(adjoint)
            spread = jnp.einsum("gik,pgi->pgk", couple_f, rounded).reshape(PERT_LOCAL, BLOCKS_ALL * OFF_BLOCKS, BLOCK_ROWS)
            collected = jnp.zeros((PERT_LOCAL, BLOCKS_ALL, BLOCK_ROWS), jnp.float32).at[:, table].add(spread)
            residual = round_trip(target - collected)
            adjoint = jnp.einsum("gji,pgj->pgi", inverse_f, residual)
        block_sums = jnp.sum(melt[None] * adjoint, axis=2)
        products = jnp.zeros((PERT_LOCAL, BLOCKS_ALL), jnp.float32).at[:, patch_of_block].set(block_sums)
        return tangent.reshape(PERT_LOCAL, ROWS_ALL), products

    slabs = probes.reshape(PERTURBATIONS // PERT_LOCAL, PERT_LOCAL, BLOCKS_ALL)
    tangents, products = lax.map(one_slab, slabs)
    tangents = tangents.reshape(PERTURBATIONS, ROWS_ALL)
    hessian_probe = products.reshape(PERTURBATIONS, BLOCKS_ALL)
    hessian_diagonal = jnp.sum(probes * hessian_probe, axis=0) / PERTURBATIONS
    return tangents, hessian_probe, hessian_diagonal
```

```python
import functools

import jax
import jax.numpy as jnp
from jax import lax
from jax.experimental import pallas as pl
from jax.experimental.pallas import tpu as pltpu
from jax.sharding import PartitionSpec as P

OFFSET_LIST = (-2, -1, 1, 2)
F32 = jnp.float32
BF16 = jnp.bfloat16
LANES = 128
HALF = 64
QUAD = 4

VMEM = pl.BlockSpec(memory_space=pltpu.VMEM)
SMEM = pl.BlockSpec(memory_space=pltpu.SMEM)
PARAMS = pltpu.CompilerParams(vmem_limit_bytes=48 * 1024 * 1024)


def low_half(shape):
    return lax.broadcasted_iota(jnp.int32, shape, len(shape) - 1) < HALF


def swap_halves(value):
    return pltpu.roll(value, HALF, 1)


def rotated(value, by):
    peers = lax.axis_size("dom")
    return lax.ppermute(value, "dom", [(i, (i + by) % peers) for i in range(peers)])


def melt_kernel(send_ref, melt_ref, patch_ref, diag_ref, w_ref, *msg_refs):
    quads = diag_ref.shape[0] // QUAD
    sub = lax.broadcasted_iota(jnp.int32, (16, LANES), 0)
    low = low_half((1, LANES))

    def one(quad, _):
        row_a = melt_ref[pl.ds(2 * quad, 1), :]
        row_b = melt_ref[pl.ds(2 * quad + 1, 1), :]
        value = jnp.where(
            sub < 4,
            jnp.where(sub < 2, row_a, swap_halves(row_a)),
            jnp.where(sub < 6, row_b, swap_halves(row_b)),
        )
        top = value.astype(BF16).astype(F32)
        value = jnp.where(sub % 2 == 0, top, value - top)[:, :HALF].astype(BF16)
        blocks = diag_ref[pl.ds(quad * QUAD, QUAD)].reshape(QUAD * HALF, HALF)
        out = lax.dot_general(
            value, blocks, (((1,), (1,)), ((), ())), preferred_element_type=F32
        )
        first = out[:, :LANES]
        second = out[:, LANES:]
        w_ref[pl.ds(2 * quad, 1), :] = jnp.where(
            low, first[0:1] + first[1:2], first[2:3] + first[3:4]
        )
        w_ref[pl.ds(2 * quad + 1, 1), :] = jnp.where(
            low, second[4:5] + second[5:6], second[6:7] + second[7:8]
        )
        return 0

    lax.fori_loop(0, quads, one, 0, unroll=4)
    patch_row = patch_ref[...].astype(F32)
    lane = lax.broadcasted_iota(jnp.int32, (1, LANES), 1)
    capacity = send_ref.shape[2]
    for group, msg_ref in enumerate(msg_refs):
        ids = jnp.zeros((1, LANES), jnp.int32)
        for slot in range(capacity):
            block = jnp.maximum(send_ref[0, group, slot], 0)
            row = w_ref[pl.ds(block // 2, 1), :]
            msg_ref[slot : slot + 1, :] = jnp.where(
                low == (block % 2 == 0), row, swap_halves(row)
            )
            ids = jnp.where(lane == group * capacity + slot, block, ids)
        picked = jnp.take_along_axis(
            jnp.broadcast_to(patch_row, (8, LANES)), jnp.broadcast_to(ids, (8, LANES)), axis=1
        )
        mine = (lane >= group * capacity) & (lane < (group + 1) * capacity)
        msg_ref[capacity : capacity + 8, :] = jnp.where(mine, picked, 0.0)


def product_kernel(diag_ref, coupling_ref, m_ref):
    def one(block, _):
        m_ref[block] = jnp.dot(
            diag_ref[block], coupling_ref[block], preferred_element_type=F32
        ).astype(BF16)
        return 0

    lax.fori_loop(0, diag_ref.shape[0], one, 0, unroll=8)


def gather_multiply(quad, cols_ref, ext_ref, m_ref, low):
    rows = []
    for place in range(QUAD):
        g = quad * QUAD + place
        tiles = [ext_ref[cols_ref[g, k]] for k in range(4)]
        rows.append(
            jnp.concatenate(
                [jnp.where(low, tiles[0], tiles[1]), jnp.where(low, tiles[2], tiles[3])], axis=1
            )
        )
    lhs = jnp.concatenate(rows, axis=0)
    rhs = m_ref[pl.ds(quad * QUAD, QUAD)].reshape(QUAD * HALF, 4 * HALF)
    out = lax.dot_general(lhs, rhs, (((1,), (1,)), ((), ())), preferred_element_type=F32)
    p = out.shape[0] // QUAD
    first = jnp.where(low, out[:p, :LANES], out[p : 2 * p, :LANES])
    second = jnp.where(low, out[2 * p : 3 * p, LANES:], out[3 * p :, LANES:])
    return first, second


def store_pair(ref, pair, value, low):
    value = value.astype(BF16)
    other = swap_halves(value.astype(F32)).astype(BF16)
    ref[2 * pair] = jnp.where(low, value, other)
    ref[2 * pair + 1] = jnp.where(low, other, value)


def fill_messages(send_ref, ref, msg_refs):
    for group, msg_ref in enumerate(msg_refs):
        for slot in range(msg_ref.shape[0]):
            msg_ref[slot] = ref[jnp.maximum(send_ref[0, group, slot], 0)]


def first_kernel(
    cols_ref, send_ref, patch_ref, probe_ref, w_ref, g0, g1, g2, g3, m_ref,
    one_hot_ref, t1_ref, t2_ref, o0, o1, o2, o3, ext_ref,
):
    ghosts = (g0, g1, g2, g3)
    pert = probe_ref.shape[1]
    capacity = send_ref.shape[2]
    blocks = cols_ref.shape[0]
    low = low_half((pert, LANES))
    lane = lax.broadcasted_iota(jnp.int32, (1, LANES), 1)
    ghost_ids = g0[capacity : capacity + 1, :]
    for ref in ghosts[1:]:
        ghost_ids = ghost_ids + ref[capacity : capacity + 1, :]
    ghost_ids = jnp.where(lane < 4 * capacity, ghost_ids, -1.0)
    ids = jnp.concatenate([patch_ref[...].astype(F32), ghost_ids], axis=1)
    parts = probe_ref.shape[0]
    total = jnp.zeros((3 * pert, 2 * LANES), F32)
    for part in range(parts):
        names = (
            lax.broadcasted_iota(jnp.int32, (LANES, 2 * LANES), 0) + part * LANES
        ).astype(F32)
        hot = jnp.where(names == ids, 1.0, 0.0).astype(BF16)
        one_hot_ref[part * LANES : (part + 1) * LANES, :] = hot
        value = probe_ref[part]
        top = value.astype(BF16)
        rest = value - top.astype(F32)
        mid = rest.astype(BF16)
        last = (rest - mid.astype(F32)).astype(BF16)
        total = total + jnp.dot(
            jnp.concatenate([top, mid, last], axis=0), hot, preferred_element_type=F32
        )
    picked = total[:pert] + total[pert : 2 * pert] + total[2 * pert :]
    local_picked = picked[:, :LANES]
    ghost_picked = picked[:, LANES:]
    full_low = low.astype(jnp.int32)

    def seed(pair, _):
        index = 2 * pair + 1 - full_low
        spread = jnp.take_along_axis(local_picked, index, axis=1)
        value = spread * w_ref[pl.ds(pair, 1), :]
        t1_ref[pair] = value
        store_pair(ext_ref, pair, value, low)
        return 0

    lax.fori_loop(0, blocks // 2, seed, 0, unroll=4)
    for group, ref in enumerate(ghosts):
        for slot in range(capacity):
            place = group * capacity + slot
            spread = jnp.broadcast_to(ghost_picked[:, place : place + 1], (pert, LANES))
            ext_ref[blocks + place] = (spread * ref[slot : slot + 1, :]).astype(BF16)

    def sweep(quad, _):
        first, second = gather_multiply(quad, cols_ref, ext_ref, m_ref, low)
        store_pair(t2_ref, 2 * quad, t1_ref[2 * quad] - first, low)
        store_pair(t2_ref, 2 * quad + 1, t1_ref[2 * quad + 1] - second, low)
        return 0

    lax.fori_loop(0, blocks // QUAD, sweep, 0, unroll=2)
    fill_messages(send_ref, t2_ref, (o0, o1, o2, o3))


def extend(ext_ref, local_ref, ghosts):
    blocks = local_ref.shape[0]
    capacity = ghosts[0].shape[0]
    ext_ref[:blocks] = local_ref[...]
    for group, ref in enumerate(ghosts):
        ext_ref[blocks + group * capacity : blocks + (group + 1) * capacity] = ref[...]


def sweep_kernel(
    cols_ref, send_ref, t1_ref, prev_ref, g0, g1, g2, g3, m_ref,
    next_ref, o0, o1, o2, o3, ext_ref,
):
    low = low_half(prev_ref.shape[1:])
    extend(ext_ref, prev_ref, (g0, g1, g2, g3))

    def sweep(quad, _):
        first, second = gather_multiply(quad, cols_ref, ext_ref, m_ref, low)
        store_pair(next_ref, 2 * quad, t1_ref[2 * quad] - first, low)
        store_pair(next_ref, 2 * quad + 1, t1_ref[2 * quad + 1] - second, low)
        return 0

    lax.fori_loop(0, cols_ref.shape[0] // QUAD, sweep, 0, unroll=2)
    fill_messages(send_ref, next_ref, (o0, o1, o2, o3))


def clear(acc_refs):
    def one(place, _):
        for ref in acc_refs:
            ref[place] = jnp.zeros(ref.shape[1:], F32)
        return 0

    lax.fori_loop(0, acc_refs[0].shape[0], one, 0, unroll=4)


def multiply_scatter(quad, cols_ref, pairs, m_ref, acc_refs, low):
    zero = jnp.zeros(pairs[0].shape, F32)
    rows = []
    for place in range(QUAD):
        value = pairs[place // 2]
        kept = jnp.where(low, value, zero) if place % 2 == 0 else jnp.where(low, zero, value)
        tiles = [kept, zero] if place < 2 else [zero, kept]
        rows.append(jnp.concatenate(tiles, axis=1))
    lhs = jnp.concatenate(rows, axis=0).astype(BF16)
    rhs = m_ref[pl.ds(quad * QUAD, QUAD)].reshape(QUAD * HALF, 4 * HALF)
    out = jnp.dot(lhs, rhs, preferred_element_type=F32)
    p = pairs[0].shape[0]
    for place in range(QUAD):
        g = quad * QUAD + place
        for k in range(4):
            column = cols_ref[g, k]
            piece = out[place * p : (place + 1) * p, (k // 2) * LANES : (k // 2 + 1) * LANES]
            acc_refs[k][column] = acc_refs[k][column] + piece


def half_sums(acc_refs, place, low):
    return jnp.where(
        low, acc_refs[0][place] + acc_refs[2][place], acc_refs[1][place] + acc_refs[3][place]
    )


def pair_sum(acc_refs, pair, low):
    even = half_sums(acc_refs, 2 * pair, low)
    odd = half_sums(acc_refs, 2 * pair + 1, low)
    return jnp.where(low, even, odd) + swap_halves(jnp.where(low, odd, even))


def ghost_sum(acc_refs, place, low):
    value = half_sums(acc_refs, place, low)
    return value + swap_halves(value)


def finish_round(base_ref, target_ref, acc_refs, msg_refs, blocks, low):
    def local(pair, _):
        base_ref[pair] = target_ref[pair] - pair_sum(acc_refs, pair, low)
        return 0

    lax.fori_loop(0, blocks // 2, local, 0, unroll=4)
    for group, ref in enumerate(msg_refs):
        capacity = ref.shape[0]
        for slot in range(capacity):
            ref[slot] = ghost_sum(acc_refs, blocks + group * capacity + slot, low).astype(BF16)


def turn_kernel(
    cols_ref, t1_ref, prev_ref, g0, g1, g2, g3, m_ref, weight_ref,
    tangent_ref, target_ref, base_ref, o0, o1, o2, o3, ext_ref, *acc_refs,
):
    low = low_half(prev_ref.shape[1:])
    blocks = cols_ref.shape[0]
    extend(ext_ref, prev_ref, (g0, g1, g2, g3))
    clear(acc_refs)

    def sweep(quad, _):
        coupled = gather_multiply(quad, cols_ref, ext_ref, m_ref, low)
        pairs = []
        for place in range(2):
            pair = 2 * quad + place
            value = t1_ref[pair] - coupled[place]
            start = pl.multiple_of(pair * LANES, LANES)
            tangent_ref[:, pl.ds(start, LANES)] = value
            target = value * weight_ref[pl.ds(pair, 1), :]
            target_ref[pair] = target
            pairs.append(target)
        multiply_scatter(quad, cols_ref, pairs, m_ref, acc_refs, low)
        return 0

    lax.fori_loop(0, blocks // QUAD, sweep, 0, unroll=2)
    finish_round(base_ref, target_ref, acc_refs, (o0, o1, o2, o3), blocks, low)


def take_returned(send_ref, base_ref, u_ref, ghosts, low):
    u_ref[...] = base_ref[...]
    for group, ref in enumerate(ghosts):
        for slot in range(ref.shape[0]):
            block = send_ref[0, group, slot]
            pair = jnp.maximum(block, 0) // 2
            odd = block % 2
            wanted = jnp.where(block < 0, 2, odd)
            keep = (1 - low.astype(jnp.int32)) == wanted
            u_ref[pair] = u_ref[pair] - jnp.where(keep, ref[slot].astype(F32), 0.0)


def scatter_all(cols_ref, u_ref, m_ref, acc_refs, low):
    clear(acc_refs)

    def sweep(quad, _):
        pairs = [u_ref[2 * quad], u_ref[2 * quad + 1]]
        multiply_scatter(quad, cols_ref, pairs, m_ref, acc_refs, low)
        return 0

    lax.fori_loop(0, cols_ref.shape[0] // QUAD, sweep, 0, unroll=2)


def adjoint_kernel(
    cols_ref, send_ref, base_in_ref, target_ref, g0, g1, g2, g3, m_ref,
    base_ref, o0, o1, o2, o3, u_ref, *acc_refs,
):
    low = low_half(u_ref.shape[1:])
    take_returned(send_ref, base_in_ref, u_ref, (g0, g1, g2, g3), low)
    scatter_all(cols_ref, u_ref, m_ref, acc_refs, low)
    finish_round(base_ref, target_ref, acc_refs, (o0, o1, o2, o3), cols_ref.shape[0], low)


def last_kernel(
    cols_ref, send_ref, base_in_ref, target_ref, g0, g1, g2, g3, m_ref, w_ref, w0, w1, w2, w3,
    one_hot_ref, out_ref, u_ref, *acc_refs,
):
    pert = u_ref.shape[1]
    blocks = cols_ref.shape[0]
    low = low_half(u_ref.shape[1:])
    lane = lax.broadcasted_iota(jnp.int32, (pert, LANES), 1)
    take_returned(send_ref, base_in_ref, u_ref, (g0, g1, g2, g3), low)
    scatter_all(cols_ref, u_ref, m_ref, acc_refs, low)

    def local(pair, terms):
        value = (target_ref[pair] - pair_sum(acc_refs, pair, low)) * w_ref[pl.ds(pair, 1), :]
        even = jnp.sum(jnp.where(low, value, 0.0), axis=1, keepdims=True)
        odd = jnp.sum(jnp.where(low, 0.0, value), axis=1, keepdims=True)
        return jnp.where(lane == 2 * pair, even, jnp.where(lane == 2 * pair + 1, odd, terms))

    local_terms = lax.fori_loop(
        0, blocks // 2, local, jnp.zeros((pert, LANES), F32), unroll=4
    )
    ghost_terms = jnp.zeros((pert, LANES), F32)
    for group, ref in enumerate((w0, w1, w2, w3)):
        capacity = g0.shape[0]
        for slot in range(capacity):
            place = group * capacity + slot
            value = half_sums(acc_refs, blocks + place, low) * ref[slot : slot + 1, :]
            ghost_terms = jnp.where(
                lane == place, -jnp.sum(value, axis=1, keepdims=True), ghost_terms
            )
    terms = jnp.concatenate([local_terms, ghost_terms], axis=1)
    top = terms.astype(BF16)
    rest = (terms - top.astype(F32)).astype(BF16)
    both = jnp.concatenate([top, rest], axis=0)
    for part in range(out_ref.shape[0]):
        hot = one_hot_ref[part * LANES : (part + 1) * LANES, :]
        out = lax.dot_general(both, hot, (((1,), (1,)), ((), ())), preferred_element_type=F32)
        out_ref[part] = (out[:pert] + out[pert:]).astype(BF16)


def owner_kernel(terms_ref, probe_ref, hessian_ref, curve_ref):
    total = terms_ref[0].astype(F32)
    for part in range(1, terms_ref.shape[0]):
        total = total + terms_ref[part].astype(F32)
    hessian_ref[...] = total
    curve_ref[...] = jnp.broadcast_to(
        jnp.sum(total * probe_ref[...], axis=0, keepdims=True), curve_ref.shape
    )


def call(body, outs, spaces, scratch=(), name=None, flops=0, moved=1 << 20):
    return pl.pallas_call(
        body,
        out_shape=outs,
        in_specs=[SMEM if s == "s" else VMEM for s in spaces],
        out_specs=jax.tree.map(lambda _: VMEM, outs),
        scratch_shapes=list(scratch),
        compiler_params=PARAMS,
        name=name,
        cost_estimate=pl.CostEstimate(flops=flops, transcendentals=0, bytes_accessed=moved),
    )


def shards(
    probes, melt_shape, obs_weight, diag_inverse, coupling, columns, send_list, patch_of_block
):
    pert = probes.shape[0]
    blocks = coupling.shape[0]
    capacity = send_list.shape[2]
    parts = lax.axis_size("dom")
    pairs = blocks // 2
    shape = jax.ShapeDtypeStruct
    msgs = [shape((capacity, pert, LANES), BF16)] * 4
    pair_array = shape((pairs, pert, LANES), F32)
    block_array = shape((blocks, pert, LANES), BF16)
    ext = pltpu.VMEM((blocks + 4 * capacity, pert, LANES), BF16)
    accs = [pltpu.VMEM((blocks + 4 * capacity, pert, LANES), F32)] * 4
    held = pltpu.VMEM((pairs, pert, LANES), F32)
    melt = melt_shape.reshape(pairs, LANES)
    weight = obs_weight.reshape(pairs, LANES)
    patch = patch_of_block.reshape(1, blocks)

    spread = lax.all_to_all(
        jnp.broadcast_to(probes[None], (parts,) + probes.shape), "dom", 0, 0, tiled=True
    )
    w, *w_msgs = call(
        melt_kernel,
        [shape((pairs, LANES), F32)] + [shape((capacity + 8, LANES), F32)] * 4,
        "svvv",
        name="melt",
    )(send_list, melt, patch, diag_inverse)
    w_ghosts = [rotated(m, o) for m, o in zip(w_msgs, OFFSET_LIST)]
    m = call(
        product_kernel, shape(coupling.shape, BF16), "vv", name="product", flops=1 << 28, moved=10 << 20
    )(diag_inverse, coupling)

    one_hot, t1, state, *out = call(
        first_kernel,
        [shape((parts * probes.shape[1], 2 * LANES), BF16), pair_array, block_array] + msgs,
        "ssvvvvvvvv",
        [ext],
        name="first",
    )(columns, send_list, patch, spread, w, *w_ghosts, m)
    ghosts = [rotated(v, o) for v, o in zip(out, OFFSET_LIST)]
    state, *out = call(
        sweep_kernel, [block_array] + msgs, "ssvvvvvvv", [ext], name="sweep"
    )(columns, send_list, t1, state, *ghosts, m)
    ghosts = [rotated(v, o) for v, o in zip(out, OFFSET_LIST)]
    tangent, target, base, *out = call(
        turn_kernel,
        [shape((pert, blocks * HALF), F32), pair_array, pair_array] + msgs,
        "svvvvvvvv",
        [ext] + accs,
        name="turn",
    )(columns, t1, state, *ghosts, m, weight)
    ghosts = [rotated(v, -o) for v, o in zip(out, OFFSET_LIST)]
    base, *out = call(
        adjoint_kernel, [pair_array] + msgs, "ssvvvvvvv", [held] + accs, name="adjoint"
    )(columns, send_list, base, target, *ghosts, m)
    ghosts = [rotated(v, -o) for v, o in zip(out, OFFSET_LIST)]
    terms = call(
        last_kernel,
        shape((parts, pert, LANES), BF16),
        "ssvvvvvvvvvvvvv",
        [held] + accs,
        name="last",
    )(columns, send_list, base, target, *ghosts, m, w, *w_ghosts, one_hot)
    terms = lax.all_to_all(terms, "dom", 0, 0, tiled=True)
    hessian_probe, curve = call(
        owner_kernel, [shape(probes.shape, F32), shape((8, LANES), F32)], "vv", name="owner"
    )(terms, probes)
    perts = lax.axis_size("pert")
    curvature = jnp.sum(lax.all_gather(curve[0], "pert", axis=0), axis=0)
    return tangent, hessian_probe, curvature / (pert * perts)


def solution(mesh):
    in_specs = (
        P("pert", "dom"),
        P("dom"),
        P("dom"),
        P("dom", None, None),
        P("dom", None, None),
        P("dom", None),
        P("dom", None, None),
        P("dom"),
    )
    out_specs = (P("pert", "dom"), P("pert", "dom"), P("dom"))
    return jax.shard_map(shards, mesh=mesh, in_specs=in_specs, out_specs=out_specs, check_vma=False)
```

```python
import functools

import jax
import jax.numpy as jnp
from jax import lax
from jax.experimental import pallas as pl
from jax.experimental.pallas import tpu as pltpu
from jax.sharding import PartitionSpec as P

OFFSET_LIST = (-2, -1, 1, 2)
F32 = jnp.float32
BF16 = jnp.bfloat16
LANES = 128
HALF = 64
QUAD = 4

VMEM = pl.BlockSpec(memory_space=pltpu.VMEM)
SMEM = pl.BlockSpec(memory_space=pltpu.SMEM)
PARAMS = pltpu.CompilerParams(vmem_limit_bytes=16 * 1024 * 1024)


def low_half(shape):
    return lax.broadcasted_iota(jnp.int32, shape, len(shape) - 1) < HALF


def swap_halves(value):
    return pltpu.roll(value, HALF, 1)


def rotated(value, by):
    peers = lax.axis_size("dom")
    return lax.ppermute(value, "dom", [(i, (i + by) % peers) for i in range(peers)])


def neighbours(parts):
    me = lax.axis_index("dom")
    return [lax.rem(me - offset + parts, parts) for offset in OFFSET_LIST]


def melt_kernel(send_ref, melt_ref, patch_ref, probe_ref, diag_ref, w_ref, out_ref, *, parts):
    pairs = melt_ref.shape[0]
    pert = probe_ref.shape[0]
    capacity = send_ref.shape[2]
    low = low_half((1, LANES))
    lane = lax.broadcasted_iota(jnp.int32, (HALF, LANES), 1)
    turned = jnp.transpose(jnp.concatenate([melt_ref[...], jnp.zeros((LANES - pairs, LANES), F32)], axis=0))
    even = jnp.take_along_axis(turned[:HALF], lane // 2, axis=1)
    odd = jnp.take_along_axis(turned[HALF:], lane // 2, axis=1)
    melt = jnp.where(lane % 2 == 0, even, odd)
    sums = [
        jnp.sum(diag_ref[i].astype(F32) * melt, axis=0, keepdims=True)
        for i in range(diag_ref.shape[0])
    ]
    sums = jnp.concatenate(sums, axis=0)
    source = 2 * (lane % HALF)
    both = jnp.concatenate(
        [
            jnp.take_along_axis(sums, source, axis=1),
            jnp.take_along_axis(sums, source + 1, axis=1),
        ],
        axis=0,
    )
    w_ref[...] = jnp.transpose(both)[:pairs]
    patch_row = jnp.broadcast_to(patch_ref[...].astype(F32), (8, LANES))
    lane = lax.broadcasted_iota(jnp.int32, (8, LANES), 1)
    for part in range(parts):
        out_ref[part, :pert] = probe_ref[...]
    me = lax.axis_index("dom")
    for group, offset in enumerate(OFFSET_LIST):
        to = lax.rem(me + offset + parts, parts)
        ids = jnp.zeros((8, LANES), jnp.int32)
        for slot in range(capacity):
            block = jnp.maximum(send_ref[0, group, slot], 0)
            row = w_ref[pl.ds(block // 2, 1), :]
            out_ref[to, pert + slot : pert + slot + 1, :] = jnp.where(
                low == (block % 2 == 0), row, swap_halves(row)
            )
            ids = jnp.where(lane == group * capacity + slot, block, ids)
        mine = (lane >= group * capacity) & (lane < (group + 1) * capacity)
        out_ref[to, pert + capacity :, :] = jnp.where(
            mine, jnp.take_along_axis(patch_row, ids, axis=1), 0.0
        )


def product_kernel(diag_ref, coupling_ref, m_ref):
    def one(block, _):
        m_ref[block] = jnp.dot(
            diag_ref[block], coupling_ref[block], preferred_element_type=F32
        ).astype(BF16)
        return 0

    lax.fori_loop(0, diag_ref.shape[0], one, 0, unroll=32)


def gather_multiply(quad, cols_ref, ext_ref, m_ref, low):
    rows = []
    for place in range(QUAD):
        g = quad * QUAD + place
        tiles = [ext_ref[cols_ref[k, g]] for k in range(4)]
        rows.append(
            jnp.concatenate(
                [jnp.where(low, tiles[0], tiles[1]), jnp.where(low, tiles[2], tiles[3])], axis=1
            )
        )
    lhs = jnp.concatenate(rows, axis=0)
    rhs = m_ref[pl.ds(quad * QUAD, QUAD)].reshape(QUAD * HALF, 4 * HALF)
    out = lax.dot_general(lhs, rhs, (((1,), (1,)), ((), ())), preferred_element_type=F32)
    p = out.shape[0] // QUAD
    first = jnp.where(low, out[:p, :LANES], out[p : 2 * p, :LANES])
    second = jnp.where(low, out[2 * p : 3 * p, LANES:], out[3 * p :, LANES:])
    return first, second


def store_pair(ref, pair, value, low):
    value = value.astype(BF16)
    other = swap_halves(value.astype(F32)).astype(BF16)
    ref[2 * pair] = jnp.where(low, value, other)
    ref[2 * pair + 1] = jnp.where(low, other, value)


def fill_messages(send_ref, ref, msg_refs, low):
    for group, msg_ref in enumerate(msg_refs):
        for pair in range(msg_ref.shape[0]):
            even, odd = (
                ref[jnp.maximum(send_ref[0, group, 2 * pair + half], 0)] for half in range(2)
            )
            msg_ref[pair] = jnp.where(low, even, odd)


def first_kernel(
    cols_ref, send_ref, patch_ref, got_ref, w_ref, m_ref,
    one_hot_ref, t1_ref, t2_ref, o0, o1, o2, o3, ext_ref,
):
    pert = t1_ref.shape[1]
    capacity = send_ref.shape[2]
    blocks = cols_ref.shape[1]
    parts = got_ref.shape[0]
    sources = neighbours(parts)
    low = low_half((pert, LANES))
    lane = lax.broadcasted_iota(jnp.int32, (1, LANES), 1)
    ghost_ids = sum(got_ref[source, pert + capacity : pert + capacity + 1, :] for source in sources)
    ghost_ids = jnp.where(lane < 4 * capacity, ghost_ids, -1.0)
    ids = jnp.concatenate([patch_ref[...].astype(F32), ghost_ids], axis=1)
    total = jnp.zeros((3 * pert, 2 * LANES), F32)
    for part in range(parts):
        names = (
            lax.broadcasted_iota(jnp.int32, (LANES, 2 * LANES), 0) + part * LANES
        ).astype(F32)
        hot = jnp.where(names == ids, 1.0, 0.0).astype(BF16)
        one_hot_ref[part * LANES : (part + 1) * LANES, :] = hot
        value = got_ref[part, :pert]
        top = value.astype(BF16)
        rest = value - top.astype(F32)
        mid = rest.astype(BF16)
        last = (rest - mid.astype(F32)).astype(BF16)
        total = total + jnp.dot(
            jnp.concatenate([top, mid, last], axis=0), hot, preferred_element_type=F32
        )
    picked = total[:pert] + total[pert : 2 * pert] + total[2 * pert :]
    local_picked = picked[:, :LANES]
    ghost_picked = picked[:, LANES:]
    full_low = low.astype(jnp.int32)

    def seed(pair, _):
        index = 2 * pair + 1 - full_low
        spread = jnp.take_along_axis(local_picked, index, axis=1)
        value = spread * w_ref[pl.ds(pair, 1), :]
        t1_ref[pair] = value
        store_pair(ext_ref, pair, value, low)
        return 0

    lax.fori_loop(0, blocks // 2, seed, 0, unroll=16)
    for group, source in enumerate(sources):
        for slot in range(capacity):
            place = group * capacity + slot
            row = got_ref[source, pert + slot : pert + slot + 1, :]
            spread = jnp.broadcast_to(ghost_picked[:, place : place + 1], (pert, LANES))
            ext_ref[blocks + place] = (spread * row).astype(BF16)

    def sweep(quad, _):
        first, second = gather_multiply(quad, cols_ref, ext_ref, m_ref, low)
        store_pair(t2_ref, 2 * quad, t1_ref[2 * quad] - first, low)
        store_pair(t2_ref, 2 * quad + 1, t1_ref[2 * quad + 1] - second, low)
        return 0

    lax.fori_loop(0, blocks // QUAD, sweep, 0, unroll=32)
    fill_messages(send_ref, t2_ref, (o0, o1, o2, o3), low)


def extend(ext_ref, local_ref, ghosts, low):
    blocks = local_ref.shape[0]
    count = ghosts[0].shape[0]
    ext_ref[:blocks] = local_ref[...]
    for group, ref in enumerate(ghosts):
        for pair in range(count):
            store_pair(ext_ref, blocks // 2 + group * count + pair, ref[pair], low)


def sweep_kernel(
    cols_ref, send_ref, t1_ref, prev_ref, g0, g1, g2, g3, m_ref,
    next_ref, o0, o1, o2, o3, ext_ref,
):
    low = low_half(prev_ref.shape[1:])
    extend(ext_ref, prev_ref, (g0, g1, g2, g3), low)

    def sweep(quad, _):
        first, second = gather_multiply(quad, cols_ref, ext_ref, m_ref, low)
        store_pair(next_ref, 2 * quad, t1_ref[2 * quad] - first, low)
        store_pair(next_ref, 2 * quad + 1, t1_ref[2 * quad + 1] - second, low)
        return 0

    lax.fori_loop(0, cols_ref.shape[1] // QUAD, sweep, 0, unroll=32)
    fill_messages(send_ref, next_ref, (o0, o1, o2, o3), low)


def clear(acc_refs):
    def one(place, _):
        for ref in acc_refs:
            ref[place] = jnp.zeros(ref.shape[1:], F32)
        return 0

    lax.fori_loop(0, acc_refs[0].shape[0], one, 0, unroll=16)


def multiply_scatter(quad, cols_ref, pairs, m_ref, acc_refs, low):
    zero = jnp.zeros(pairs[0].shape, F32)
    rows = []
    for place in range(QUAD):
        value = pairs[place // 2]
        kept = jnp.where(low, value, zero) if place % 2 == 0 else jnp.where(low, zero, value)
        tiles = [kept, zero] if place < 2 else [zero, kept]
        rows.append(jnp.concatenate(tiles, axis=1))
    lhs = jnp.concatenate(rows, axis=0).astype(BF16)
    rhs = m_ref[pl.ds(quad * QUAD, QUAD)].reshape(QUAD * HALF, 4 * HALF)
    out = jnp.dot(lhs, rhs, preferred_element_type=F32)
    p = pairs[0].shape[0]
    for place in range(QUAD):
        g = quad * QUAD + place
        for k in range(4):
            column = cols_ref[k, g]
            piece = out[place * p : (place + 1) * p, (k // 2) * LANES : (k // 2 + 1) * LANES]
            acc_refs[k][column] = acc_refs[k][column] + piece


def half_sums(acc_refs, place, low):
    return jnp.where(
        low, acc_refs[0][place] + acc_refs[2][place], acc_refs[1][place] + acc_refs[3][place]
    )


def pair_sum(acc_refs, pair, low):
    even = half_sums(acc_refs, 2 * pair, low)
    odd = half_sums(acc_refs, 2 * pair + 1, low)
    return jnp.where(low, even, odd) + swap_halves(jnp.where(low, odd, even))


def finish_round(base_ref, target_ref, acc_refs, msg_refs, blocks, low):
    def local(pair, _):
        base_ref[pair] = target_ref[pair] - pair_sum(acc_refs, pair, low)
        return 0

    lax.fori_loop(0, blocks // 2, local, 0, unroll=16)
    for group, ref in enumerate(msg_refs):
        count = ref.shape[0]
        for pair in range(count):
            ref[pair] = pair_sum(acc_refs, blocks // 2 + group * count + pair, low).astype(BF16)


def turn_kernel(
    cols_ref, t1_ref, prev_ref, g0, g1, g2, g3, m_ref, weight_ref,
    tangent_ref, target_ref, base_ref, o0, o1, o2, o3, ext_ref, *acc_refs,
):
    low = low_half(prev_ref.shape[1:])
    blocks = cols_ref.shape[1]
    extend(ext_ref, prev_ref, (g0, g1, g2, g3), low)
    clear(acc_refs)

    def sweep(quad, _):
        coupled = gather_multiply(quad, cols_ref, ext_ref, m_ref, low)
        pairs = []
        for place in range(2):
            pair = 2 * quad + place
            value = t1_ref[pair] - coupled[place]
            start = pl.multiple_of(pair * LANES, LANES)
            tangent_ref[:, pl.ds(start, LANES)] = value
            target = value * weight_ref[pl.ds(pair, 1), :]
            target_ref[pair] = target
            pairs.append(target)
        multiply_scatter(quad, cols_ref, pairs, m_ref, acc_refs, low)
        return 0

    lax.fori_loop(0, blocks // QUAD, sweep, 0, unroll=32)
    finish_round(base_ref, target_ref, acc_refs, (o0, o1, o2, o3), blocks, low)


def take_returned(send_ref, base_ref, u_ref, ghosts, low):
    u_ref[...] = base_ref[...]
    which = 1 - low.astype(jnp.int32)
    for group, ref in enumerate(ghosts):
        for pair in range(ref.shape[0]):
            value = ref[pair].astype(F32)
            other = swap_halves(value)
            for half, both in enumerate(
                (jnp.where(low, value, other), jnp.where(low, other, value))
            ):
                block = send_ref[0, group, 2 * pair + half]
                place = jnp.maximum(block, 0) // 2
                wanted = jnp.where(block < 0, 2, block % 2)
                u_ref[place] = u_ref[place] - jnp.where(which == wanted, both, 0.0)


def scatter_all(cols_ref, u_ref, m_ref, acc_refs, low):
    clear(acc_refs)

    def sweep(quad, _):
        pairs = [u_ref[2 * quad], u_ref[2 * quad + 1]]
        multiply_scatter(quad, cols_ref, pairs, m_ref, acc_refs, low)
        return 0

    lax.fori_loop(0, cols_ref.shape[1] // QUAD, sweep, 0, unroll=32)


def adjoint_kernel(
    cols_ref, send_ref, base_in_ref, target_ref, g0, g1, g2, g3, m_ref,
    base_ref, o0, o1, o2, o3, u_ref, *acc_refs,
):
    low = low_half(u_ref.shape[1:])
    take_returned(send_ref, base_in_ref, u_ref, (g0, g1, g2, g3), low)
    scatter_all(cols_ref, u_ref, m_ref, acc_refs, low)
    finish_round(base_ref, target_ref, acc_refs, (o0, o1, o2, o3), cols_ref.shape[1], low)


def last_kernel(
    cols_ref, send_ref, base_in_ref, target_ref, g0, g1, g2, g3, m_ref, w_ref, got_ref,
    one_hot_ref, out_ref, u_ref, *acc_refs,
):
    pert = u_ref.shape[1]
    blocks = cols_ref.shape[1]
    low = low_half(u_ref.shape[1:])
    lane = lax.broadcasted_iota(jnp.int32, (pert, LANES), 1)
    take_returned(send_ref, base_in_ref, u_ref, (g0, g1, g2, g3), low)
    scatter_all(cols_ref, u_ref, m_ref, acc_refs, low)

    def local(pair, terms):
        value = (target_ref[pair] - pair_sum(acc_refs, pair, low)) * w_ref[pl.ds(pair, 1), :]
        even = jnp.sum(jnp.where(low, value, 0.0), axis=1, keepdims=True)
        odd = jnp.sum(jnp.where(low, 0.0, value), axis=1, keepdims=True)
        return jnp.where(lane == 2 * pair, even, jnp.where(lane == 2 * pair + 1, odd, terms))

    local_terms = lax.fori_loop(
        0, blocks // 2, local, jnp.zeros((pert, LANES), F32), unroll=4
    )
    ghost_terms = jnp.zeros((pert, LANES), F32)
    parts = got_ref.shape[0]
    capacity = send_ref.shape[2]
    for group, source in enumerate(neighbours(parts)):
        for slot in range(capacity):
            place = group * capacity + slot
            row = got_ref[source, pert + slot : pert + slot + 1, :]
            value = half_sums(acc_refs, blocks + place, low) * row
            ghost_terms = jnp.where(
                lane == place, -jnp.sum(value, axis=1, keepdims=True), ghost_terms
            )
    terms = jnp.concatenate([local_terms, ghost_terms], axis=1)
    top = terms.astype(BF16)
    rest = (terms - top.astype(F32)).astype(BF16)
    both = jnp.concatenate([top, rest], axis=0)
    perts = out_ref.shape[0] // parts
    sub = lax.broadcasted_iota(jnp.int32, (8, LANES), 0)
    for part in range(parts):
        hot = one_hot_ref[part * LANES : (part + 1) * LANES, :]
        out = lax.dot_general(both, hot, (((1,), (1,)), ((), ())), preferred_element_type=F32)
        value = out[:pert] + out[pert:]
        curve = jnp.sum(value * got_ref[part, :pert], axis=0, keepdims=True)
        top = curve.astype(BF16).astype(F32)
        extra = jnp.where(sub == 0, top, jnp.where(sub == 1, curve - top, 0.0))
        for place in range(perts):
            out_ref[part * perts + place, :pert] = value.astype(BF16)
            out_ref[part * perts + place, pert:] = extra.astype(BF16)


def owner_kernel(terms_ref, hessian_ref, curve_ref, *, parts, scale):
    pert = hessian_ref.shape[0]
    perts = terms_ref.shape[0] // parts
    mine = lax.axis_index("pert")
    total = jnp.zeros(hessian_ref.shape, F32)
    for part in range(parts):
        total = total + terms_ref[part * perts + mine, :pert].astype(F32)
    hessian_ref[...] = total
    curve = jnp.zeros((8, LANES), F32)
    for place in range(terms_ref.shape[0]):
        curve = curve + terms_ref[place, pert:].astype(F32)
    curve_ref[...] = (curve[0:1] + curve[1:2]) * scale


def call(body, outs, spaces, scratch=(), name=None, flops=0, moved=1 << 20):
    return pl.pallas_call(
        body,
        out_shape=outs,
        in_specs=[SMEM if s == "s" else VMEM for s in spaces],
        out_specs=jax.tree.map(lambda _: VMEM, outs),
        scratch_shapes=list(scratch),
        compiler_params=PARAMS,
        name=name,
        cost_estimate=pl.CostEstimate(flops=flops, transcendentals=0, bytes_accessed=moved),
    )


def shards(
    probes, melt_shape, obs_weight, diag_inverse, coupling, columns, send_list, patch_of_block
):
    pert = probes.shape[0]
    blocks = coupling.shape[0]
    capacity = send_list.shape[2]
    parts = lax.axis_size("dom")
    pairs = blocks // 2
    shape = jax.ShapeDtypeStruct
    msgs = [shape((capacity // 2, pert, LANES), BF16)] * 4
    pair_array = shape((pairs, pert, LANES), F32)
    block_array = shape((blocks, pert, LANES), BF16)
    ext = pltpu.VMEM((blocks + 4 * capacity, pert, LANES), BF16)
    accs = [pltpu.VMEM((blocks + 4 * capacity, pert, LANES), F32)] * 4
    held = pltpu.VMEM((pairs, pert, LANES), F32)
    melt = melt_shape.reshape(pairs, LANES)
    weight = obs_weight.reshape(pairs, LANES)
    patch = patch_of_block.reshape(1, blocks)

    perts = lax.axis_size("pert")
    columns = columns.T
    w, outgoing = call(
        functools.partial(melt_kernel, parts=parts),
        [shape((pairs, LANES), F32), shape((parts, pert + capacity + 8, LANES), F32)],
        "svvvv",
        name="melt",
    )(send_list, melt, patch, probes, jnp.transpose(diag_inverse, (1, 2, 0)))
    got = lax.all_to_all(outgoing, "dom", 0, 0, tiled=True)
    m = call(
        product_kernel, shape(coupling.shape, BF16), "vv", name="product", flops=1 << 28, moved=10 << 20
    )(diag_inverse, coupling)

    one_hot, t1, state, *out = call(
        first_kernel,
        [shape((parts * probes.shape[1], 2 * LANES), BF16), pair_array, block_array] + msgs,
        "ssvvvv",
        [ext],
        name="first",
    )(columns, send_list, patch, got, w, m)
    ghosts = [rotated(v, o) for v, o in zip(out, OFFSET_LIST)]
    state, *out = call(
        sweep_kernel, [block_array] + msgs, "ssvvvvvvv", [ext], name="sweep"
    )(columns, send_list, t1, state, *ghosts, m)
    ghosts = [rotated(v, o) for v, o in zip(out, OFFSET_LIST)]
    tangent, target, base, *out = call(
        turn_kernel,
        [shape((pert, blocks * HALF), F32), pair_array, pair_array] + msgs,
        "svvvvvvvv",
        [ext] + accs,
        name="turn",
    )(columns, t1, state, *ghosts, m, weight)
    ghosts = [rotated(v, -o) for v, o in zip(out, OFFSET_LIST)]
    base, *out = call(
        adjoint_kernel, [pair_array] + msgs, "ssvvvvvvv", [held] + accs, name="adjoint"
    )(columns, send_list, base, target, *ghosts, m)
    ghosts = [rotated(v, -o) for v, o in zip(out, OFFSET_LIST)]
    terms = call(
        last_kernel,
        shape((parts * perts, pert + 8, LANES), BF16),
        "ssvvvvvvvvvv",
        [held] + accs,
        name="last",
    )(columns, send_list, base, target, *ghosts, m, w, got, one_hot)
    terms = lax.all_to_all(terms, ("dom", "pert"), 0, 0, tiled=True)
    hessian_probe, curvature = call(
        functools.partial(owner_kernel, parts=parts, scale=1.0 / (pert * perts)),
        [shape(probes.shape, F32), shape((1, LANES), F32)],
        "v",
        name="owner",
    )(terms)
    return tangent, hessian_probe, curvature.reshape(-1)


def solution(mesh):
    in_specs = (
        P("pert", "dom"),
        P("dom"),
        P("dom"),
        P("dom", None, None),
        P("dom", None, None),
        P("dom", None),
        P("dom", None, None),
        P("dom"),
    )
    out_specs = (P("pert", "dom"), P("pert", "dom"), P("dom"))
    return jax.shard_map(shards, mesh=mesh, in_specs=in_specs, out_specs=out_specs, check_vma=False)
```

```python
import functools

import jax
import jax.numpy as jnp
from jax import lax
from jax.experimental import pallas as pl
from jax.experimental.pallas import tpu as pltpu
from jax.sharding import PartitionSpec as P

OFFSET_LIST = (-2, -1, 1, 2)
F32 = jnp.float32
BF16 = jnp.bfloat16
LANES = 128
HALF = 64
QUAD = 4

VMEM = pl.BlockSpec(memory_space=pltpu.VMEM)
SMEM = pl.BlockSpec(memory_space=pltpu.SMEM)
HBM = pl.BlockSpec(memory_space=pltpu.HBM)
MIB = 1024 * 1024


def low_half(shape):
    return lax.broadcasted_iota(jnp.int32, shape, len(shape) - 1) < HALF


def swap_halves(value):
    return pltpu.roll(value, HALF, 1)


def rotated(value, by):
    peers = lax.axis_size("dom")
    return lax.ppermute(value, "dom", [(i, (i + by) % peers) for i in range(peers)])


def neighbours(parts):
    me = lax.axis_index("dom")
    return [lax.rem(me - offset + parts, parts) for offset in OFFSET_LIST]


def melt_kernel(
    send_hbm, melt_hbm, patch_hbm, probe_hbm, diag_hbm, w_ref, out_ref,
    send_ref, melt_ref, patch_ref, probe_ref, diag_ref, sems, *, parts,
):
    copies = [
        pltpu.make_async_copy(source, target, sems.at[number])
        for number, (source, target) in enumerate(
            (
                (diag_hbm, diag_ref),
                (melt_hbm, melt_ref),
                (patch_hbm, patch_ref),
                (probe_hbm, probe_ref),
                (send_hbm, send_ref),
            )
        )
    ]
    for copy in copies:
        copy.start()
    for copy in copies:
        copy.wait()
    pairs = melt_ref.shape[0]
    pert = probe_ref.shape[0]
    capacity = send_ref.shape[2]
    low = low_half((1, LANES))
    lane = lax.broadcasted_iota(jnp.int32, (HALF, LANES), 1)
    turned = jnp.transpose(jnp.concatenate([melt_ref[...], jnp.zeros((LANES - pairs, LANES), F32)], axis=0))
    even = jnp.take_along_axis(turned[:HALF], lane // 2, axis=1)
    odd = jnp.take_along_axis(turned[HALF:], lane // 2, axis=1)
    melt = jnp.where(lane % 2 == 0, even, odd)
    sums = [
        jnp.sum(diag_ref[i].astype(F32) * melt, axis=0, keepdims=True)
        for i in range(diag_ref.shape[0])
    ]
    sums = jnp.concatenate(sums, axis=0)
    source = 2 * (lane % HALF)
    both = jnp.concatenate(
        [
            jnp.take_along_axis(sums, source, axis=1),
            jnp.take_along_axis(sums, source + 1, axis=1),
        ],
        axis=0,
    )
    w_ref[...] = jnp.transpose(both)[:pairs]
    patch_row = jnp.broadcast_to(patch_ref[...].astype(F32), (8, LANES))
    lane = lax.broadcasted_iota(jnp.int32, (8, LANES), 1)
    for part in range(parts):
        out_ref[part, :pert] = probe_ref[...]
    me = lax.axis_index("dom")
    for group, offset in enumerate(OFFSET_LIST):
        to = lax.rem(me + offset + parts, parts)
        ids = jnp.zeros((8, LANES), jnp.int32)
        for slot in range(capacity):
            block = jnp.maximum(send_ref[0, group, slot], 0)
            row = w_ref[pl.ds(block // 2, 1), :]
            out_ref[to, pert + slot : pert + slot + 1, :] = jnp.where(
                low == (block % 2 == 0), row, swap_halves(row)
            )
            ids = jnp.where(lane == group * capacity + slot, block, ids)
        mine = (lane >= group * capacity) & (lane < (group + 1) * capacity)
        out_ref[to, pert + capacity :, :] = jnp.where(
            mine, jnp.take_along_axis(patch_row, ids, axis=1), 0.0
        )


def gather_multiply(quad, cols_ref, ext_ref, m_ref, low):
    rows = []
    for place in range(QUAD):
        g = quad * QUAD + place
        tiles = [ext_ref[cols_ref[k, g]] for k in range(4)]
        rows.append(
            jnp.concatenate(
                [jnp.where(low, tiles[0], tiles[1]), jnp.where(low, tiles[2], tiles[3])], axis=1
            )
        )
    lhs = jnp.concatenate(rows, axis=0)
    rhs = m_ref[pl.ds(quad * QUAD, QUAD)].reshape(QUAD * HALF, 4 * HALF)
    out = lax.dot_general(lhs, rhs, (((1,), (1,)), ((), ())), preferred_element_type=F32)
    p = out.shape[0] // QUAD
    first = jnp.where(low, out[:p, :LANES], out[p : 2 * p, :LANES])
    second = jnp.where(low, out[2 * p : 3 * p, LANES:], out[3 * p :, LANES:])
    return first, second


def store_pair(ref, pair, value, low):
    value = value.astype(BF16)
    other = swap_halves(value.astype(F32)).astype(BF16)
    ref[2 * pair] = jnp.where(low, value, other)
    ref[2 * pair + 1] = jnp.where(low, other, value)


def fill_messages(send_ref, ref, msg_refs, low):
    for group, msg_ref in enumerate(msg_refs):
        for pair in range(msg_ref.shape[0]):
            even, odd = (
                ref[jnp.maximum(send_ref[0, group, 2 * pair + half], 0)] for half in range(2)
            )
            msg_ref[pair] = jnp.where(low, even, odd)


def first_kernel(
    cols_ref, send_ref, patch_ref, got_ref, w_ref, diag_ref, coupling_hbm,
    m_ref, one_hot_ref, t1_ref, t2_ref, o0, o1, o2, o3, ext_ref, coupling_ref, sems,
):
    chunks = sems.shape[0]
    size = diag_ref.shape[0] // chunks
    copies = [
        pltpu.make_async_copy(
            coupling_hbm.at[chunk * size : (chunk + 1) * size],
            coupling_ref.at[chunk * size : (chunk + 1) * size],
            sems.at[chunk],
        )
        for chunk in range(chunks)
    ]
    for copy in copies:
        copy.start()
    pert = t1_ref.shape[1]
    capacity = send_ref.shape[2]
    blocks = cols_ref.shape[1]
    parts = got_ref.shape[0]
    sources = neighbours(parts)
    low = low_half((pert, LANES))
    lane = lax.broadcasted_iota(jnp.int32, (1, LANES), 1)
    ghost_ids = sum(got_ref[source, pert + capacity : pert + capacity + 1, :] for source in sources)
    ghost_ids = jnp.where(lane < 4 * capacity, ghost_ids, -1.0)
    ids = jnp.concatenate([patch_ref[...].astype(F32), ghost_ids], axis=1)
    total = jnp.zeros((3 * pert, 2 * LANES), F32)
    for part in range(parts):
        names = (
            lax.broadcasted_iota(jnp.int32, (LANES, 2 * LANES), 0) + part * LANES
        ).astype(F32)
        hot = jnp.where(names == ids, 1.0, 0.0).astype(BF16)
        one_hot_ref[part * LANES : (part + 1) * LANES, :] = hot
        value = got_ref[part, :pert]
        top = value.astype(BF16)
        rest = value - top.astype(F32)
        mid = rest.astype(BF16)
        last = (rest - mid.astype(F32)).astype(BF16)
        total = total + jnp.dot(
            jnp.concatenate([top, mid, last], axis=0), hot, preferred_element_type=F32
        )
    picked = total[:pert] + total[pert : 2 * pert] + total[2 * pert :]
    local_picked = picked[:, :LANES]
    ghost_picked = picked[:, LANES:]
    full_low = low.astype(jnp.int32)

    def seed(pair, _):
        index = 2 * pair + 1 - full_low
        spread = jnp.take_along_axis(local_picked, index, axis=1)
        value = spread * w_ref[pl.ds(pair, 1), :]
        t1_ref[pair] = value
        store_pair(ext_ref, pair, value, low)
        return 0

    lax.fori_loop(0, blocks // 2, seed, 0, unroll=16)
    for group, source in enumerate(sources):
        for slot in range(capacity):
            place = group * capacity + slot
            row = got_ref[source, pert + slot : pert + slot + 1, :]
            spread = jnp.broadcast_to(ghost_picked[:, place : place + 1], (pert, LANES))
            ext_ref[blocks + place] = (spread * row).astype(BF16)

    for chunk, copy in enumerate(copies):
        copy.wait()
        for block in range(chunk * size, (chunk + 1) * size):
            m_ref[block] = jnp.dot(
                diag_ref[block], coupling_ref[block], preferred_element_type=F32
            ).astype(BF16)

    def sweep(quad, _):
        first, second = gather_multiply(quad, cols_ref, ext_ref, m_ref, low)
        store_pair(t2_ref, 2 * quad, t1_ref[2 * quad] - first, low)
        store_pair(t2_ref, 2 * quad + 1, t1_ref[2 * quad + 1] - second, low)
        return 0

    lax.fori_loop(0, blocks // QUAD, sweep, 0, unroll=32)
    fill_messages(send_ref, t2_ref, (o0, o1, o2, o3), low)


def extend(ext_ref, local_ref, ghosts, low):
    blocks = local_ref.shape[0]
    count = ghosts[0].shape[0]
    ext_ref[:blocks] = local_ref[...]
    for group, ref in enumerate(ghosts):
        for pair in range(count):
            store_pair(ext_ref, blocks // 2 + group * count + pair, ref[pair], low)


def sweep_kernel(
    cols_ref, send_ref, t1_ref, prev_ref, g0, g1, g2, g3, m_ref,
    next_ref, o0, o1, o2, o3, ext_ref,
):
    low = low_half(prev_ref.shape[1:])
    extend(ext_ref, prev_ref, (g0, g1, g2, g3), low)

    def sweep(quad, _):
        first, second = gather_multiply(quad, cols_ref, ext_ref, m_ref, low)
        store_pair(next_ref, 2 * quad, t1_ref[2 * quad] - first, low)
        store_pair(next_ref, 2 * quad + 1, t1_ref[2 * quad + 1] - second, low)
        return 0

    lax.fori_loop(0, cols_ref.shape[1] // QUAD, sweep, 0, unroll=32)
    fill_messages(send_ref, next_ref, (o0, o1, o2, o3), low)


def clear(acc_refs):
    def one(place, _):
        for ref in acc_refs:
            ref[place] = jnp.zeros(ref.shape[1:], F32)
        return 0

    lax.fori_loop(0, acc_refs[0].shape[0], one, 0, unroll=16)


def multiply_scatter(quad, cols_ref, pairs, m_ref, acc_refs, low):
    zero = jnp.zeros(pairs[0].shape, F32)
    rows = []
    for place in range(QUAD):
        value = pairs[place // 2]
        kept = jnp.where(low, value, zero) if place % 2 == 0 else jnp.where(low, zero, value)
        tiles = [kept, zero] if place < 2 else [zero, kept]
        rows.append(jnp.concatenate(tiles, axis=1))
    lhs = jnp.concatenate(rows, axis=0).astype(BF16)
    rhs = m_ref[pl.ds(quad * QUAD, QUAD)].reshape(QUAD * HALF, 4 * HALF)
    out = jnp.dot(lhs, rhs, preferred_element_type=F32)
    p = pairs[0].shape[0]
    for place in range(QUAD):
        g = quad * QUAD + place
        for k in range(4):
            column = cols_ref[k, g]
            piece = out[place * p : (place + 1) * p, (k // 2) * LANES : (k // 2 + 1) * LANES]
            acc_refs[k][column] = acc_refs[k][column] + piece


def half_sums(acc_refs, place, low):
    return jnp.where(
        low, acc_refs[0][place] + acc_refs[2][place], acc_refs[1][place] + acc_refs[3][place]
    )


def pair_sum(acc_refs, pair, low):
    even = half_sums(acc_refs, 2 * pair, low)
    odd = half_sums(acc_refs, 2 * pair + 1, low)
    return jnp.where(low, even, odd) + swap_halves(jnp.where(low, odd, even))


def finish_round(base_ref, target_ref, acc_refs, msg_refs, blocks, low):
    def local(pair, _):
        base_ref[pair] = target_ref[pair] - pair_sum(acc_refs, pair, low)
        return 0

    lax.fori_loop(0, blocks // 2, local, 0, unroll=16)
    for group, ref in enumerate(msg_refs):
        count = ref.shape[0]
        for pair in range(count):
            ref[pair] = pair_sum(acc_refs, blocks // 2 + group * count + pair, low).astype(BF16)


def turn_kernel(
    cols_ref, t1_ref, prev_ref, g0, g1, g2, g3, m_ref, weight_ref,
    tangent_ref, target_ref, base_ref, o0, o1, o2, o3, ext_ref, *acc_refs,
):
    low = low_half(prev_ref.shape[1:])
    blocks = cols_ref.shape[1]
    extend(ext_ref, prev_ref, (g0, g1, g2, g3), low)

    def sweep(quad, _):
        coupled = gather_multiply(quad, cols_ref, ext_ref, m_ref, low)
        for place in range(2):
            pair = 2 * quad + place
            value = t1_ref[pair] - coupled[place]
            start = pl.multiple_of(pair * LANES, LANES)
            tangent_ref[:, pl.ds(start, LANES)] = value
            target_ref[pair] = value * weight_ref[pl.ds(pair, 1), :]
        return 0

    lax.fori_loop(0, blocks // QUAD, sweep, 0, unroll=32)
    scatter_all(cols_ref, target_ref, m_ref, acc_refs, low)
    finish_round(base_ref, target_ref, acc_refs, (o0, o1, o2, o3), blocks, low)


def take_returned(send_ref, base_ref, u_ref, ghosts, low):
    u_ref[...] = base_ref[...]
    which = 1 - low.astype(jnp.int32)
    for group, ref in enumerate(ghosts):
        for pair in range(ref.shape[0]):
            value = ref[pair].astype(F32)
            other = swap_halves(value)
            for half, both in enumerate(
                (jnp.where(low, value, other), jnp.where(low, other, value))
            ):
                block = send_ref[0, group, 2 * pair + half]
                place = jnp.maximum(block, 0) // 2
                wanted = jnp.where(block < 0, 2, block % 2)
                u_ref[place] = u_ref[place] - jnp.where(which == wanted, both, 0.0)


def scatter_all(cols_ref, u_ref, m_ref, acc_refs, low):
    clear(acc_refs)

    def sweep(quad, _):
        pairs = [u_ref[2 * quad], u_ref[2 * quad + 1]]
        multiply_scatter(quad, cols_ref, pairs, m_ref, acc_refs, low)
        return 0

    lax.fori_loop(0, cols_ref.shape[1] // QUAD, sweep, 0, unroll=32)


def adjoint_kernel(
    cols_ref, send_ref, base_in_ref, target_ref, g0, g1, g2, g3, m_ref,
    base_ref, o0, o1, o2, o3, u_ref, *acc_refs,
):
    low = low_half(u_ref.shape[1:])
    take_returned(send_ref, base_in_ref, u_ref, (g0, g1, g2, g3), low)
    scatter_all(cols_ref, u_ref, m_ref, acc_refs, low)
    finish_round(base_ref, target_ref, acc_refs, (o0, o1, o2, o3), cols_ref.shape[1], low)


def last_kernel(
    cols_ref, send_ref, base_in_ref, target_ref, g0, g1, g2, g3, m_ref, w_ref, got_ref,
    one_hot_ref, out_ref, u_ref, *acc_refs,
):
    pert = u_ref.shape[1]
    blocks = cols_ref.shape[1]
    low = low_half(u_ref.shape[1:])
    lane = lax.broadcasted_iota(jnp.int32, (pert, LANES), 1)
    take_returned(send_ref, base_in_ref, u_ref, (g0, g1, g2, g3), low)
    scatter_all(cols_ref, u_ref, m_ref, acc_refs, low)

    def local(pair, terms):
        value = (target_ref[pair] - pair_sum(acc_refs, pair, low)) * w_ref[pl.ds(pair, 1), :]
        even = jnp.sum(jnp.where(low, value, 0.0), axis=1, keepdims=True)
        odd = jnp.sum(jnp.where(low, 0.0, value), axis=1, keepdims=True)
        return jnp.where(lane == 2 * pair, even, jnp.where(lane == 2 * pair + 1, odd, terms))

    local_terms = lax.fori_loop(
        0, blocks // 2, local, jnp.zeros((pert, LANES), F32), unroll=4
    )
    ghost_terms = jnp.zeros((pert, LANES), F32)
    parts = got_ref.shape[0]
    capacity = send_ref.shape[2]
    for group, source in enumerate(neighbours(parts)):
        for slot in range(capacity):
            place = group * capacity + slot
            row = got_ref[source, pert + slot : pert + slot + 1, :]
            value = half_sums(acc_refs, blocks + place, low) * row
            ghost_terms = jnp.where(
                lane == place, -jnp.sum(value, axis=1, keepdims=True), ghost_terms
            )
    terms = jnp.concatenate([local_terms, ghost_terms], axis=1)
    top = terms.astype(BF16)
    rest = (terms - top.astype(F32)).astype(BF16)
    both = jnp.concatenate([top, rest], axis=0)
    perts = out_ref.shape[0] // parts
    sub = lax.broadcasted_iota(jnp.int32, (8, LANES), 0)
    for part in range(parts):
        hot = one_hot_ref[part * LANES : (part + 1) * LANES, :]
        out = lax.dot_general(both, hot, (((1,), (1,)), ((), ())), preferred_element_type=F32)
        value = out[:pert] + out[pert:]
        curve = jnp.sum(value * got_ref[part, :pert], axis=0, keepdims=True)
        top = curve.astype(BF16).astype(F32)
        extra = jnp.where(sub == 0, top, jnp.where(sub == 1, curve - top, 0.0))
        for place in range(perts):
            out_ref[part * perts + place, :pert] = value.astype(BF16)
            out_ref[part * perts + place, pert:] = extra.astype(BF16)


def owner_kernel(terms_ref, hessian_ref, curve_ref, *, parts, scale):
    pert = hessian_ref.shape[0]
    perts = terms_ref.shape[0] // parts
    mine = lax.axis_index("pert")
    total = jnp.zeros(hessian_ref.shape, F32)
    for part in range(parts):
        total = total + terms_ref[part * perts + mine, :pert].astype(F32)
    hessian_ref[...] = total
    curve = jnp.zeros((8, LANES), F32)
    for place in range(terms_ref.shape[0]):
        curve = curve + terms_ref[place, pert:].astype(F32)
    curve_ref[...] = (curve[0:1] + curve[1:2]) * scale


def call(body, outs, spaces, scratch=(), name=None, flops=0, moved=1 << 20, limit=12):
    return pl.pallas_call(
        body,
        out_shape=outs,
        in_specs=[{"s": SMEM, "v": VMEM, "h": HBM}[s] for s in spaces],
        out_specs=jax.tree.map(lambda _: VMEM, outs),
        scratch_shapes=list(scratch),
        compiler_params=pltpu.CompilerParams(vmem_limit_bytes=limit * MIB),
        name=name,
        cost_estimate=pl.CostEstimate(flops=flops, transcendentals=0, bytes_accessed=moved),
    )


def shards(
    probes, melt_shape, obs_weight, diag_inverse, coupling, columns, send_list, patch_of_block
):
    pert = probes.shape[0]
    blocks = coupling.shape[0]
    capacity = send_list.shape[2]
    parts = lax.axis_size("dom")
    pairs = blocks // 2
    shape = jax.ShapeDtypeStruct
    msgs = [shape((capacity // 2, pert, LANES), BF16)] * 4
    pair_array = shape((pairs, pert, LANES), F32)
    block_array = shape((blocks, pert, LANES), BF16)
    ext = pltpu.VMEM((blocks + 4 * capacity, pert, LANES), BF16)
    accs = [pltpu.VMEM((blocks + 4 * capacity, pert, LANES), F32)] * 4
    held = pltpu.VMEM((pairs, pert, LANES), F32)
    melt = melt_shape.reshape(pairs, LANES)
    weight = obs_weight.reshape(pairs, LANES)
    patch = patch_of_block.reshape(1, blocks)

    perts = lax.axis_size("pert")
    columns = columns.T
    w, outgoing = call(
        functools.partial(melt_kernel, parts=parts),
        [shape((pairs, LANES), F32), shape((parts, pert + capacity + 8, LANES), F32)],
        "hhhhh",
        [
            pltpu.SMEM(send_list.shape, jnp.int32),
            pltpu.VMEM((pairs, LANES), F32),
            pltpu.VMEM((1, blocks), jnp.int32),
            pltpu.VMEM(probes.shape, F32),
            pltpu.VMEM((HALF, HALF, blocks), BF16),
            pltpu.SemaphoreType.DMA((5,)),
        ],
        name="melt",
        limit=60,
    )(send_list, melt, patch, probes, jnp.transpose(diag_inverse, (1, 2, 0)))
    got = lax.all_to_all(outgoing, "dom", 0, 0, tiled=True)
    m, one_hot, t1, state, *out = call(
        first_kernel,
        [shape(coupling.shape, BF16), shape((parts * probes.shape[1], 2 * LANES), BF16), pair_array, block_array] + msgs,
        "ssvvvvh",
        [ext, pltpu.VMEM(coupling.shape, BF16), pltpu.SemaphoreType.DMA((8,))],
        name="first",
        limit=46,
    )(columns, send_list, patch, got, w, diag_inverse, coupling)
    ghosts = [rotated(v, o) for v, o in zip(out, OFFSET_LIST)]
    state, *out = call(
        sweep_kernel, [block_array] + msgs, "ssvvvvvvv", [ext], name="sweep"
    )(columns, send_list, t1, state, *ghosts, m)
    ghosts = [rotated(v, o) for v, o in zip(out, OFFSET_LIST)]
    tangent, target, base, *out = call(
        turn_kernel,
        [shape((pert, blocks * HALF), F32), pair_array, pair_array] + msgs,
        "svvvvvvvv",
        [ext] + accs,
        name="turn",
    )(columns, t1, state, *ghosts, m, weight)
    ghosts = [rotated(v, -o) for v, o in zip(out, OFFSET_LIST)]
    base, *out = call(
        adjoint_kernel, [pair_array] + msgs, "ssvvvvvvv", [held] + accs, name="adjoint"
    )(columns, send_list, base, target, *ghosts, m)
    ghosts = [rotated(v, -o) for v, o in zip(out, OFFSET_LIST)]
    terms = call(
        last_kernel,
        shape((parts * perts, pert + 8, LANES), BF16),
        "ssvvvvvvvvvv",
        [held] + accs,
        name="last",
    )(columns, send_list, base, target, *ghosts, m, w, got, one_hot)
    terms = lax.all_to_all(terms, ("dom", "pert"), 0, 0, tiled=True)
    hessian_probe, curvature = call(
        functools.partial(owner_kernel, parts=parts, scale=1.0 / (pert * perts)),
        [shape(probes.shape, F32), shape((1, LANES), F32)],
        "v",
        name="owner",
    )(terms)
    return tangent, hessian_probe, curvature.reshape(-1)


def solution(mesh):
    in_specs = (
        P("pert", "dom"),
        P("dom"),
        P("dom"),
        P("dom", None, None),
        P("dom", None, None),
        P("dom", None),
        P("dom", None, None),
        P("dom"),
    )
    out_specs = (P("pert", "dom"), P("pert", "dom"), P("dom"))
    return jax.shard_map(shards, mesh=mesh, in_specs=in_specs, out_specs=out_specs, check_vma=False)
```

```python
import functools

import jax
import jax.numpy as jnp
from jax import lax
from jax.experimental import pallas as pl
from jax.experimental.pallas import tpu as pltpu
from jax.sharding import PartitionSpec as P

OFFSET_LIST = (-2, -1, 1, 2)
F32 = jnp.float32
BF16 = jnp.bfloat16
LANES = 128
HALF = 64
QUAD = 4
RADIX = 64

VMEM = pl.BlockSpec(memory_space=pltpu.VMEM)
SMEM = pl.BlockSpec(memory_space=pltpu.SMEM)
HBM = pl.BlockSpec(memory_space=pltpu.HBM)
MIB = 1024 * 1024


def low_half(shape):
    return lax.broadcasted_iota(jnp.int32, shape, len(shape) - 1) < HALF


def swap_halves(value):
    return pltpu.roll(value, HALF, 1)


def rotated(value, by):
    peers = lax.axis_size("dom")
    return lax.ppermute(value, "dom", [(i, (i + by) % peers) for i in range(peers)])


def neighbours(parts):
    me = lax.axis_index("dom")
    return [lax.rem(me - offset + parts, parts) for offset in OFFSET_LIST]


def melt_kernel(
    send_hbm, melt_hbm, patch_hbm, probe_hbm, diag_hbm, w_ref, out_ref,
    send_ref, melt_ref, patch_ref, probe_ref, diag_ref, sems, *, parts,
):
    copies = [
        pltpu.make_async_copy(source, target, sems.at[number])
        for number, (source, target) in enumerate(
            (
                (diag_hbm, diag_ref),
                (melt_hbm, melt_ref),
                (patch_hbm, patch_ref),
                (probe_hbm, probe_ref),
                (send_hbm, send_ref),
            )
        )
    ]
    for copy in copies:
        copy.start()
    for copy in copies:
        copy.wait()
    pairs = melt_ref.shape[0]
    pert = probe_ref.shape[0]
    capacity = send_ref.shape[2]
    low = low_half((1, LANES))
    lane = lax.broadcasted_iota(jnp.int32, (HALF, LANES), 1)
    turned = jnp.transpose(jnp.concatenate([melt_ref[...], jnp.zeros((LANES - pairs, LANES), F32)], axis=0))
    even = jnp.take_along_axis(turned[:HALF], lane // 2, axis=1)
    odd = jnp.take_along_axis(turned[HALF:], lane // 2, axis=1)
    melt = jnp.where(lane % 2 == 0, even, odd)
    sums = [
        jnp.sum(diag_ref[i].astype(F32) * melt, axis=0, keepdims=True)
        for i in range(diag_ref.shape[0])
    ]
    sums = jnp.concatenate(sums, axis=0)
    source = 2 * (lane % HALF)
    both = jnp.concatenate(
        [
            jnp.take_along_axis(sums, source, axis=1),
            jnp.take_along_axis(sums, source + 1, axis=1),
        ],
        axis=0,
    )
    w_ref[...] = jnp.transpose(both)[:pairs]
    patch_row = jnp.broadcast_to(patch_ref[...].astype(F32), (8, LANES))
    lane = lax.broadcasted_iota(jnp.int32, (8, LANES), 1)
    for part in range(parts):
        out_ref[part, :pert] = probe_ref[...]
    me = lax.axis_index("dom")
    for group, offset in enumerate(OFFSET_LIST):
        to = lax.rem(me + offset + parts, parts)
        ids = jnp.zeros((8, LANES), jnp.int32)
        for slot in range(capacity):
            block = jnp.maximum(send_ref[0, group, slot], 0)
            row = w_ref[pl.ds(block // 2, 1), :]
            out_ref[to, pert + slot : pert + slot + 1, :] = jnp.where(
                low == (block % 2 == 0), row, swap_halves(row)
            )
            ids = jnp.where(lane == group * capacity + slot, block, ids)
        mine = (lane >= group * capacity) & (lane < (group + 1) * capacity)
        out_ref[to, pert + capacity :, :] = jnp.where(
            mine, jnp.take_along_axis(patch_row, ids, axis=1), 0.0
        )


def gather_rows(quad, cols_ref, ext_ref, low):
    rows = []
    for place in range(QUAD):
        g = quad * QUAD + place
        tiles = [ext_ref[cols_ref[k, g]] for k in range(4)]
        rows.append(
            jnp.concatenate(
                [jnp.where(low, tiles[0], tiles[1]), jnp.where(low, tiles[2], tiles[3])], axis=1
            )
        )
    return rows


def coupled_rows(quad, rows, m_ref):
    rhs = m_ref[pl.ds(quad * QUAD, QUAD)].reshape(QUAD * HALF, 4 * HALF)
    return lax.dot_general(
        jnp.concatenate(rows, axis=0), rhs, (((1,), (1,)), ((), ())), preferred_element_type=F32
    )


def own_pairs(out, size, low):
    first = jnp.where(low, out[:size, :LANES], out[size : 2 * size, :LANES])
    second = jnp.where(low, out[2 * size : 3 * size, LANES:], out[3 * size : 4 * size, LANES:])
    return first, second


def gather_multiply(quad, cols_ref, ext_ref, m_ref, low):
    out = coupled_rows(quad, gather_rows(quad, cols_ref, ext_ref, low), m_ref)
    return own_pairs(out, out.shape[0] // QUAD, low)


def store_pair(ref, pair, value, low):
    value = value.astype(BF16)
    other = swap_halves(value.astype(F32)).astype(BF16)
    ref[2 * pair] = jnp.where(low, value, other)
    ref[2 * pair + 1] = jnp.where(low, other, value)


def fill_messages(send_ref, ref, msg_refs, low):
    for group, msg_ref in enumerate(msg_refs):
        for pair in range(send_ref.shape[2] // 2):
            even, odd = (
                ref[jnp.maximum(send_ref[0, group, 2 * pair + half], 0)] for half in range(2)
            )
            msg_ref[pair] = jnp.where(low, even, odd)


def patches_of_columns(columns_ref, ids):
    columns = jnp.concatenate([columns_ref[...], columns_ref[...]], axis=0)
    here = jnp.broadcast_to(ids[:, :LANES], columns.shape)
    there = jnp.broadcast_to(ids[:, LANES:], columns.shape)
    return jnp.where(
        columns < LANES,
        jnp.take_along_axis(here, jnp.minimum(columns, LANES - 1), axis=1),
        jnp.take_along_axis(there, jnp.maximum(columns - LANES, 0), axis=1),
    )


def first_kernel(
    cols_ref, send_ref, patch_ref, columns_ref, got_ref, w_hbm, diag_ref, coupling_hbm,
    m_ref, v_ref, names_ref, t1_ref, t2_ref, o0, o1, o2, o3,
    ext_ref, row_ref, w_ref, coupling_ref, w_sem, sems,
):
    w_copy = pltpu.make_async_copy(w_hbm, w_ref, w_sem)
    w_copy.start()
    chunks = sems.shape[0]
    size = diag_ref.shape[0] // chunks
    copies = [
        pltpu.make_async_copy(
            coupling_hbm.at[chunk * size : (chunk + 1) * size],
            coupling_ref.at[chunk * size : (chunk + 1) * size],
            sems.at[chunk],
        )
        for chunk in range(chunks)
    ]
    for copy in copies:
        copy.start()
    pert = t1_ref.shape[1]
    capacity = send_ref.shape[2]
    blocks = cols_ref.shape[1]
    parts = got_ref.shape[0]
    sources = neighbours(parts)
    low = low_half((pert, LANES))
    lane = lax.broadcasted_iota(jnp.int32, (1, LANES), 1)
    ghost_ids = sum(got_ref[source, pert + capacity : pert + capacity + 1, :] for source in sources)
    ghost_ids = jnp.where(lane < 4 * capacity, ghost_ids, -1.0)
    ids = jnp.concatenate([patch_ref[...].astype(F32), ghost_ids], axis=1)
    total = jnp.zeros((3 * pert, 2 * LANES), F32)
    for part in range(parts):
        names = (
            lax.broadcasted_iota(jnp.int32, (LANES, 2 * LANES), 0) + part * LANES
        ).astype(F32)
        hot = jnp.where(names == ids, 1.0, 0.0).astype(BF16)
        value = got_ref[part, :pert]
        top = value.astype(BF16)
        rest = value - top.astype(F32)
        mid = rest.astype(BF16)
        last = (rest - mid.astype(F32)).astype(BF16)
        total = total + jnp.dot(
            jnp.concatenate([top, mid, last], axis=0), hot, preferred_element_type=F32
        )
    picked = total[:pert] + total[pert : 2 * pert] + total[2 * pert :]
    local_picked = picked[:, :LANES]
    ghost_picked = picked[:, LANES:]
    full_low = low.astype(jnp.int32)
    column_patches = patches_of_columns(columns_ref, ids)
    sub = lax.broadcasted_iota(jnp.int32, (8, LANES), 0)
    lane8 = lax.broadcasted_iota(jnp.int32, (8, LANES), 1)
    wanted = sub == lane8 % 4

    def listed(blocks_of_lanes):
        taken = jnp.take_along_axis(column_patches, blocks_of_lanes, axis=1)
        return jnp.sum(jnp.where(wanted, taken, 0.0), axis=0, keepdims=True)

    for tile in range(4 * blocks // LANES):
        names_ref[tile : tile + 1, :] = listed(tile * (LANES // 4) + lane8 // 4)
    w_copy.wait()
    w = w_ref[...]
    w_other = swap_halves(w)
    low_w = low_half(w.shape)
    row_ref[pl.ds(0, blocks // 2, stride=2), :] = jnp.where(low_w, w, w_other)
    row_ref[pl.ds(1, blocks // 2, stride=2), :] = jnp.where(low_w, w_other, w)
    for group, source in enumerate(sources):
        start = blocks + group * capacity
        row_ref[start : start + capacity, :] = got_ref[source, pert : pert + capacity, :]

    def seed(pair, _):
        index = 2 * pair + 1 - full_low
        spread = jnp.take_along_axis(local_picked, index, axis=1)
        value = spread * w_ref[pl.ds(pair, 1), :]
        t1_ref[pair] = value
        store_pair(ext_ref, pair, value, low)
        return 0

    lax.fori_loop(0, blocks // 2, seed, 0, unroll=16)
    for group, source in enumerate(sources):
        for slot in range(capacity):
            place = group * capacity + slot
            row = got_ref[source, pert + slot : pert + slot + 1, :]
            spread = jnp.broadcast_to(ghost_picked[:, place : place + 1], (pert, LANES))
            ext_ref[blocks + place] = (spread * row).astype(BF16)

    for chunk, copy in enumerate(copies):
        copy.wait()
        for block in range(chunk * size, (chunk + 1) * size):
            m_ref[block] = jnp.dot(
                diag_ref[block], coupling_ref[block], preferred_element_type=F32
            ).astype(BF16)

    low8 = low_half((8, LANES))
    masks = [(sub % 4 == k) & (low8 if k % 2 == 0 else ~low8) for k in range(4)]
    nothing = jnp.zeros((8, LANES), F32)

    def sweep(quad, _):
        rows = gather_rows(quad, cols_ref, ext_ref, low)
        tiles = ([], [])
        for place in range(QUAD):
            w_rows = [row_ref[pl.ds(cols_ref[k, quad * QUAD + place], 1), :] for k in range(4)]
            for side in range(2):
                tiles[side].append(
                    jnp.where(
                        masks[2 * side],
                        w_rows[2 * side],
                        jnp.where(masks[2 * side + 1], w_rows[2 * side + 1], nothing),
                    )
                )
        extra = jnp.concatenate([jnp.concatenate(side, axis=0) for side in tiles], axis=1)
        out = coupled_rows(quad, rows + [extra.astype(BF16)], m_ref)
        for place, value in enumerate(own_pairs(out, pert, low)):
            pair = 2 * quad + place
            store_pair(t2_ref, pair, t1_ref[pair] - value, low)
        for place, value in enumerate(own_pairs(out[QUAD * pert :], 8, low8)):
            v_ref[2 * quad + place] = value
        return 0

    lax.fori_loop(0, blocks // QUAD, sweep, 0, unroll=32)
    msgs = (o0, o1, o2, o3)
    fill_messages(send_ref, t2_ref, msgs, low)
    half = capacity // 2
    for group, ref in enumerate(msgs):
        places = jnp.zeros((8, LANES), jnp.int32)
        values = []
        for slot in range(capacity):
            block = jnp.maximum(send_ref[0, group, slot], 0)
            value = v_ref[block // 2]
            right = (slot - block) % 2 == 0
            values.append(jnp.where(right, value, swap_halves(value)))
            places = jnp.where(lane8 // 4 == slot, block, places)
        pairs = [
            jnp.where(low8, values[2 * pair], values[2 * pair + 1]) for pair in range(half)
        ]
        for tile in range(half // 2):
            ref[half + tile] = jnp.concatenate(pairs[2 * tile : 2 * tile + 2], axis=0).astype(BF16)
        patch = listed(places).astype(jnp.int32)
        ref[half + half // 2] = jnp.concatenate(
            [
                jnp.broadcast_to(patch // RADIX, (8, LANES)),
                jnp.broadcast_to(patch % RADIX, (8, LANES)),
            ],
            axis=0,
        ).astype(F32).astype(BF16)


def extend(ext_ref, local_ref, ghosts, low):
    blocks = local_ref.shape[0]
    count = (ext_ref.shape[0] - blocks) // 2 // len(ghosts)
    ext_ref[:blocks] = local_ref[...]
    for group, ref in enumerate(ghosts):
        for pair in range(count):
            store_pair(ext_ref, blocks // 2 + group * count + pair, ref[pair], low)


def sweep_kernel(
    cols_ref, send_ref, t1_ref, prev_ref, g0, g1, g2, g3, m_ref,
    next_ref, o0, o1, o2, o3, ext_ref,
):
    low = low_half(prev_ref.shape[1:])
    extend(ext_ref, prev_ref, (g0, g1, g2, g3), low)

    def sweep(quad, _):
        first, second = gather_multiply(quad, cols_ref, ext_ref, m_ref, low)
        store_pair(next_ref, 2 * quad, t1_ref[2 * quad] - first, low)
        store_pair(next_ref, 2 * quad + 1, t1_ref[2 * quad + 1] - second, low)
        return 0

    lax.fori_loop(0, cols_ref.shape[1] // QUAD, sweep, 0, unroll=32)
    fill_messages(send_ref, next_ref, (o0, o1, o2, o3), low)


def clear(acc_refs):
    def one(place, _):
        for ref in acc_refs:
            ref[place] = jnp.zeros(ref.shape[1:], F32)
        return 0

    lax.fori_loop(0, acc_refs[0].shape[0], one, 0, unroll=16)


def multiply_scatter(quad, cols_ref, pairs, m_ref, acc_refs, low):
    zero = jnp.zeros(pairs[0].shape, F32)
    rows = []
    for place in range(QUAD):
        value = pairs[place // 2]
        kept = jnp.where(low, value, zero) if place % 2 == 0 else jnp.where(low, zero, value)
        tiles = [kept, zero] if place < 2 else [zero, kept]
        rows.append(jnp.concatenate(tiles, axis=1))
    lhs = jnp.concatenate(rows, axis=0).astype(BF16)
    rhs = m_ref[pl.ds(quad * QUAD, QUAD)].reshape(QUAD * HALF, 4 * HALF)
    out = jnp.dot(lhs, rhs, preferred_element_type=F32)
    p = pairs[0].shape[0]
    for place in range(QUAD):
        g = quad * QUAD + place
        for k in range(4):
            column = cols_ref[k, g]
            piece = out[place * p : (place + 1) * p, (k // 2) * LANES : (k // 2 + 1) * LANES]
            acc_refs[k][column] = acc_refs[k][column] + piece


def half_sums(acc_refs, place, low):
    return jnp.where(
        low, acc_refs[0][place] + acc_refs[2][place], acc_refs[1][place] + acc_refs[3][place]
    )


def pair_sum(acc_refs, pair, low):
    even = half_sums(acc_refs, 2 * pair, low)
    odd = half_sums(acc_refs, 2 * pair + 1, low)
    return jnp.where(low, even, odd) + swap_halves(jnp.where(low, odd, even))


def finish_round(base_ref, target_ref, acc_refs, msg_refs, blocks, low):
    def local(pair, _):
        base_ref[pair] = target_ref[pair] - pair_sum(acc_refs, pair, low)
        return 0

    lax.fori_loop(0, blocks // 2, local, 0, unroll=16)
    for group, ref in enumerate(msg_refs):
        count = ref.shape[0]
        for pair in range(count):
            ref[pair] = pair_sum(acc_refs, blocks // 2 + group * count + pair, low).astype(BF16)


def turn_kernel(
    cols_ref, t1_ref, prev_ref, g0, g1, g2, g3, m_ref, weight_ref,
    tangent_ref, target_ref, base_ref, o0, o1, o2, o3, ext_ref, *acc_refs,
):
    low = low_half(prev_ref.shape[1:])
    blocks = cols_ref.shape[1]
    extend(ext_ref, prev_ref, (g0, g1, g2, g3), low)

    def sweep(quad, _):
        coupled = gather_multiply(quad, cols_ref, ext_ref, m_ref, low)
        for place in range(2):
            pair = 2 * quad + place
            value = t1_ref[pair] - coupled[place]
            start = pl.multiple_of(pair * LANES, LANES)
            tangent_ref[:, pl.ds(start, LANES)] = value
            target_ref[pair] = value * weight_ref[pl.ds(pair, 1), :]
        return 0

    lax.fori_loop(0, blocks // QUAD, sweep, 0, unroll=32)
    scatter_all(cols_ref, target_ref, m_ref, acc_refs, low)
    finish_round(base_ref, target_ref, acc_refs, (o0, o1, o2, o3), blocks, low)


def take_returned(send_ref, base_ref, u_ref, ghosts, low):
    u_ref[...] = base_ref[...]
    which = 1 - low.astype(jnp.int32)
    for group, ref in enumerate(ghosts):
        for pair in range(ref.shape[0]):
            value = ref[pair].astype(F32)
            other = swap_halves(value)
            for half, both in enumerate(
                (jnp.where(low, value, other), jnp.where(low, other, value))
            ):
                block = send_ref[0, group, 2 * pair + half]
                place = jnp.maximum(block, 0) // 2
                wanted = jnp.where(block < 0, 2, block % 2)
                u_ref[place] = u_ref[place] - jnp.where(which == wanted, both, 0.0)


def scatter_all(cols_ref, u_ref, m_ref, acc_refs, low):
    clear(acc_refs)

    def sweep(quad, _):
        pairs = [u_ref[2 * quad], u_ref[2 * quad + 1]]
        multiply_scatter(quad, cols_ref, pairs, m_ref, acc_refs, low)
        return 0

    lax.fori_loop(0, cols_ref.shape[1] // QUAD, sweep, 0, unroll=32)


def prepare_kernel(
    patch_ref, names_ref, g0, g1, g2, g3, target_ref, w_ref, hot_ref, terms_ref
):
    pairs, pert, _ = target_ref.shape
    low8 = low_half((1, LANES))
    rows = [patch_ref[...].astype(F32)] + [names_ref[tile : tile + 1] for tile in range(4)]
    ghosts = []
    for ref in (g0, g1, g2, g3):
        digits = ref[ref.shape[0] - 1].astype(F32)
        ghosts.append(digits[0:1] * RADIX + digits[8:9])
    for tile in range(2):
        rows.append(jnp.where(low8, ghosts[2 * tile], swap_halves(ghosts[2 * tile + 1])))
    low = low_half((pert, LANES))
    lane = lax.broadcasted_iota(jnp.int32, (pert, LANES), 1)
    first = lax.broadcasted_iota(jnp.int32, (LANES, LANES), 0).astype(F32)

    def one(part, _):
        start = pl.multiple_of(part * LANES, LANES)
        base = (part * LANES).astype(F32)
        for tile, row in enumerate(rows):
            hot_ref[pl.ds(start, LANES), tile * LANES : (tile + 1) * LANES] = jnp.where(
                first == row - base, 1.0, 0.0
            ).astype(BF16)
        return 0

    lax.fori_loop(0, hot_ref.shape[0] // LANES, one, 0, unroll=2)

    def local(pair, terms):
        value = target_ref[pair] * w_ref[pl.ds(pair, 1), :]
        even = jnp.sum(jnp.where(low, value, 0.0), axis=1, keepdims=True)
        odd = jnp.sum(jnp.where(low, 0.0, value), axis=1, keepdims=True)
        return jnp.where(lane == 2 * pair, even, jnp.where(lane == 2 * pair + 1, odd, terms))

    terms_ref[...] = lax.fori_loop(0, pairs, local, jnp.zeros((pert, LANES), F32), unroll=16)


def last_kernel(
    cols_ref, send_ref, base_in_ref, target_ref, g0, g1, g2, g3, m_ref, v_ref, v0, v1, v2, v3,
    hot_ref, terms_ref, got_ref, out_ref, u_ref, *acc_refs,
):
    pert = u_ref.shape[1]
    blocks = cols_ref.shape[1]
    half = send_ref.shape[2] // 2
    parts = got_ref.shape[0]
    low = low_half(u_ref.shape[1:])
    take_returned(send_ref, base_in_ref, u_ref, (g0, g1, g2, g3), low)
    scatter_all(cols_ref, u_ref, m_ref, acc_refs, low)
    sub = lax.broadcasted_iota(jnp.int32, (8, LANES), 0)
    own = (sub < 4) == low_half((8, LANES))
    nothing = jnp.zeros((8, LANES), F32)

    def products(pair, first_v, second_v, first_z, second_z):
        rhs = jnp.concatenate(
            [
                jnp.concatenate([jnp.where(own, first_v, nothing), nothing], axis=1),
                jnp.concatenate([nothing, jnp.where(own, second_v, nothing)], axis=1),
            ],
            axis=0,
        )
        lhs = jnp.concatenate([first_z, second_z], axis=1)
        return lax.dot_general(
            lhs.astype(BF16), rhs.astype(BF16), (((1,), (1,)), ((), ())),
            preferred_element_type=F32,
        )

    pieces = []
    for pair in range(0, blocks // 2, 2):
        z = [pair_sum(acc_refs, pair + i, low) - target_ref[pair + i] for i in range(2)]
        pieces.append(products(pair, v_ref[pair], v_ref[pair + 1], *z))
    for group, ref in enumerate((v0, v1, v2, v3)):
        for tile in range(half // 2):
            both = ref[half + tile].astype(F32)
            pair = blocks // 2 + group * half + 2 * tile
            z = [pair_sum(acc_refs, pair + i, low) for i in range(2)]
            pieces.append(products(pair, both[:8], both[8:], *z))
    terms = jnp.concatenate([terms_ref[...]] + pieces, axis=1)
    top = terms.astype(BF16)
    rest = (terms - top.astype(F32)).astype(BF16)
    both = jnp.concatenate([top, rest], axis=0)
    perts = out_ref.shape[0] // parts
    sub = lax.broadcasted_iota(jnp.int32, (8, LANES), 0)
    for part in range(parts):
        hot = hot_ref[part * LANES : (part + 1) * LANES, :]
        out = lax.dot_general(both, hot, (((1,), (1,)), ((), ())), preferred_element_type=F32)
        value = out[:pert] + out[pert:]
        curve = jnp.sum(value * got_ref[part, :pert], axis=0, keepdims=True)
        top = curve.astype(BF16).astype(F32)
        extra = jnp.where(sub == 0, top, jnp.where(sub == 1, curve - top, 0.0))
        for place in range(perts):
            out_ref[part * perts + place, :pert] = value.astype(BF16)
            out_ref[part * perts + place, pert:] = extra.astype(BF16)


def owner_kernel(terms_ref, hessian_ref, curve_ref, *, parts, scale):
    pert = hessian_ref.shape[0]
    perts = terms_ref.shape[0] // parts
    mine = lax.axis_index("pert")
    total = jnp.zeros(hessian_ref.shape, F32)
    for part in range(parts):
        total = total + terms_ref[part * perts + mine, :pert].astype(F32)
    hessian_ref[...] = total
    curve = jnp.zeros((8, LANES), F32)
    for place in range(terms_ref.shape[0]):
        curve = curve + terms_ref[place, pert:].astype(F32)
    curve_ref[...] = (curve[0:1] + curve[1:2]) * scale


def call(body, outs, spaces, scratch=(), name=None, flops=0, moved=1 << 20, limit=12):
    return pl.pallas_call(
        body,
        out_shape=outs,
        in_specs=[{"s": SMEM, "v": VMEM, "h": HBM}[s] for s in spaces],
        out_specs=jax.tree.map(lambda _: VMEM, outs),
        scratch_shapes=list(scratch),
        compiler_params=pltpu.CompilerParams(vmem_limit_bytes=limit * MIB),
        name=name,
        cost_estimate=pl.CostEstimate(flops=flops, transcendentals=0, bytes_accessed=moved),
    )


def shards(
    probes, melt_shape, obs_weight, diag_inverse, coupling, columns, send_list, patch_of_block
):
    pert = probes.shape[0]
    blocks = coupling.shape[0]
    capacity = send_list.shape[2]
    parts = lax.axis_size("dom")
    pairs = blocks // 2
    shape = jax.ShapeDtypeStruct
    msgs = [shape((capacity // 2, pert, LANES), BF16)] * 4
    pair_array = shape((pairs, pert, LANES), F32)
    block_array = shape((blocks, pert, LANES), BF16)
    ext = pltpu.VMEM((blocks + 4 * capacity, pert, LANES), BF16)
    accs = [pltpu.VMEM((blocks + 4 * capacity, pert, LANES), F32)] * 4
    held = pltpu.VMEM((pairs, pert, LANES), F32)
    melt = melt_shape.reshape(pairs, LANES)
    weight = obs_weight.reshape(pairs, LANES)
    patch = patch_of_block.reshape(1, blocks)

    perts = lax.axis_size("pert")
    columns = columns.T
    w, outgoing = call(
        functools.partial(melt_kernel, parts=parts),
        [shape((pairs, LANES), F32), shape((parts, pert + capacity + 8, LANES), F32)],
        "hhhhh",
        [
            pltpu.SMEM(send_list.shape, jnp.int32),
            pltpu.VMEM((pairs, LANES), F32),
            pltpu.VMEM((1, blocks), jnp.int32),
            pltpu.VMEM(probes.shape, F32),
            pltpu.VMEM((HALF, HALF, blocks), BF16),
            pltpu.SemaphoreType.DMA((5,)),
        ],
        name="melt",
        limit=60,
    )(send_list, melt, patch, probes, jnp.transpose(diag_inverse, (1, 2, 0)))
    got = lax.all_to_all(outgoing, "dom", 0, 0, tiled=True)
    wide = [shape((capacity // 2 + capacity // 4 + 1, pert, LANES), BF16)] * 4
    m, v, names, t1, state, *out = call(
        first_kernel,
        [
            shape(coupling.shape, BF16),
            shape((pairs, 8, LANES), F32),
            shape((8, LANES), F32),
            pair_array,
            block_array,
        ]
        + wide,
        "ssvvvhvh",
        [
            ext,
            pltpu.VMEM((blocks + 4 * capacity, LANES), F32),
            pltpu.VMEM((pairs, LANES), F32),
            pltpu.VMEM(coupling.shape, BF16),
            pltpu.SemaphoreType.DMA,
            pltpu.SemaphoreType.DMA((8,)),
        ],
        name="first",
        limit=46,
    )(columns, send_list, patch, columns, got, w, diag_inverse, coupling)
    carried = [rotated(x, o) for x, o in zip(out, OFFSET_LIST)]
    state, *out = call(
        sweep_kernel, [block_array] + msgs, "ssvvvvvvv", [ext], name="sweep"
    )(columns, send_list, t1, state, *carried, m)
    ghosts = [rotated(v, o) for v, o in zip(out, OFFSET_LIST)]
    tangent, target, base, *out = call(
        turn_kernel,
        [shape((pert, blocks * HALF), F32), pair_array, pair_array] + msgs,
        "svvvvvvvv",
        [ext] + accs,
        name="turn",
    )(columns, t1, state, *ghosts, m, weight)
    ghosts = [rotated(v, -o) for v, o in zip(out, OFFSET_LIST)]
    hot, terms = call(
        prepare_kernel,
        [shape((parts * LANES, 7 * LANES), BF16), shape((pert, LANES), F32)],
        "vvvvvvvv",
        name="prepare",
        moved=4 << 20,
    )(patch, names, *carried, target, w)
    terms = call(
        last_kernel,
        shape((parts * perts, pert + 8, LANES), BF16),
        "ss" + "v" * 15,
        [held] + accs,
        name="last",
    )(columns, send_list, base, target, *ghosts, m, v, *carried, hot, terms, got)
    terms = lax.all_to_all(terms, ("dom", "pert"), 0, 0, tiled=True)
    hessian_probe, curvature = call(
        functools.partial(owner_kernel, parts=parts, scale=1.0 / (pert * perts)),
        [shape(probes.shape, F32), shape((1, LANES), F32)],
        "v",
        name="owner",
    )(terms)
    return tangent, hessian_probe, curvature.reshape(-1)


def solution(mesh):
    in_specs = (
        P("pert", "dom"),
        P("dom"),
        P("dom"),
        P("dom", None, None),
        P("dom", None, None),
        P("dom", None),
        P("dom", None, None),
        P("dom"),
    )
    out_specs = (P("pert", "dom"), P("pert", "dom"), P("dom"))
    return jax.shard_map(shards, mesh=mesh, in_specs=in_specs, out_specs=out_specs, check_vma=False)
```

```python
import functools

import jax
import jax.numpy as jnp
from jax import lax
from jax.experimental import pallas as pl
from jax.experimental.pallas import tpu as pltpu
from jax.sharding import PartitionSpec as P

OFFSET_LIST = (-2, -1, 1, 2)
F32 = jnp.float32
BF16 = jnp.bfloat16
LANES = 128
HALF = 64
QUAD = 4
RADIX = 64

VMEM = pl.BlockSpec(memory_space=pltpu.VMEM)
SMEM = pl.BlockSpec(memory_space=pltpu.SMEM)
HBM = pl.BlockSpec(memory_space=pltpu.HBM)
MIB = 1024 * 1024


def low_half(shape):
    return lax.broadcasted_iota(jnp.int32, shape, len(shape) - 1) < HALF


def swap_halves(value):
    return pltpu.roll(value, HALF, 1)


def rotated(value, by):
    peers = lax.axis_size("dom")
    return lax.ppermute(value, "dom", [(i, (i + by) % peers) for i in range(peers)])


def neighbours(parts):
    me = lax.axis_index("dom")
    return [lax.rem(me - offset + parts, parts) for offset in OFFSET_LIST]


def melt_kernel(
    send_hbm, melt_hbm, patch_hbm, probe_hbm, diag_hbm, w_ref, out_ref,
    send_ref, melt_ref, patch_ref, probe_ref, diag_ref, sems, *, parts,
):
    copies = [
        pltpu.make_async_copy(source, target, sems.at[number])
        for number, (source, target) in enumerate(
            (
                (diag_hbm, diag_ref),
                (melt_hbm, melt_ref),
                (patch_hbm, patch_ref),
                (probe_hbm, probe_ref),
                (send_hbm, send_ref),
            )
        )
    ]
    for copy in copies:
        copy.start()
    for copy in copies:
        copy.wait()
    pairs = melt_ref.shape[0]
    pert = probe_ref.shape[0]
    capacity = send_ref.shape[2]
    low = low_half((1, LANES))
    lane = lax.broadcasted_iota(jnp.int32, (HALF, LANES), 1)
    turned = jnp.transpose(jnp.concatenate([melt_ref[...], jnp.zeros((LANES - pairs, LANES), F32)], axis=0))
    even = jnp.take_along_axis(turned[:HALF], lane // 2, axis=1)
    odd = jnp.take_along_axis(turned[HALF:], lane // 2, axis=1)
    melt = jnp.where(lane % 2 == 0, even, odd)
    sums = [
        jnp.sum(diag_ref[i].astype(F32) * melt, axis=0, keepdims=True)
        for i in range(diag_ref.shape[0])
    ]
    sums = jnp.concatenate(sums, axis=0)
    source = 2 * (lane % HALF)
    both = jnp.concatenate(
        [
            jnp.take_along_axis(sums, source, axis=1),
            jnp.take_along_axis(sums, source + 1, axis=1),
        ],
        axis=0,
    )
    w_ref[...] = jnp.transpose(both)[:pairs]
    patch_row = jnp.broadcast_to(patch_ref[...].astype(F32), (8, LANES))
    lane = lax.broadcasted_iota(jnp.int32, (8, LANES), 1)
    for part in range(parts):
        out_ref[part, :pert] = probe_ref[...]
    me = lax.axis_index("dom")
    for group, offset in enumerate(OFFSET_LIST):
        to = lax.rem(me + offset + parts, parts)
        ids = jnp.zeros((8, LANES), jnp.int32)
        for slot in range(capacity):
            block = jnp.maximum(send_ref[0, group, slot], 0)
            row = w_ref[pl.ds(block // 2, 1), :]
            out_ref[to, pert + slot : pert + slot + 1, :] = jnp.where(
                low == (block % 2 == 0), row, swap_halves(row)
            )
            ids = jnp.where(lane == group * capacity + slot, block, ids)
        mine = (lane >= group * capacity) & (lane < (group + 1) * capacity)
        out_ref[to, pert + capacity :, :] = jnp.where(
            mine, jnp.take_along_axis(patch_row, ids, axis=1), 0.0
        )


def gather_rows(quad, cols_ref, ext_ref, low):
    rows = []
    for place in range(QUAD):
        g = quad * QUAD + place
        tiles = [ext_ref[cols_ref[k, g]] for k in range(4)]
        rows.append(
            jnp.concatenate(
                [jnp.where(low, tiles[0], tiles[1]), jnp.where(low, tiles[2], tiles[3])], axis=1
            )
        )
    return rows


def coupled_rows(quad, rows, m_ref):
    rhs = m_ref[pl.ds(quad * QUAD, QUAD)].reshape(QUAD * HALF, 4 * HALF)
    return lax.dot_general(
        jnp.concatenate(rows, axis=0), rhs, (((1,), (1,)), ((), ())), preferred_element_type=F32
    )


def own_pairs(out, size, low):
    first = jnp.where(low, out[:size, :LANES], out[size : 2 * size, :LANES])
    second = jnp.where(low, out[2 * size : 3 * size, LANES:], out[3 * size : 4 * size, LANES:])
    return first, second


def gather_multiply(quad, cols_ref, ext_ref, m_ref, low):
    out = coupled_rows(quad, gather_rows(quad, cols_ref, ext_ref, low), m_ref)
    return own_pairs(out, out.shape[0] // QUAD, low)


def store_pair(ref, pair, value, low):
    value = value.astype(BF16)
    other = swap_halves(value.astype(F32)).astype(BF16)
    ref[2 * pair] = jnp.where(low, value, other)
    ref[2 * pair + 1] = jnp.where(low, other, value)


def fill_messages(send_ref, ref, msg_refs, low):
    for group, msg_ref in enumerate(msg_refs):
        for pair in range(send_ref.shape[2] // 2):
            even, odd = (
                ref[jnp.maximum(send_ref[0, group, 2 * pair + half], 0)] for half in range(2)
            )
            msg_ref[pair] = jnp.where(low, even, odd)


def product_kernel(diag_ref, coupling_hbm, m_hbm, coupling_ref, m_ref, in_sems, out_sems):
    chunks = in_sems.shape[0]
    size = diag_ref.shape[0] // chunks
    spans = [pl.ds(chunk * size, size) for chunk in range(chunks)]
    loads = [
        pltpu.make_async_copy(coupling_hbm.at[span], coupling_ref.at[span], in_sems.at[chunk])
        for chunk, span in enumerate(spans)
    ]
    stores = [
        pltpu.make_async_copy(m_ref.at[span], m_hbm.at[span], out_sems.at[chunk])
        for chunk, span in enumerate(spans)
    ]
    for load in loads:
        load.start()
    for chunk in range(chunks):
        loads[chunk].wait()
        for block in range(chunk * size, (chunk + 1) * size):
            m_ref[block] = jnp.dot(
                diag_ref[block], coupling_ref[block], preferred_element_type=F32
            ).astype(BF16)
        stores[chunk].start()
    for store in stores:
        store.wait()


def patches_of_columns(columns_ref, ids):
    columns = jnp.concatenate([columns_ref[...], columns_ref[...]], axis=0)
    here = jnp.broadcast_to(ids[:, :LANES], columns.shape)
    there = jnp.broadcast_to(ids[:, LANES:], columns.shape)
    return jnp.where(
        columns < LANES,
        jnp.take_along_axis(here, jnp.minimum(columns, LANES - 1), axis=1),
        jnp.take_along_axis(there, jnp.maximum(columns - LANES, 0), axis=1),
    )


def first_kernel(
    cols_ref, send_ref, patch_ref, columns_ref, got_ref, w_hbm, m_hbm,
    m_ref, v_ref, names_ref, t1_ref, t2_ref, o0, o1, o2, o3,
    ext_ref, row_ref, w_ref, w_sem, sems,
):
    w_copy = pltpu.make_async_copy(w_hbm, w_ref, w_sem)
    w_copy.start()
    chunks = sems.shape[0]
    size = m_ref.shape[0] // chunks
    copies = []
    for chunk in range(chunks):
        span = pl.ds(chunk * size, size)
        copies.append(pltpu.make_async_copy(m_hbm.at[span], m_ref.at[span], sems.at[chunk]))
        copies[-1].start()
    pert = t1_ref.shape[1]
    capacity = send_ref.shape[2]
    blocks = cols_ref.shape[1]
    parts = got_ref.shape[0]
    sources = neighbours(parts)
    low = low_half((pert, LANES))
    lane = lax.broadcasted_iota(jnp.int32, (1, LANES), 1)
    ghost_ids = sum(got_ref[source, pert + capacity : pert + capacity + 1, :] for source in sources)
    ghost_ids = jnp.where(lane < 4 * capacity, ghost_ids, -1.0)
    ids = jnp.concatenate([patch_ref[...].astype(F32), ghost_ids], axis=1)
    total = jnp.zeros((3 * pert, 2 * LANES), F32)
    for part in range(parts):
        names = (
            lax.broadcasted_iota(jnp.int32, (LANES, 2 * LANES), 0) + part * LANES
        ).astype(F32)
        hot = jnp.where(names == ids, 1.0, 0.0).astype(BF16)
        value = got_ref[part, :pert]
        top = value.astype(BF16)
        rest = value - top.astype(F32)
        mid = rest.astype(BF16)
        last = (rest - mid.astype(F32)).astype(BF16)
        total = total + jnp.dot(
            jnp.concatenate([top, mid, last], axis=0), hot, preferred_element_type=F32
        )
    picked = total[:pert] + total[pert : 2 * pert] + total[2 * pert :]
    local_picked = picked[:, :LANES]
    ghost_picked = picked[:, LANES:]
    full_low = low.astype(jnp.int32)
    column_patches = patches_of_columns(columns_ref, ids)
    sub = lax.broadcasted_iota(jnp.int32, (8, LANES), 0)
    lane8 = lax.broadcasted_iota(jnp.int32, (8, LANES), 1)
    wanted = sub == lane8 % 4

    def listed(blocks_of_lanes):
        taken = jnp.take_along_axis(column_patches, blocks_of_lanes, axis=1)
        return jnp.sum(jnp.where(wanted, taken, 0.0), axis=0, keepdims=True)

    for tile in range(4 * blocks // LANES):
        names_ref[tile : tile + 1, :] = listed(tile * (LANES // 4) + lane8 // 4)
    w_copy.wait()
    w = w_ref[...]
    w_other = swap_halves(w)
    low_w = low_half(w.shape)
    row_ref[pl.ds(0, blocks // 2, stride=2), :] = jnp.where(low_w, w, w_other)
    row_ref[pl.ds(1, blocks // 2, stride=2), :] = jnp.where(low_w, w_other, w)
    for group, source in enumerate(sources):
        start = blocks + group * capacity
        row_ref[start : start + capacity, :] = got_ref[source, pert : pert + capacity, :]

    def seed(pair, _):
        index = 2 * pair + 1 - full_low
        spread = jnp.take_along_axis(local_picked, index, axis=1)
        value = spread * w_ref[pl.ds(pair, 1), :]
        t1_ref[pair] = value
        store_pair(ext_ref, pair, value, low)
        return 0

    lax.fori_loop(0, blocks // 2, seed, 0, unroll=16)
    for group, source in enumerate(sources):
        for slot in range(capacity):
            place = group * capacity + slot
            row = got_ref[source, pert + slot : pert + slot + 1, :]
            spread = jnp.broadcast_to(ghost_picked[:, place : place + 1], (pert, LANES))
            ext_ref[blocks + place] = (spread * row).astype(BF16)

    for copy in copies:
        copy.wait()
    low8 = low_half((8, LANES))
    masks = [(sub % 4 == k) & (low8 if k % 2 == 0 else ~low8) for k in range(4)]
    nothing = jnp.zeros((8, LANES), F32)

    def sweep(quad, _):
        rows = gather_rows(quad, cols_ref, ext_ref, low)
        tiles = ([], [])
        for place in range(QUAD):
            w_rows = [row_ref[pl.ds(cols_ref[k, quad * QUAD + place], 1), :] for k in range(4)]
            for side in range(2):
                tiles[side].append(
                    jnp.where(
                        masks[2 * side],
                        w_rows[2 * side],
                        jnp.where(masks[2 * side + 1], w_rows[2 * side + 1], nothing),
                    )
                )
        extra = jnp.concatenate([jnp.concatenate(side, axis=0) for side in tiles], axis=1)
        out = coupled_rows(quad, rows + [extra.astype(BF16)], m_ref)
        for place, value in enumerate(own_pairs(out, pert, low)):
            pair = 2 * quad + place
            store_pair(t2_ref, pair, t1_ref[pair] - value, low)
        for place, value in enumerate(own_pairs(out[QUAD * pert :], 8, low8)):
            v_ref[2 * quad + place] = value
        return 0

    lax.fori_loop(0, blocks // QUAD, sweep, 0, unroll=32)
    msgs = (o0, o1, o2, o3)
    fill_messages(send_ref, t2_ref, msgs, low)
    half = capacity // 2
    for group, ref in enumerate(msgs):
        places = jnp.zeros((8, LANES), jnp.int32)
        values = []
        for slot in range(capacity):
            block = jnp.maximum(send_ref[0, group, slot], 0)
            value = v_ref[block // 2]
            right = (slot - block) % 2 == 0
            values.append(jnp.where(right, value, swap_halves(value)))
            places = jnp.where(lane8 // 4 == slot, block, places)
        pairs = [
            jnp.where(low8, values[2 * pair], values[2 * pair + 1]) for pair in range(half)
        ]
        for tile in range(half // 2):
            ref[half + tile] = jnp.concatenate(pairs[2 * tile : 2 * tile + 2], axis=0).astype(BF16)
        patch = listed(places).astype(jnp.int32)
        ref[half + half // 2] = jnp.concatenate(
            [
                jnp.broadcast_to(patch // RADIX, (8, LANES)),
                jnp.broadcast_to(patch % RADIX, (8, LANES)),
            ],
            axis=0,
        ).astype(F32).astype(BF16)


def extend(ext_ref, local_ref, ghosts, low):
    blocks = local_ref.shape[0]
    count = (ext_ref.shape[0] - blocks) // 2 // len(ghosts)
    ext_ref[:blocks] = local_ref[...]
    for group, ref in enumerate(ghosts):
        for pair in range(count):
            store_pair(ext_ref, blocks // 2 + group * count + pair, ref[pair], low)


def sweep_kernel(
    cols_ref, send_ref, t1_ref, prev_ref, g0, g1, g2, g3, m_ref,
    next_ref, o0, o1, o2, o3, ext_ref,
):
    low = low_half(prev_ref.shape[1:])
    extend(ext_ref, prev_ref, (g0, g1, g2, g3), low)

    def sweep(quad, _):
        first, second = gather_multiply(quad, cols_ref, ext_ref, m_ref, low)
        store_pair(next_ref, 2 * quad, t1_ref[2 * quad] - first, low)
        store_pair(next_ref, 2 * quad + 1, t1_ref[2 * quad + 1] - second, low)
        return 0

    lax.fori_loop(0, cols_ref.shape[1] // QUAD, sweep, 0, unroll=32)
    fill_messages(send_ref, next_ref, (o0, o1, o2, o3), low)


def clear(acc_refs):
    def one(place, _):
        for ref in acc_refs:
            ref[place] = jnp.zeros(ref.shape[1:], F32)
        return 0

    lax.fori_loop(0, acc_refs[0].shape[0], one, 0, unroll=16)


def multiply_scatter(quad, cols_ref, pairs, m_ref, acc_refs, low):
    zero = jnp.zeros(pairs[0].shape, F32)
    rows = []
    for place in range(QUAD):
        value = pairs[place // 2]
        kept = jnp.where(low, value, zero) if place % 2 == 0 else jnp.where(low, zero, value)
        tiles = [kept, zero] if place < 2 else [zero, kept]
        rows.append(jnp.concatenate(tiles, axis=1))
    lhs = jnp.concatenate(rows, axis=0).astype(BF16)
    rhs = m_ref[pl.ds(quad * QUAD, QUAD)].reshape(QUAD * HALF, 4 * HALF)
    out = jnp.dot(lhs, rhs, preferred_element_type=F32)
    p = pairs[0].shape[0]
    for place in range(QUAD):
        g = quad * QUAD + place
        for k in range(4):
            column = cols_ref[k, g]
            piece = out[place * p : (place + 1) * p, (k // 2) * LANES : (k // 2 + 1) * LANES]
            acc_refs[k][column] = acc_refs[k][column] + piece


def half_sums(acc_refs, place, low):
    return jnp.where(
        low, acc_refs[0][place] + acc_refs[2][place], acc_refs[1][place] + acc_refs[3][place]
    )


def pair_sum(acc_refs, pair, low):
    even = half_sums(acc_refs, 2 * pair, low)
    odd = half_sums(acc_refs, 2 * pair + 1, low)
    return jnp.where(low, even, odd) + swap_halves(jnp.where(low, odd, even))


def finish_round(base_ref, target_ref, acc_refs, msg_refs, blocks, low):
    def local(pair, _):
        base_ref[pair] = target_ref[pair] - pair_sum(acc_refs, pair, low)
        return 0

    lax.fori_loop(0, blocks // 2, local, 0, unroll=16)
    for group, ref in enumerate(msg_refs):
        count = ref.shape[0]
        for pair in range(count):
            ref[pair] = pair_sum(acc_refs, blocks // 2 + group * count + pair, low).astype(BF16)


def turn_kernel(
    cols_ref, t1_ref, prev_ref, g0, g1, g2, g3, m_ref, weight_ref,
    tangent_ref, target_ref, base_ref, o0, o1, o2, o3, ext_ref, *acc_refs,
):
    low = low_half(prev_ref.shape[1:])
    blocks = cols_ref.shape[1]
    extend(ext_ref, prev_ref, (g0, g1, g2, g3), low)

    def sweep(quad, _):
        coupled = gather_multiply(quad, cols_ref, ext_ref, m_ref, low)
        for place in range(2):
            pair = 2 * quad + place
            value = t1_ref[pair] - coupled[place]
            start = pl.multiple_of(pair * LANES, LANES)
            tangent_ref[:, pl.ds(start, LANES)] = value
            target_ref[pair] = value * weight_ref[pl.ds(pair, 1), :]
        return 0

    lax.fori_loop(0, blocks // QUAD, sweep, 0, unroll=32)
    scatter_all(cols_ref, target_ref, m_ref, acc_refs, low)
    finish_round(base_ref, target_ref, acc_refs, (o0, o1, o2, o3), blocks, low)


def take_returned(send_ref, base_ref, u_ref, ghosts, low):
    u_ref[...] = base_ref[...]
    which = 1 - low.astype(jnp.int32)
    for group, ref in enumerate(ghosts):
        for pair in range(ref.shape[0]):
            value = ref[pair].astype(F32)
            other = swap_halves(value)
            for half, both in enumerate(
                (jnp.where(low, value, other), jnp.where(low, other, value))
            ):
                block = send_ref[0, group, 2 * pair + half]
                place = jnp.maximum(block, 0) // 2
                wanted = jnp.where(block < 0, 2, block % 2)
                u_ref[place] = u_ref[place] - jnp.where(which == wanted, both, 0.0)


def scatter_all(cols_ref, u_ref, m_ref, acc_refs, low):
    clear(acc_refs)

    def sweep(quad, _):
        pairs = [u_ref[2 * quad], u_ref[2 * quad + 1]]
        multiply_scatter(quad, cols_ref, pairs, m_ref, acc_refs, low)
        return 0

    lax.fori_loop(0, cols_ref.shape[1] // QUAD, sweep, 0, unroll=32)


def prepare_kernel(
    patch_ref, names_ref, g0, g1, g2, g3, target_ref, w_ref, hot_ref, terms_ref
):
    pairs, pert, _ = target_ref.shape
    low8 = low_half((1, LANES))
    rows = [patch_ref[...].astype(F32)] + [names_ref[tile : tile + 1] for tile in range(4)]
    ghosts = []
    for ref in (g0, g1, g2, g3):
        digits = ref[ref.shape[0] - 1].astype(F32)
        ghosts.append(digits[0:1] * RADIX + digits[8:9])
    for tile in range(2):
        rows.append(jnp.where(low8, ghosts[2 * tile], swap_halves(ghosts[2 * tile + 1])))
    low = low_half((pert, LANES))
    lane = lax.broadcasted_iota(jnp.int32, (pert, LANES), 1)
    first = lax.broadcasted_iota(jnp.int32, (LANES, LANES), 0).astype(F32)

    def one(part, _):
        start = pl.multiple_of(part * LANES, LANES)
        base = (part * LANES).astype(F32)
        for tile, row in enumerate(rows):
            hot_ref[pl.ds(start, LANES), tile * LANES : (tile + 1) * LANES] = jnp.where(
                first == row - base, 1.0, 0.0
            ).astype(BF16)
        return 0

    lax.fori_loop(0, hot_ref.shape[0] // LANES, one, 0, unroll=2)

    def local(pair, terms):
        value = target_ref[pair] * w_ref[pl.ds(pair, 1), :]
        even = jnp.sum(jnp.where(low, value, 0.0), axis=1, keepdims=True)
        odd = jnp.sum(jnp.where(low, 0.0, value), axis=1, keepdims=True)
        return jnp.where(lane == 2 * pair, even, jnp.where(lane == 2 * pair + 1, odd, terms))

    terms_ref[...] = lax.fori_loop(0, pairs, local, jnp.zeros((pert, LANES), F32), unroll=16)


def last_kernel(
    cols_ref, send_ref, base_in_ref, target_ref, g0, g1, g2, g3, m_ref, v_ref, v0, v1, v2, v3,
    hot_ref, terms_ref, got_ref, out_ref, u_ref, *acc_refs,
):
    pert = u_ref.shape[1]
    blocks = cols_ref.shape[1]
    half = send_ref.shape[2] // 2
    parts = got_ref.shape[0]
    low = low_half(u_ref.shape[1:])
    take_returned(send_ref, base_in_ref, u_ref, (g0, g1, g2, g3), low)
    scatter_all(cols_ref, u_ref, m_ref, acc_refs, low)
    sub = lax.broadcasted_iota(jnp.int32, (8, LANES), 0)
    own = (sub < 4) == low_half((8, LANES))
    nothing = jnp.zeros((8, LANES), F32)

    def products(pair, first_v, second_v, first_z, second_z):
        rhs = jnp.concatenate(
            [
                jnp.concatenate([jnp.where(own, first_v, nothing), nothing], axis=1),
                jnp.concatenate([nothing, jnp.where(own, second_v, nothing)], axis=1),
            ],
            axis=0,
        )
        lhs = jnp.concatenate([first_z, second_z], axis=1)
        return lax.dot_general(
            lhs.astype(BF16), rhs.astype(BF16), (((1,), (1,)), ((), ())),
            preferred_element_type=F32,
        )

    pieces = []
    for pair in range(0, blocks // 2, 2):
        z = [pair_sum(acc_refs, pair + i, low) - target_ref[pair + i] for i in range(2)]
        pieces.append(products(pair, v_ref[pair], v_ref[pair + 1], *z))
    for group, ref in enumerate((v0, v1, v2, v3)):
        for tile in range(half // 2):
            both = ref[half + tile].astype(F32)
            pair = blocks // 2 + group * half + 2 * tile
            z = [pair_sum(acc_refs, pair + i, low) for i in range(2)]
            pieces.append(products(pair, both[:8], both[8:], *z))
    terms = jnp.concatenate([terms_ref[...]] + pieces, axis=1)
    top = terms.astype(BF16)
    rest = (terms - top.astype(F32)).astype(BF16)
    both = jnp.concatenate([top, rest], axis=0)
    perts = out_ref.shape[0] // parts
    sub = lax.broadcasted_iota(jnp.int32, (8, LANES), 0)
    for part in range(parts):
        hot = hot_ref[part * LANES : (part + 1) * LANES, :]
        out = lax.dot_general(both, hot, (((1,), (1,)), ((), ())), preferred_element_type=F32)
        value = out[:pert] + out[pert:]
        curve = jnp.sum(value * got_ref[part, :pert], axis=0, keepdims=True)
        top = curve.astype(BF16).astype(F32)
        extra = jnp.where(sub == 0, top, jnp.where(sub == 1, curve - top, 0.0))
        for place in range(perts):
            out_ref[part * perts + place, :pert] = value.astype(BF16)
            out_ref[part * perts + place, pert:] = extra.astype(BF16)


def owner_kernel(terms_ref, hessian_ref, curve_ref, *, parts, scale):
    pert = hessian_ref.shape[0]
    perts = terms_ref.shape[0] // parts
    mine = lax.axis_index("pert")
    total = jnp.zeros(hessian_ref.shape, F32)
    for part in range(parts):
        total = total + terms_ref[part * perts + mine, :pert].astype(F32)
    hessian_ref[...] = total
    curve = jnp.zeros((8, LANES), F32)
    for place in range(terms_ref.shape[0]):
        curve = curve + terms_ref[place, pert:].astype(F32)
    curve_ref[...] = (curve[0:1] + curve[1:2]) * scale


def call(body, outs, spaces, scratch=(), name=None, flops=0, moved=1 << 20, limit=12, out_specs=None):
    return pl.pallas_call(
        body,
        out_shape=outs,
        in_specs=[{"s": SMEM, "v": VMEM, "h": HBM}[s] for s in spaces],
        out_specs=out_specs or jax.tree.map(lambda _: VMEM, outs),
        scratch_shapes=list(scratch),
        compiler_params=pltpu.CompilerParams(vmem_limit_bytes=limit * MIB),
        name=name,
        cost_estimate=pl.CostEstimate(flops=flops, transcendentals=0, bytes_accessed=moved),
    )


def shards(
    probes, melt_shape, obs_weight, diag_inverse, coupling, columns, send_list, patch_of_block
):
    pert = probes.shape[0]
    blocks = coupling.shape[0]
    capacity = send_list.shape[2]
    parts = lax.axis_size("dom")
    pairs = blocks // 2
    shape = jax.ShapeDtypeStruct
    msgs = [shape((capacity // 2, pert, LANES), BF16)] * 4
    pair_array = shape((pairs, pert, LANES), F32)
    block_array = shape((blocks, pert, LANES), BF16)
    ext = pltpu.VMEM((blocks + 4 * capacity, pert, LANES), BF16)
    accs = [pltpu.VMEM((blocks + 4 * capacity, pert, LANES), F32)] * 4
    held = pltpu.VMEM((pairs, pert, LANES), F32)
    melt = melt_shape.reshape(pairs, LANES)
    weight = obs_weight.reshape(pairs, LANES)
    patch = patch_of_block.reshape(1, blocks)

    perts = lax.axis_size("pert")
    columns = columns.T
    w, outgoing = call(
        functools.partial(melt_kernel, parts=parts),
        [shape((pairs, LANES), F32), shape((parts, pert + capacity + 8, LANES), F32)],
        "hhhhh",
        [
            pltpu.SMEM(send_list.shape, jnp.int32),
            pltpu.VMEM((pairs, LANES), F32),
            pltpu.VMEM((1, blocks), jnp.int32),
            pltpu.VMEM(probes.shape, F32),
            pltpu.VMEM((HALF, HALF, blocks), BF16),
            pltpu.SemaphoreType.DMA((5,)),
        ],
        name="melt",
        limit=60,
    )(send_list, melt, patch, probes, jnp.transpose(diag_inverse, (1, 2, 0)))
    got = lax.all_to_all(outgoing, "dom", 0, 0, tiled=True)
    wide = [shape((capacity // 2 + capacity // 4 + 1, pert, LANES), BF16)] * 4
    m = call(
        product_kernel,
        shape(coupling.shape, BF16),
        "vh",
        [pltpu.VMEM(coupling.shape, BF16)] * 2 + [pltpu.SemaphoreType.DMA((8,))] * 2,
        out_specs=HBM,
        name="product",
        flops=1 << 28,
        moved=10 << 20,
        limit=50,
    )(diag_inverse, coupling)
    m, v, names, t1, state, *out = call(
        first_kernel,
        [
            shape(coupling.shape, BF16),
            shape((pairs, 8, LANES), F32),
            shape((8, LANES), F32),
            pair_array,
            block_array,
        ]
        + wide,
        "ssvvvhh",
        [
            ext,
            pltpu.VMEM((blocks + 4 * capacity, LANES), F32),
            pltpu.VMEM((pairs, LANES), F32),
            pltpu.SemaphoreType.DMA,
            pltpu.SemaphoreType.DMA((8,)),
        ],
        name="first",
        limit=47,
    )(columns, send_list, patch, columns, got, w, m)
    carried = [rotated(x, o) for x, o in zip(out, OFFSET_LIST)]
    state, *out = call(
        sweep_kernel, [block_array] + msgs, "ssvvvvvvv", [ext], name="sweep"
    )(columns, send_list, t1, state, *carried, m)
    ghosts = [rotated(v, o) for v, o in zip(out, OFFSET_LIST)]
    tangent, target, base, *out = call(
        turn_kernel,
        [shape((pert, blocks * HALF), F32), pair_array, pair_array] + msgs,
        "svvvvvvvv",
        [ext] + accs,
        name="turn",
    )(columns, t1, state, *ghosts, m, weight)
    ghosts = [rotated(v, -o) for v, o in zip(out, OFFSET_LIST)]
    hot, terms = call(
        prepare_kernel,
        [shape((parts * LANES, 7 * LANES), BF16), shape((pert, LANES), F32)],
        "vvvvvvvv",
        name="prepare",
        moved=4 << 20,
    )(patch, names, *carried, target, w)
    terms = call(
        last_kernel,
        shape((parts * perts, pert + 8, LANES), BF16),
        "ss" + "v" * 15,
        [held] + accs,
        name="last",
    )(columns, send_list, base, target, *ghosts, m, v, *carried, hot, terms, got)
    terms = lax.all_to_all(terms, ("dom", "pert"), 0, 0, tiled=True)
    hessian_probe, curvature = call(
        functools.partial(owner_kernel, parts=parts, scale=1.0 / (pert * perts)),
        [shape(probes.shape, F32), shape((1, LANES), F32)],
        "v",
        name="owner",
    )(terms)
    return tangent, hessian_probe, curvature.reshape(-1)


def solution(mesh):
    in_specs = (
        P("pert", "dom"),
        P("dom"),
        P("dom"),
        P("dom", None, None),
        P("dom", None, None),
        P("dom", None),
        P("dom", None, None),
        P("dom"),
    )
    out_specs = (P("pert", "dom"), P("pert", "dom"), P("dom"))
    return jax.shard_map(shards, mesh=mesh, in_specs=in_specs, out_specs=out_specs, check_vma=False)
```

```python
import functools

import jax
import jax.numpy as jnp
from jax import lax
from jax.experimental import pallas as pl
from jax.experimental.pallas import tpu as pltpu
from jax.sharding import PartitionSpec as P

OFFSET_LIST = (-2, -1, 1, 2)
F32 = jnp.float32
BF16 = jnp.bfloat16
LANES = 128
HALF = 64
QUAD = 4
RADIX = 64

VMEM = pl.BlockSpec(memory_space=pltpu.VMEM)
SMEM = pl.BlockSpec(memory_space=pltpu.SMEM)
HBM = pl.BlockSpec(memory_space=pltpu.HBM)
MIB = 1024 * 1024


def low_half(shape):
    return lax.broadcasted_iota(jnp.int32, shape, len(shape) - 1) < HALF


def swap_halves(value):
    return pltpu.roll(value, HALF, 1)


def rotated(value, by):
    peers = lax.axis_size("dom")
    return lax.ppermute(value, "dom", [(i, (i + by) % peers) for i in range(peers)])


def neighbours(parts):
    me = lax.axis_index("dom")
    return [lax.rem(me - offset + parts, parts) for offset in OFFSET_LIST]


def melt_kernel(
    send_hbm, melt_hbm, patch_hbm, probe_hbm, diag_hbm, w_ref, out_ref,
    send_ref, melt_ref, patch_ref, probe_ref, diag_ref, sems, *, parts,
):
    copies = [
        pltpu.make_async_copy(source, target, sems.at[number])
        for number, (source, target) in enumerate(
            (
                (diag_hbm, diag_ref),
                (melt_hbm, melt_ref),
                (patch_hbm, patch_ref),
                (probe_hbm, probe_ref),
                (send_hbm, send_ref),
            )
        )
    ]
    for copy in copies:
        copy.start()
    for copy in copies:
        copy.wait()
    pairs = melt_ref.shape[0]
    pert = probe_ref.shape[0]
    capacity = send_ref.shape[2]
    low = low_half((1, LANES))
    lane = lax.broadcasted_iota(jnp.int32, (HALF, LANES), 1)
    turned = jnp.transpose(jnp.concatenate([melt_ref[...], jnp.zeros((LANES - pairs, LANES), F32)], axis=0))
    even = jnp.take_along_axis(turned[:HALF], lane // 2, axis=1)
    odd = jnp.take_along_axis(turned[HALF:], lane // 2, axis=1)
    melt = jnp.where(lane % 2 == 0, even, odd)
    sums = [
        jnp.sum(diag_ref[i].astype(F32) * melt, axis=0, keepdims=True)
        for i in range(diag_ref.shape[0])
    ]
    sums = jnp.concatenate(sums, axis=0)
    source = 2 * (lane % HALF)
    both = jnp.concatenate(
        [
            jnp.take_along_axis(sums, source, axis=1),
            jnp.take_along_axis(sums, source + 1, axis=1),
        ],
        axis=0,
    )
    w_ref[...] = jnp.transpose(both)[:pairs]
    patch_row = jnp.broadcast_to(patch_ref[...].astype(F32), (8, LANES))
    lane = lax.broadcasted_iota(jnp.int32, (8, LANES), 1)
    for part in range(parts):
        out_ref[part, :pert] = probe_ref[...]
    me = lax.axis_index("dom")
    for group, offset in enumerate(OFFSET_LIST):
        to = lax.rem(me + offset + parts, parts)
        ids = jnp.zeros((8, LANES), jnp.int32)
        for slot in range(capacity):
            block = jnp.maximum(send_ref[0, group, slot], 0)
            row = w_ref[pl.ds(block // 2, 1), :]
            out_ref[to, pert + slot : pert + slot + 1, :] = jnp.where(
                low == (block % 2 == 0), row, swap_halves(row)
            )
            ids = jnp.where(lane == group * capacity + slot, block, ids)
        mine = (lane >= group * capacity) & (lane < (group + 1) * capacity)
        out_ref[to, pert + capacity :, :] = jnp.where(
            mine, jnp.take_along_axis(patch_row, ids, axis=1), 0.0
        )


def gather_rows(quad, cols_ref, ext_ref, low):
    rows = []
    for place in range(QUAD):
        g = quad * QUAD + place
        tiles = [ext_ref[cols_ref[k, g]] for k in range(4)]
        rows.append(
            jnp.concatenate(
                [jnp.where(low, tiles[0], tiles[1]), jnp.where(low, tiles[2], tiles[3])], axis=1
            )
        )
    return rows


def coupled_rows(quad, rows, m_ref):
    rhs = m_ref[pl.ds(quad * QUAD, QUAD)].reshape(QUAD * HALF, 4 * HALF)
    return lax.dot_general(
        jnp.concatenate(rows, axis=0), rhs, (((1,), (1,)), ((), ())), preferred_element_type=F32
    )


def own_pairs(out, size, low):
    first = jnp.where(low, out[:size, :LANES], out[size : 2 * size, :LANES])
    second = jnp.where(low, out[2 * size : 3 * size, LANES:], out[3 * size : 4 * size, LANES:])
    return first, second


def gather_multiply(quad, cols_ref, ext_ref, m_ref, low):
    out = coupled_rows(quad, gather_rows(quad, cols_ref, ext_ref, low), m_ref)
    return own_pairs(out, out.shape[0] // QUAD, low)


def store_pair(ref, pair, value, low):
    value = value.astype(BF16)
    other = swap_halves(value.astype(F32)).astype(BF16)
    ref[2 * pair] = jnp.where(low, value, other)
    ref[2 * pair + 1] = jnp.where(low, other, value)


def fill_messages(send_ref, ref, msg_refs, low):
    for group, msg_ref in enumerate(msg_refs):
        for pair in range(send_ref.shape[2] // 2):
            even, odd = (
                ref[jnp.maximum(send_ref[0, group, 2 * pair + half], 0)] for half in range(2)
            )
            msg_ref[pair] = jnp.where(low, even, odd)


def patches_of_columns(columns_ref, ids):
    columns = jnp.concatenate([columns_ref[...], columns_ref[...]], axis=0)
    here = jnp.broadcast_to(ids[:, :LANES], columns.shape)
    there = jnp.broadcast_to(ids[:, LANES:], columns.shape)
    return jnp.where(
        columns < LANES,
        jnp.take_along_axis(here, jnp.minimum(columns, LANES - 1), axis=1),
        jnp.take_along_axis(there, jnp.maximum(columns - LANES, 0), axis=1),
    )


def first_kernel(
    cols_ref, send_ref, patch_ref, columns_ref, got_ref, w_hbm, diag_ref, coupling_hbm,
    m_ref, v_ref, names_ref, patches_ref, t1_ref, t2_ref, o0, o1, o2, o3,
    ext_ref, row_ref, w_ref, coupling_ref, w_sem, sems,
):
    w_copy = pltpu.make_async_copy(w_hbm, w_ref, w_sem)
    w_copy.start()
    chunks = sems.shape[0]
    size = diag_ref.shape[0] // chunks
    copies = [
        pltpu.make_async_copy(
            coupling_hbm.at[chunk * size : (chunk + 1) * size],
            coupling_ref.at[chunk * size : (chunk + 1) * size],
            sems.at[chunk],
        )
        for chunk in range(chunks)
    ]
    for copy in copies:
        copy.start()
    pert = t1_ref.shape[1]
    capacity = send_ref.shape[2]
    blocks = cols_ref.shape[1]
    parts = got_ref.shape[0]
    sources = neighbours(parts)
    low = low_half((pert, LANES))
    lane = lax.broadcasted_iota(jnp.int32, (1, LANES), 1)
    ghost_ids = sum(got_ref[source, pert + capacity : pert + capacity + 1, :] for source in sources)
    ghost_ids = jnp.where(lane < 4 * capacity, ghost_ids, -1.0)
    ids = jnp.concatenate([patch_ref[...].astype(F32), ghost_ids], axis=1)
    total = jnp.zeros((3 * pert, 2 * LANES), F32)
    for part in range(parts):
        names = (
            lax.broadcasted_iota(jnp.int32, (LANES, 2 * LANES), 0) + part * LANES
        ).astype(F32)
        hot = jnp.where(names == ids, 1.0, 0.0).astype(BF16)
        value = got_ref[part, :pert]
        top = value.astype(BF16)
        rest = value - top.astype(F32)
        mid = rest.astype(BF16)
        last = (rest - mid.astype(F32)).astype(BF16)
        total = total + jnp.dot(
            jnp.concatenate([top, mid, last], axis=0), hot, preferred_element_type=F32
        )
    picked = total[:pert] + total[pert : 2 * pert] + total[2 * pert :]
    local_picked = picked[:, :LANES]
    ghost_picked = picked[:, LANES:]
    full_low = low.astype(jnp.int32)
    column_patches = patches_of_columns(columns_ref, ids)
    patches_ref[...] = column_patches
    sub = lax.broadcasted_iota(jnp.int32, (8, LANES), 0)
    lane8 = lax.broadcasted_iota(jnp.int32, (8, LANES), 1)
    wanted = sub == lane8 % 4

    def listed(blocks_of_lanes):
        taken = jnp.take_along_axis(column_patches, blocks_of_lanes, axis=1)
        return jnp.sum(jnp.where(wanted, taken, 0.0), axis=0, keepdims=True)

    for tile in range(4 * blocks // LANES):
        names_ref[tile : tile + 1, :] = listed(tile * (LANES // 4) + lane8 // 4)
    w_copy.wait()
    w = w_ref[...]
    w_other = swap_halves(w)
    low_w = low_half(w.shape)
    row_ref[pl.ds(0, blocks // 2, stride=2), :] = jnp.where(low_w, w, w_other)
    row_ref[pl.ds(1, blocks // 2, stride=2), :] = jnp.where(low_w, w_other, w)
    for group, source in enumerate(sources):
        start = blocks + group * capacity
        row_ref[start : start + capacity, :] = got_ref[source, pert : pert + capacity, :]

    def seed(pair, _):
        index = 2 * pair + 1 - full_low
        spread = jnp.take_along_axis(local_picked, index, axis=1)
        value = spread * w_ref[pl.ds(pair, 1), :]
        t1_ref[pair] = value
        store_pair(ext_ref, pair, value, low)
        return 0

    lax.fori_loop(0, blocks // 2, seed, 0, unroll=16)
    for group, source in enumerate(sources):
        for slot in range(capacity):
            place = group * capacity + slot
            row = got_ref[source, pert + slot : pert + slot + 1, :]
            spread = jnp.broadcast_to(ghost_picked[:, place : place + 1], (pert, LANES))
            ext_ref[blocks + place] = (spread * row).astype(BF16)

    for chunk, copy in enumerate(copies):
        copy.wait()
        for block in range(chunk * size, (chunk + 1) * size):
            m_ref[block] = jnp.dot(
                diag_ref[block], coupling_ref[block], preferred_element_type=F32
            ).astype(BF16)

    low8 = low_half((8, LANES))
    masks = [(sub % 4 == k) & (low8 if k % 2 == 0 else ~low8) for k in range(4)]
    nothing = jnp.zeros((8, LANES), F32)

    def sweep(quad, _):
        rows = gather_rows(quad, cols_ref, ext_ref, low)
        tiles = ([], [])
        for place in range(QUAD):
            w_rows = [row_ref[pl.ds(cols_ref[k, quad * QUAD + place], 1), :] for k in range(4)]
            for side in range(2):
                tiles[side].append(
                    jnp.where(
                        masks[2 * side],
                        w_rows[2 * side],
                        jnp.where(masks[2 * side + 1], w_rows[2 * side + 1], nothing),
                    )
                )
        extra = jnp.concatenate([jnp.concatenate(side, axis=0) for side in tiles], axis=1)
        out = coupled_rows(quad, rows + [extra.astype(BF16)], m_ref)
        for place, value in enumerate(own_pairs(out, pert, low)):
            pair = 2 * quad + place
            store_pair(t2_ref, pair, t1_ref[pair] - value, low)
        for place, value in enumerate(own_pairs(out[QUAD * pert :], 8, low8)):
            v_ref[2 * quad + place] = value
        return 0

    lax.fori_loop(0, blocks // QUAD, sweep, 0, unroll=32)
    msgs = (o0, o1, o2, o3)
    fill_messages(send_ref, t2_ref, msgs, low)
    half = capacity // 2
    for group, ref in enumerate(msgs):
        places = jnp.zeros((8, LANES), jnp.int32)
        values = []
        for slot in range(capacity):
            block = jnp.maximum(send_ref[0, group, slot], 0)
            value = v_ref[block // 2]
            right = (slot - block) % 2 == 0
            values.append(jnp.where(right, value, swap_halves(value)))
            places = jnp.where(lane8 // 4 == slot, block, places)
        pairs = [
            jnp.where(low8, values[2 * pair], values[2 * pair + 1]) for pair in range(half)
        ]
        for tile in range(half // 2):
            ref[half + tile] = jnp.concatenate(pairs[2 * tile : 2 * tile + 2], axis=0).astype(BF16)
        patch = listed(places).astype(jnp.int32)
        ref[half + half // 2] = jnp.concatenate(
            [
                jnp.broadcast_to(patch // RADIX, (8, LANES)),
                jnp.broadcast_to(patch % RADIX, (8, LANES)),
            ],
            axis=0,
        ).astype(F32).astype(BF16)


def extend(ext_ref, local_ref, ghosts, low):
    blocks = local_ref.shape[0]
    count = (ext_ref.shape[0] - blocks) // 2 // len(ghosts)
    ext_ref[:blocks] = local_ref[...]
    for group, ref in enumerate(ghosts):
        for pair in range(count):
            store_pair(ext_ref, blocks // 2 + group * count + pair, ref[pair], low)


def sweep_kernel(
    cols_ref, send_ref, t1_ref, prev_ref, g0, g1, g2, g3, m_ref,
    next_ref, o0, o1, o2, o3, ext_ref,
):
    low = low_half(prev_ref.shape[1:])
    extend(ext_ref, prev_ref, (g0, g1, g2, g3), low)

    def sweep(quad, _):
        first, second = gather_multiply(quad, cols_ref, ext_ref, m_ref, low)
        store_pair(next_ref, 2 * quad, t1_ref[2 * quad] - first, low)
        store_pair(next_ref, 2 * quad + 1, t1_ref[2 * quad + 1] - second, low)
        return 0

    lax.fori_loop(0, cols_ref.shape[1] // QUAD, sweep, 0, unroll=32)
    fill_messages(send_ref, next_ref, (o0, o1, o2, o3), low)


def clear(acc_refs):
    def one(place, _):
        for ref in acc_refs:
            ref[place] = jnp.zeros(ref.shape[1:], F32)
        return 0

    lax.fori_loop(0, acc_refs[0].shape[0], one, 0, unroll=16)


def multiply_scatter(quad, cols_ref, pairs, m_ref, acc_refs, low):
    zero = jnp.zeros(pairs[0].shape, F32)
    rows = []
    for place in range(QUAD):
        value = pairs[place // 2]
        kept = jnp.where(low, value, zero) if place % 2 == 0 else jnp.where(low, zero, value)
        tiles = [kept, zero] if place < 2 else [zero, kept]
        rows.append(jnp.concatenate(tiles, axis=1))
    lhs = jnp.concatenate(rows, axis=0).astype(BF16)
    rhs = m_ref[pl.ds(quad * QUAD, QUAD)].reshape(QUAD * HALF, 4 * HALF)
    out = jnp.dot(lhs, rhs, preferred_element_type=F32)
    p = pairs[0].shape[0]
    for place in range(QUAD):
        g = quad * QUAD + place
        for k in range(4):
            column = cols_ref[k, g]
            piece = out[place * p : (place + 1) * p, (k // 2) * LANES : (k // 2 + 1) * LANES]
            acc_refs[k][column] = acc_refs[k][column] + piece


def half_sums(acc_refs, place, low):
    return jnp.where(
        low, acc_refs[0][place] + acc_refs[2][place], acc_refs[1][place] + acc_refs[3][place]
    )


def pair_sum(acc_refs, pair, low):
    even = half_sums(acc_refs, 2 * pair, low)
    odd = half_sums(acc_refs, 2 * pair + 1, low)
    return jnp.where(low, even, odd) + swap_halves(jnp.where(low, odd, even))


def turn_kernel(
    cols_ref, t1_ref, prev_ref, g0, g1, g2, g3, m_ref, weight_ref, w_ref,
    tangent_ref, terms_ref, z_ref, y_ref, ext_ref, target_ref, u_ref, *acc_refs,
):
    pert = prev_ref.shape[1]
    low = low_half(prev_ref.shape[1:])
    lane = lax.broadcasted_iota(jnp.int32, (pert, LANES), 1)
    blocks = cols_ref.shape[1]
    extend(ext_ref, prev_ref, (g0, g1, g2, g3), low)

    def sweep(quad, terms):
        coupled = gather_multiply(quad, cols_ref, ext_ref, m_ref, low)
        for place in range(2):
            pair = 2 * quad + place
            value = t1_ref[pair] - coupled[place]
            start = pl.multiple_of(pair * LANES, LANES)
            tangent_ref[:, pl.ds(start, LANES)] = value
            target = value * weight_ref[pl.ds(pair, 1), :]
            target_ref[pair] = target
            product = target * w_ref[pl.ds(pair, 1), :]
            even = jnp.sum(jnp.where(low, product, 0.0), axis=1, keepdims=True)
            odd = jnp.sum(jnp.where(low, 0.0, product), axis=1, keepdims=True)
            terms = jnp.where(
                lane == 2 * pair, even, jnp.where(lane == 2 * pair + 1, odd, terms)
            )
        return terms

    terms_ref[...] = lax.fori_loop(
        0, blocks // QUAD, sweep, jnp.zeros((pert, LANES), F32), unroll=32
    )
    scatter_all(cols_ref, target_ref, m_ref, acc_refs, low)

    def own(pair, _):
        u_ref[pair] = target_ref[pair] - pair_sum(acc_refs, pair, low)
        return 0

    lax.fori_loop(0, blocks // 2, own, 0, unroll=16)
    for pair in range(y_ref.shape[0]):
        y_ref[pair] = (-pair_sum(acc_refs, blocks // 2 + pair, low)).astype(BF16)
    scatter_all(cols_ref, u_ref, m_ref, acc_refs, low)

    def second(pair, _):
        z_ref[pair] = (pair_sum(acc_refs, pair, low) - target_ref[pair]).astype(BF16)
        return 0

    lax.fori_loop(0, blocks // 2, second, 0, unroll=16)
    for pair in range(blocks // 2, z_ref.shape[0]):
        z_ref[pair] = pair_sum(acc_refs, pair, low).astype(BF16)


def scatter_all(cols_ref, u_ref, m_ref, acc_refs, low):
    clear(acc_refs)

    def sweep(quad, _):
        pairs = [u_ref[2 * quad], u_ref[2 * quad + 1]]
        multiply_scatter(quad, cols_ref, pairs, m_ref, acc_refs, low)
        return 0

    lax.fori_loop(0, cols_ref.shape[1] // QUAD, sweep, 0, unroll=32)


def write_hot(hot_ref, rows, part):
    start = pl.multiple_of(part * LANES, LANES)
    names = lax.broadcasted_iota(jnp.int32, (LANES, LANES), 0) + part * LANES
    names = names.astype(F32)
    for tile, row in enumerate(rows):
        hot_ref[pl.ds(start, LANES), tile * LANES : (tile + 1) * LANES] = jnp.where(
            names == row, 1.0, 0.0
        ).astype(BF16)


def window_kernel(
    cols_ref, send_ref, columns_ref, patch_ref, names_ref, patches_ref, g0, g1, g2, g3,
    v_ref, m_ref, hot_ref, o0, o1, o2, o3, vector_ref,
):
    ghosts = (g0, g1, g2, g3)
    capacity = send_ref.shape[2]
    half = capacity // 2
    blocks = cols_ref.shape[1]
    low8 = low_half((8, LANES))
    sub = lax.broadcasted_iota(jnp.int32, (8, LANES), 0)
    lane = lax.broadcasted_iota(jnp.int32, (8, LANES), 1)

    listed = []
    there = jnp.zeros((8, LANES), F32)
    for group, ref in enumerate(ghosts):
        digits = ref[ref.shape[0] - 1].astype(F32)
        listed.append(digits[0:1] * RADIX + digits[8:9])
        taken = jnp.take_along_axis(
            jnp.broadcast_to(listed[-1], (8, LANES)), (lane % capacity) * 4 + sub % 4, axis=1
        )
        there = jnp.where(lane // capacity == group, taken, there)
    here = patches_ref[...]
    rows = [patch_ref[...].astype(F32)] + [names_ref[tile : tile + 1] for tile in range(4)]
    for tile in range(2):
        rows.append(
            jnp.where(low8[:1], listed[2 * tile], swap_halves(listed[2 * tile + 1]))
        )

    def spread(pair, value):
        other = swap_halves(value)
        vector_ref[2 * pair] = jnp.where(low8, value, other)
        vector_ref[2 * pair + 1] = jnp.where(low8, other, value)

    for pair in range(blocks // 2):
        spread(pair, v_ref[pair])
    for group, ref in enumerate(ghosts):
        for tile in range(half // 2):
            both = ref[half + tile].astype(F32)
            for side in range(2):
                pair = blocks // 2 + group * half + 2 * tile + side
                spread(pair, both[8 * side : 8 * side + 8])

    own = (sub < 4) == low8
    nothing = jnp.zeros((8, LANES), F32)
    low = low_half((16, LANES))
    columns = jnp.concatenate([columns_ref[...], columns_ref[...]], axis=0)
    sub16 = lax.broadcasted_iota(jnp.int32, (16, LANES), 0)
    for group, ref in enumerate((o0, o1, o2, o3)):
        slots = [jnp.maximum(send_ref[0, group, slot], 0) for slot in range(capacity)]
        for four in range(capacity // QUAD):
            lhs = []
            rhs = []
            for block in slots[four * QUAD : (four + 1) * QUAD]:
                a0, a1, a2, a3 = (vector_ref[cols_ref[k, block]] for k in range(4))
                left = jnp.where(own, jnp.where(sub < 4, a0, a1), nothing)
                right = jnp.where(own, jnp.where(sub < 4, a2, a3), nothing)
                lhs.append(
                    jnp.concatenate(
                        [
                            jnp.concatenate([left, nothing], axis=0),
                            jnp.concatenate([nothing, right], axis=0),
                        ],
                        axis=1,
                    ).astype(BF16)
                )
                rhs.append(m_ref[block])
            out = lax.dot_general(
                jnp.concatenate(lhs, axis=0),
                jnp.concatenate(rhs, axis=0),
                (((1,), (1,)), ((), ())),
                preferred_element_type=F32,
            )
            for side, value in enumerate(own_pairs(out, 16, low)):
                ref[2 * four + side] = value.astype(BF16)
        digits = jnp.zeros((16, LANES), F32)
        for tile in range(2):
            places = jnp.zeros((8, LANES), jnp.int32)
            for slot in range(half):
                places = jnp.where(lane // 16 == slot, slots[tile * half + slot], places)
            taken = jnp.take_along_axis(columns, places, axis=1).astype(F32)
            mine = jnp.sum(
                jnp.where(sub == (lane % 16) // 4, taken, 0.0), axis=0, keepdims=True
            )
            mine = jnp.broadcast_to(mine, (8, LANES)).astype(jnp.int32)
            taken = jnp.where(
                mine < LANES,
                jnp.take_along_axis(here, jnp.minimum(mine, LANES - 1), axis=1),
                jnp.take_along_axis(there, jnp.maximum(mine - LANES, 0), axis=1),
            )
            patch = jnp.sum(jnp.where(sub == lane % 4, taken, 0.0), axis=0, keepdims=True)
            patch = patch.astype(jnp.int32)
            digits = jnp.where(
                sub16 == 2 * tile,
                (patch // RADIX).astype(F32),
                jnp.where(sub16 == 2 * tile + 1, (patch % RADIX).astype(F32), digits),
            )
        ref[half] = digits.astype(BF16)

    def one(part, _):
        write_hot(hot_ref, rows, part)
        return 0

    lax.fori_loop(0, hot_ref.shape[0] // LANES, one, 0, unroll=2)


def last_kernel(
    z_ref, y_ref, v_ref, v0, v1, v2, v3, x0, x1, x2, x3,
    hot_ref, terms_ref, got_ref, out_ref,
):
    pert = z_ref.shape[1]
    local_pairs = v_ref.shape[0]
    half = (z_ref.shape[0] - local_pairs) // 4
    parts = got_ref.shape[0]
    low8 = low_half((8, LANES))
    low = low_half((16, LANES))
    sub = lax.broadcasted_iota(jnp.int32, (8, LANES), 0)
    own = (sub < 4) == low8
    nothing = jnp.zeros((8, LANES), F32)
    zero = jnp.zeros((16, LANES), F32)

    def wide(left, right):
        return jnp.concatenate([left, right], axis=1)

    def product(lhs, rhs):
        return lax.dot_general(
            lhs, rhs.astype(BF16), (((1,), (1,)), ((), ())), preferred_element_type=F32
        )

    def first_level(first, second):
        return jnp.concatenate(
            [
                wide(jnp.where(own, first, nothing), nothing),
                wide(nothing, jnp.where(own, second, nothing)),
            ],
            axis=0,
        )

    def second_level(first, second):
        return jnp.concatenate(
            [
                wide(jnp.where(low, first, zero), zero),
                wide(jnp.where(low, zero, first), zero),
                wide(zero, jnp.where(low, second, zero)),
                wide(zero, jnp.where(low, zero, second)),
            ],
            axis=0,
        )

    pieces = [terms_ref[...]]
    for pair in range(0, local_pairs, 2):
        lhs = wide(z_ref[pair], z_ref[pair + 1])
        pieces.append(product(lhs, first_level(v_ref[pair], v_ref[pair + 1])))
    for group, ref in enumerate((v0, v1, v2, v3)):
        for tile in range(half // 2):
            both = ref[half + tile].astype(F32)
            pair = local_pairs + group * half + 2 * tile
            lhs = wide(z_ref[pair], z_ref[pair + 1])
            pieces.append(product(lhs, first_level(both[:8], both[8:])))
    rows = []
    for group, ref in enumerate((x0, x1, x2, x3)):
        for tile in range(half // 2):
            pair = group * half + 2 * tile
            lhs = wide(y_ref[pair], y_ref[pair + 1])
            first, second = (ref[2 * tile + side].astype(F32) for side in range(2))
            pieces.append(product(lhs, second_level(first, second)))
        digits = ref[half].astype(F32)
        for tile in range(2):
            rows.append(
                digits[2 * tile : 2 * tile + 1] * RADIX + digits[2 * tile + 1 : 2 * tile + 2]
            )
    terms = jnp.concatenate(pieces, axis=1)
    top = terms.astype(BF16)
    rest = (terms - top.astype(F32)).astype(BF16)
    both = jnp.concatenate([top, rest], axis=0)
    near = hot_ref.shape[1]
    perts = out_ref.shape[0] // parts
    first_names = lax.broadcasted_iota(jnp.int32, (LANES, LANES), 0).astype(F32)
    for part in range(parts):
        hot = jnp.concatenate(
            [hot_ref[part * LANES : (part + 1) * LANES, :]]
            + [
                jnp.where(first_names == row - part * LANES, 1.0, 0.0).astype(BF16)
                for row in rows
            ],
            axis=1,
        )
        out = lax.dot_general(both, hot, (((1,), (1,)), ((), ())), preferred_element_type=F32)
        value = out[:pert] + out[pert:]
        curve = jnp.sum(value * got_ref[part, :pert], axis=0, keepdims=True)
        top = curve.astype(BF16).astype(F32)
        extra = jnp.where(sub == 0, top, jnp.where(sub == 1, curve - top, 0.0))
        for place in range(perts):
            out_ref[part * perts + place, :pert] = value.astype(BF16)
            out_ref[part * perts + place, pert:] = extra.astype(BF16)


def owner_kernel(terms_ref, hessian_ref, curve_ref, *, parts, scale):
    pert = hessian_ref.shape[0]
    perts = terms_ref.shape[0] // parts
    mine = lax.axis_index("pert")
    total = jnp.zeros(hessian_ref.shape, F32)
    for part in range(parts):
        total = total + terms_ref[part * perts + mine, :pert].astype(F32)
    hessian_ref[...] = total
    curve = jnp.zeros((8, LANES), F32)
    for place in range(terms_ref.shape[0]):
        curve = curve + terms_ref[place, pert:].astype(F32)
    curve_ref[...] = (curve[0:1] + curve[1:2]) * scale


def call(body, outs, spaces, scratch=(), name=None, flops=0, moved=1 << 20, limit=12):
    return pl.pallas_call(
        body,
        out_shape=outs,
        in_specs=[{"s": SMEM, "v": VMEM, "h": HBM}[s] for s in spaces],
        out_specs=jax.tree.map(lambda _: VMEM, outs),
        scratch_shapes=list(scratch),
        compiler_params=pltpu.CompilerParams(vmem_limit_bytes=limit * MIB),
        name=name,
        cost_estimate=pl.CostEstimate(flops=flops, transcendentals=0, bytes_accessed=moved),
    )


def shards(
    probes, melt_shape, obs_weight, diag_inverse, coupling, columns, send_list, patch_of_block
):
    pert = probes.shape[0]
    blocks = coupling.shape[0]
    capacity = send_list.shape[2]
    parts = lax.axis_size("dom")
    pairs = blocks // 2
    shape = jax.ShapeDtypeStruct
    msgs = [shape((capacity // 2, pert, LANES), BF16)] * 4
    pair_array = shape((pairs, pert, LANES), F32)
    block_array = shape((blocks, pert, LANES), BF16)
    ext = pltpu.VMEM((blocks + 4 * capacity, pert, LANES), BF16)
    accs = [pltpu.VMEM((blocks + 4 * capacity, pert, LANES), F32)] * 4
    held = pltpu.VMEM((pairs, pert, LANES), F32)
    melt = melt_shape.reshape(pairs, LANES)
    weight = obs_weight.reshape(pairs, LANES)
    patch = patch_of_block.reshape(1, blocks)

    perts = lax.axis_size("pert")
    columns = columns.T
    w, outgoing = call(
        functools.partial(melt_kernel, parts=parts),
        [shape((pairs, LANES), F32), shape((parts, pert + capacity + 8, LANES), F32)],
        "hhhhh",
        [
            pltpu.SMEM(send_list.shape, jnp.int32),
            pltpu.VMEM((pairs, LANES), F32),
            pltpu.VMEM((1, blocks), jnp.int32),
            pltpu.VMEM(probes.shape, F32),
            pltpu.VMEM((HALF, HALF, blocks), BF16),
            pltpu.SemaphoreType.DMA((5,)),
        ],
        name="melt",
        limit=60,
    )(send_list, melt, patch, probes, jnp.transpose(diag_inverse, (1, 2, 0)))
    got = lax.all_to_all(outgoing, "dom", 0, 0, tiled=True)
    wide = [shape((capacity // 2 + capacity // 4 + 1, pert, LANES), BF16)] * 4
    m, v, names, patches, t1, state, *out = call(
        first_kernel,
        [
            shape(coupling.shape, BF16),
            shape((pairs, 8, LANES), F32),
            shape((8, LANES), F32),
            shape((8, LANES), F32),
            pair_array,
            block_array,
        ]
        + wide,
        "ssvvvhvh",
        [
            ext,
            pltpu.VMEM((blocks + 4 * capacity, LANES), F32),
            pltpu.VMEM((pairs, LANES), F32),
            pltpu.VMEM(coupling.shape, BF16),
            pltpu.SemaphoreType.DMA,
            pltpu.SemaphoreType.DMA((8,)),
        ],
        name="first",
        limit=46,
    )(columns, send_list, patch, columns, got, w, diag_inverse, coupling)
    carried = [rotated(x, o) for x, o in zip(out, OFFSET_LIST)]
    state, *out = call(
        sweep_kernel, [block_array] + msgs, "ssvvvvvvv", [ext], name="sweep"
    )(columns, send_list, t1, state, *carried, m)
    ghosts = [rotated(v, o) for v, o in zip(out, OFFSET_LIST)]
    hot, *far = call(
        window_kernel,
        [shape((parts * LANES, 7 * LANES), BF16)]
        + [shape((capacity // 2 + 1, pert, LANES), BF16)] * 4,
        "ss" + "v" * 10,
        [pltpu.VMEM((blocks + 4 * capacity, 8, LANES), F32)],
        name="window",
        moved=4 << 20,
    )(columns, send_list, columns, patch, names, patches, *carried, v, m)
    far = [rotated(x, o) for x, o in zip(far, OFFSET_LIST)]
    tangent, terms, z, y = call(
        turn_kernel,
        [
            shape((pert, blocks * HALF), F32),
            shape((pert, LANES), F32),
            shape((pairs + 2 * capacity, pert, LANES), BF16),
            shape((2 * capacity, pert, LANES), BF16),
        ],
        "s" + "v" * 9,
        [ext, held, held] + accs,
        name="turn",
        moved=16 << 20,
    )(columns, t1, state, *ghosts, m, weight, w)
    terms = call(
        last_kernel, shape((parts * perts, pert + 8, LANES), BF16), "v" * 14, name="last"
    )(z, y, v, *carried, *far, hot, terms, got)
    terms = lax.all_to_all(terms, ("dom", "pert"), 0, 0, tiled=True)
    hessian_probe, curvature = call(
        functools.partial(owner_kernel, parts=parts, scale=1.0 / (pert * perts)),
        [shape(probes.shape, F32), shape((1, LANES), F32)],
        "v",
        name="owner",
    )(terms)
    return tangent, hessian_probe, curvature.reshape(-1)


def solution(mesh):
    in_specs = (
        P("pert", "dom"),
        P("dom"),
        P("dom"),
        P("dom", None, None),
        P("dom", None, None),
        P("dom", None),
        P("dom", None, None),
        P("dom"),
    )
    out_specs = (P("pert", "dom"), P("pert", "dom"), P("dom"))
    return jax.shard_map(shards, mesh=mesh, in_specs=in_specs, out_specs=out_specs, check_vma=False)
```

```python
import functools

import jax
import jax.numpy as jnp
from jax import lax
from jax.experimental import pallas as pl
from jax.experimental.pallas import tpu as pltpu
from jax.sharding import PartitionSpec as P

OFFSET_LIST = (-2, -1, 1, 2)
F32 = jnp.float32
BF16 = jnp.bfloat16
LANES = 128
HALF = 64
QUAD = 4
RADIX = 64

VMEM = pl.BlockSpec(memory_space=pltpu.VMEM)
SMEM = pl.BlockSpec(memory_space=pltpu.SMEM)
HBM = pl.BlockSpec(memory_space=pltpu.HBM)
MIB = 1024 * 1024


def low_half(shape):
    return lax.broadcasted_iota(jnp.int32, shape, len(shape) - 1) < HALF


def swap_halves(value):
    return pltpu.roll(value, HALF, 1)


def rotated(value, by):
    peers = lax.axis_size("dom")
    return lax.ppermute(value, "dom", [(i, (i + by) % peers) for i in range(peers)])


def neighbours(parts):
    me = lax.axis_index("dom")
    return [lax.rem(me - offset + parts, parts) for offset in OFFSET_LIST]


def melt_kernel(
    send_hbm, melt_hbm, patch_hbm, probe_hbm, diag_hbm, w_ref, out_ref,
    send_ref, melt_ref, patch_ref, probe_ref, diag_ref, sems, *, parts,
):
    copies = [
        pltpu.make_async_copy(source, target, sems.at[number])
        for number, (source, target) in enumerate(
            (
                (diag_hbm, diag_ref),
                (melt_hbm, melt_ref),
                (patch_hbm, patch_ref),
                (probe_hbm, probe_ref),
                (send_hbm, send_ref),
            )
        )
    ]
    for copy in copies:
        copy.start()
    for copy in copies:
        copy.wait()
    pairs = melt_ref.shape[0]
    pert = probe_ref.shape[0]
    capacity = send_ref.shape[2]
    low = low_half((1, LANES))
    lane = lax.broadcasted_iota(jnp.int32, (HALF, LANES), 1)
    turned = jnp.transpose(jnp.concatenate([melt_ref[...], jnp.zeros((LANES - pairs, LANES), F32)], axis=0))
    even = jnp.take_along_axis(turned[:HALF], lane // 2, axis=1)
    odd = jnp.take_along_axis(turned[HALF:], lane // 2, axis=1)
    melt = jnp.where(lane % 2 == 0, even, odd)
    sums = [
        jnp.sum(diag_ref[i].astype(F32) * melt, axis=0, keepdims=True)
        for i in range(diag_ref.shape[0])
    ]
    sums = jnp.concatenate(sums, axis=0)
    source = 2 * (lane % HALF)
    both = jnp.concatenate(
        [
            jnp.take_along_axis(sums, source, axis=1),
            jnp.take_along_axis(sums, source + 1, axis=1),
        ],
        axis=0,
    )
    w_ref[...] = jnp.transpose(both)[:pairs]
    patch_row = jnp.broadcast_to(patch_ref[...].astype(F32), (8, LANES))
    lane = lax.broadcasted_iota(jnp.int32, (8, LANES), 1)
    for part in range(parts):
        out_ref[part, :pert] = probe_ref[...]
    me = lax.axis_index("dom")
    for group, offset in enumerate(OFFSET_LIST):
        to = lax.rem(me + offset + parts, parts)
        ids = jnp.zeros((8, LANES), jnp.int32)
        for slot in range(capacity):
            block = jnp.maximum(send_ref[0, group, slot], 0)
            row = w_ref[pl.ds(block // 2, 1), :]
            out_ref[to, pert + slot : pert + slot + 1, :] = jnp.where(
                low == (block % 2 == 0), row, swap_halves(row)
            )
            ids = jnp.where(lane == group * capacity + slot, block, ids)
        mine = (lane >= group * capacity) & (lane < (group + 1) * capacity)
        out_ref[to, pert + capacity :, :] = jnp.where(
            mine, jnp.take_along_axis(patch_row, ids, axis=1), 0.0
        )


def gather_rows(quad, cols_ref, ext_ref, low):
    rows = []
    for place in range(QUAD):
        g = quad * QUAD + place
        tiles = [ext_ref[cols_ref[k, g]] for k in range(4)]
        rows.append(
            jnp.concatenate(
                [jnp.where(low, tiles[0], tiles[1]), jnp.where(low, tiles[2], tiles[3])], axis=1
            )
        )
    return rows


def coupled_rows(quad, rows, m_ref):
    rhs = m_ref[pl.ds(quad * QUAD, QUAD)].reshape(QUAD * HALF, 4 * HALF)
    return lax.dot_general(
        jnp.concatenate(rows, axis=0), rhs, (((1,), (1,)), ((), ())), preferred_element_type=F32
    )


def own_pairs(out, size, low):
    first = jnp.where(low, out[:size, :LANES], out[size : 2 * size, :LANES])
    second = jnp.where(low, out[2 * size : 3 * size, LANES:], out[3 * size : 4 * size, LANES:])
    return first, second


def gather_multiply(quad, cols_ref, ext_ref, m_ref, low):
    out = coupled_rows(quad, gather_rows(quad, cols_ref, ext_ref, low), m_ref)
    return own_pairs(out, out.shape[0] // QUAD, low)


def store_pair(ref, pair, value, low):
    value = value.astype(BF16)
    other = swap_halves(value.astype(F32)).astype(BF16)
    ref[2 * pair] = jnp.where(low, value, other)
    ref[2 * pair + 1] = jnp.where(low, other, value)


def fill_messages(send_ref, ref, msg_refs, low):
    for group, msg_ref in enumerate(msg_refs):
        for pair in range(send_ref.shape[2] // 2):
            even, odd = (
                ref[jnp.maximum(send_ref[0, group, 2 * pair + half], 0)] for half in range(2)
            )
            msg_ref[pair] = jnp.where(low, even, odd)


def patches_of_columns(columns_ref, ids):
    columns = jnp.concatenate([columns_ref[...], columns_ref[...]], axis=0)
    here = jnp.broadcast_to(ids[:, :LANES], columns.shape)
    there = jnp.broadcast_to(ids[:, LANES:], columns.shape)
    return jnp.where(
        columns < LANES,
        jnp.take_along_axis(here, jnp.minimum(columns, LANES - 1), axis=1),
        jnp.take_along_axis(there, jnp.maximum(columns - LANES, 0), axis=1),
    )


def first_kernel(
    cols_ref, send_ref, patch_ref, columns_ref, got_ref, w_hbm, diag_ref, coupling_hbm,
    m_ref, v_ref, names_ref, patches_ref, t1_ref, t2_ref, o0, o1, o2, o3,
    ext_ref, row_ref, w_ref, coupling_ref, w_sem, sems,
):
    w_copy = pltpu.make_async_copy(w_hbm, w_ref, w_sem)
    w_copy.start()
    chunks = sems.shape[0]
    size = diag_ref.shape[0] // chunks
    copies = [
        pltpu.make_async_copy(
            coupling_hbm.at[chunk * size : (chunk + 1) * size],
            coupling_ref.at[chunk * size : (chunk + 1) * size],
            sems.at[chunk],
        )
        for chunk in range(chunks)
    ]
    for copy in copies:
        copy.start()
    pert = t1_ref.shape[1]
    capacity = send_ref.shape[2]
    blocks = cols_ref.shape[1]
    parts = got_ref.shape[0]
    sources = neighbours(parts)
    low = low_half((pert, LANES))
    lane = lax.broadcasted_iota(jnp.int32, (1, LANES), 1)
    ghost_ids = sum(got_ref[source, pert + capacity : pert + capacity + 1, :] for source in sources)
    ghost_ids = jnp.where(lane < 4 * capacity, ghost_ids, -1.0)
    ids = jnp.concatenate([patch_ref[...].astype(F32), ghost_ids], axis=1)
    total = jnp.zeros((3 * pert, 2 * LANES), F32)
    for part in range(parts):
        names = (
            lax.broadcasted_iota(jnp.int32, (LANES, 2 * LANES), 0) + part * LANES
        ).astype(F32)
        hot = jnp.where(names == ids, 1.0, 0.0).astype(BF16)
        value = got_ref[part, :pert]
        top = value.astype(BF16)
        rest = value - top.astype(F32)
        mid = rest.astype(BF16)
        last = (rest - mid.astype(F32)).astype(BF16)
        total = total + jnp.dot(
            jnp.concatenate([top, mid, last], axis=0), hot, preferred_element_type=F32
        )
    picked = total[:pert] + total[pert : 2 * pert] + total[2 * pert :]
    local_picked = picked[:, :LANES]
    ghost_picked = picked[:, LANES:]
    full_low = low.astype(jnp.int32)
    column_patches = patches_of_columns(columns_ref, ids)
    patches_ref[...] = column_patches
    sub = lax.broadcasted_iota(jnp.int32, (8, LANES), 0)
    lane8 = lax.broadcasted_iota(jnp.int32, (8, LANES), 1)
    wanted = sub == lane8 % 4

    def listed(blocks_of_lanes):
        taken = jnp.take_along_axis(column_patches, blocks_of_lanes, axis=1)
        return jnp.sum(jnp.where(wanted, taken, 0.0), axis=0, keepdims=True)

    for tile in range(4 * blocks // LANES):
        names_ref[tile : tile + 1, :] = listed(tile * (LANES // 4) + lane8 // 4)
    w_copy.wait()
    w = w_ref[...]
    w_other = swap_halves(w)
    low_w = low_half(w.shape)
    row_ref[pl.ds(0, blocks // 2, stride=2), :] = jnp.where(low_w, w, w_other)
    row_ref[pl.ds(1, blocks // 2, stride=2), :] = jnp.where(low_w, w_other, w)
    for group, source in enumerate(sources):
        start = blocks + group * capacity
        row_ref[start : start + capacity, :] = got_ref[source, pert : pert + capacity, :]

    def seed(pair, _):
        index = 2 * pair + 1 - full_low
        spread = jnp.take_along_axis(local_picked, index, axis=1)
        value = spread * w_ref[pl.ds(pair, 1), :]
        t1_ref[pair] = value
        store_pair(ext_ref, pair, value, low)
        return 0

    lax.fori_loop(0, blocks // 2, seed, 0, unroll=16)
    for group, source in enumerate(sources):
        for slot in range(capacity):
            place = group * capacity + slot
            row = got_ref[source, pert + slot : pert + slot + 1, :]
            spread = jnp.broadcast_to(ghost_picked[:, place : place + 1], (pert, LANES))
            ext_ref[blocks + place] = (spread * row).astype(BF16)

    for chunk, copy in enumerate(copies):
        copy.wait()
        for block in range(chunk * size, (chunk + 1) * size):
            m_ref[block] = jnp.dot(
                diag_ref[block], coupling_ref[block], preferred_element_type=F32
            ).astype(BF16)

    low8 = low_half((8, LANES))
    masks = [(sub % 4 == k) & (low8 if k % 2 == 0 else ~low8) for k in range(4)]
    nothing = jnp.zeros((8, LANES), F32)

    def sweep(quad, _):
        rows = gather_rows(quad, cols_ref, ext_ref, low)
        tiles = ([], [])
        for place in range(QUAD):
            w_rows = [row_ref[pl.ds(cols_ref[k, quad * QUAD + place], 1), :] for k in range(4)]
            for side in range(2):
                tiles[side].append(
                    jnp.where(
                        masks[2 * side],
                        w_rows[2 * side],
                        jnp.where(masks[2 * side + 1], w_rows[2 * side + 1], nothing),
                    )
                )
        extra = jnp.concatenate([jnp.concatenate(side, axis=0) for side in tiles], axis=1)
        out = coupled_rows(quad, rows + [extra.astype(BF16)], m_ref)
        for place, value in enumerate(own_pairs(out, pert, low)):
            pair = 2 * quad + place
            store_pair(t2_ref, pair, t1_ref[pair] - value, low)
        for place, value in enumerate(own_pairs(out[QUAD * pert :], 8, low8)):
            v_ref[2 * quad + place] = value
        return 0

    lax.fori_loop(0, blocks // QUAD, sweep, 0, unroll=32)
    msgs = (o0, o1, o2, o3)
    fill_messages(send_ref, t2_ref, msgs, low)
    half = capacity // 2
    for group, ref in enumerate(msgs):
        places = jnp.zeros((8, LANES), jnp.int32)
        values = []
        for slot in range(capacity):
            block = jnp.maximum(send_ref[0, group, slot], 0)
            value = v_ref[block // 2]
            right = (slot - block) % 2 == 0
            values.append(jnp.where(right, value, swap_halves(value)))
            places = jnp.where(lane8 // 4 == slot, block, places)
        pairs = [
            jnp.where(low8, values[2 * pair], values[2 * pair + 1]) for pair in range(half)
        ]
        for tile in range(half // 2):
            ref[half + tile] = jnp.concatenate(pairs[2 * tile : 2 * tile + 2], axis=0).astype(BF16)
        patch = listed(places).astype(jnp.int32)
        ref[half + half // 2] = jnp.concatenate(
            [
                jnp.broadcast_to(patch // RADIX, (8, LANES)),
                jnp.broadcast_to(patch % RADIX, (8, LANES)),
            ],
            axis=0,
        ).astype(F32).astype(BF16)


def extend(ext_ref, local_ref, ghosts, low):
    blocks = local_ref.shape[0]
    count = (ext_ref.shape[0] - blocks) // 2 // len(ghosts)
    ext_ref[:blocks] = local_ref[...]
    for group, ref in enumerate(ghosts):
        for pair in range(count):
            store_pair(ext_ref, blocks // 2 + group * count + pair, ref[pair], low)


def sweep_kernel(
    cols_ref, send_ref, t1_ref, prev_ref, g0, g1, g2, g3, m_ref,
    next_ref, o0, o1, o2, o3, ext_ref,
):
    low = low_half(prev_ref.shape[1:])
    extend(ext_ref, prev_ref, (g0, g1, g2, g3), low)

    def sweep(quad, _):
        first, second = gather_multiply(quad, cols_ref, ext_ref, m_ref, low)
        store_pair(next_ref, 2 * quad, t1_ref[2 * quad] - first, low)
        store_pair(next_ref, 2 * quad + 1, t1_ref[2 * quad + 1] - second, low)
        return 0

    lax.fori_loop(0, cols_ref.shape[1] // QUAD, sweep, 0, unroll=32)
    fill_messages(send_ref, next_ref, (o0, o1, o2, o3), low)


def clear(acc_refs):
    def one(place, _):
        for ref in acc_refs:
            ref[place] = jnp.zeros(ref.shape[1:], F32)
        return 0

    lax.fori_loop(0, acc_refs[0].shape[0], one, 0, unroll=16)


def multiply_scatter(quad, cols_ref, pairs, m_ref, acc_refs, low):
    zero = jnp.zeros(pairs[0].shape, F32)
    rows = []
    for place in range(QUAD):
        value = pairs[place // 2]
        kept = jnp.where(low, value, zero) if place % 2 == 0 else jnp.where(low, zero, value)
        tiles = [kept, zero] if place < 2 else [zero, kept]
        rows.append(jnp.concatenate(tiles, axis=1))
    lhs = jnp.concatenate(rows, axis=0).astype(BF16)
    rhs = m_ref[pl.ds(quad * QUAD, QUAD)].reshape(QUAD * HALF, 4 * HALF)
    out = jnp.dot(lhs, rhs, preferred_element_type=F32)
    p = pairs[0].shape[0]
    for place in range(QUAD):
        g = quad * QUAD + place
        for k in range(4):
            column = cols_ref[k, g]
            piece = out[place * p : (place + 1) * p, (k // 2) * LANES : (k // 2 + 1) * LANES]
            acc_refs[k][column] = acc_refs[k][column] + piece


def half_sums(acc_refs, place, low):
    return jnp.where(
        low, acc_refs[0][place] + acc_refs[2][place], acc_refs[1][place] + acc_refs[3][place]
    )


def pair_sum(acc_refs, pair, low):
    even = half_sums(acc_refs, 2 * pair, low)
    odd = half_sums(acc_refs, 2 * pair + 1, low)
    return jnp.where(low, even, odd) + swap_halves(jnp.where(low, odd, even))


def turn_kernel(
    cols_ref, t1_ref, prev_ref, g0, g1, g2, g3, m_ref, weight_ref, w_ref,
    tangent_ref, terms_ref, z_ref, y_ref, ext_ref, target_ref, u_ref, *acc_refs,
):
    pert = prev_ref.shape[1]
    low = low_half(prev_ref.shape[1:])
    lane = lax.broadcasted_iota(jnp.int32, (pert, LANES), 1)
    blocks = cols_ref.shape[1]
    extend(ext_ref, prev_ref, (g0, g1, g2, g3), low)

    def sweep(quad, terms):
        coupled = gather_multiply(quad, cols_ref, ext_ref, m_ref, low)
        for place in range(2):
            pair = 2 * quad + place
            value = t1_ref[pair] - coupled[place]
            start = pl.multiple_of(pair * LANES, LANES)
            tangent_ref[:, pl.ds(start, LANES)] = value
            target = value * weight_ref[pl.ds(pair, 1), :]
            target_ref[pair] = target
            product = target * w_ref[pl.ds(pair, 1), :]
            even = jnp.sum(jnp.where(low, product, 0.0), axis=1, keepdims=True)
            odd = jnp.sum(jnp.where(low, 0.0, product), axis=1, keepdims=True)
            terms = jnp.where(
                lane == 2 * pair, even, jnp.where(lane == 2 * pair + 1, odd, terms)
            )
        return terms

    terms_ref[...] = lax.fori_loop(
        0, blocks // QUAD, sweep, jnp.zeros((pert, LANES), F32), unroll=32
    )
    scatter_all(cols_ref, target_ref, m_ref, acc_refs, low)

    def own(pair, _):
        u_ref[pair] = target_ref[pair] - pair_sum(acc_refs, pair, low)
        return 0

    lax.fori_loop(0, blocks // 2, own, 0, unroll=16)
    for pair in range(y_ref.shape[0]):
        y_ref[pair] = (-pair_sum(acc_refs, blocks // 2 + pair, low)).astype(BF16)
    scatter_all(cols_ref, u_ref, m_ref, acc_refs, low)

    def second(pair, _):
        z_ref[pair] = (pair_sum(acc_refs, pair, low) - target_ref[pair]).astype(BF16)
        return 0

    lax.fori_loop(0, blocks // 2, second, 0, unroll=16)
    for pair in range(blocks // 2, z_ref.shape[0]):
        z_ref[pair] = pair_sum(acc_refs, pair, low).astype(BF16)


def scatter_all(cols_ref, u_ref, m_ref, acc_refs, low):
    clear(acc_refs)

    def sweep(quad, _):
        pairs = [u_ref[2 * quad], u_ref[2 * quad + 1]]
        multiply_scatter(quad, cols_ref, pairs, m_ref, acc_refs, low)
        return 0

    lax.fori_loop(0, cols_ref.shape[1] // QUAD, sweep, 0, unroll=32)


def write_hot(hot_ref, rows, part):
    start = pl.multiple_of(part * LANES, LANES)
    names = lax.broadcasted_iota(jnp.int32, (LANES, LANES), 0) + part * LANES
    names = names.astype(F32)
    for tile, row in enumerate(rows):
        hot_ref[pl.ds(start, LANES), tile * LANES : (tile + 1) * LANES] = jnp.where(
            names == row, 1.0, 0.0
        ).astype(BF16)


def window_kernel(
    cols_ref, send_ref, columns_ref, patch_ref, names_ref, patches_ref, g0, g1, g2, g3,
    v_ref, m_ref, hot_ref, o0, o1, o2, o3, vector_ref,
):
    ghosts = (g0, g1, g2, g3)
    capacity = send_ref.shape[2]
    half = capacity // 2
    blocks = cols_ref.shape[1]
    low8 = low_half((8, LANES))
    sub = lax.broadcasted_iota(jnp.int32, (8, LANES), 0)
    lane = lax.broadcasted_iota(jnp.int32, (8, LANES), 1)

    listed = []
    there = jnp.zeros((8, LANES), F32)
    for group, ref in enumerate(ghosts):
        digits = ref[ref.shape[0] - 1].astype(F32)
        listed.append(digits[0:1] * RADIX + digits[8:9])
        taken = jnp.take_along_axis(
            jnp.broadcast_to(listed[-1], (8, LANES)), (lane % capacity) * 4 + sub % 4, axis=1
        )
        there = jnp.where(lane // capacity == group, taken, there)
    here = patches_ref[...]
    rows = [patch_ref[...].astype(F32)] + [names_ref[tile : tile + 1] for tile in range(4)]
    for tile in range(2):
        rows.append(
            jnp.where(low8[:1], listed[2 * tile], swap_halves(listed[2 * tile + 1]))
        )

    def spread(pair, value):
        other = swap_halves(value)
        vector_ref[2 * pair] = jnp.where(low8, value, other)
        vector_ref[2 * pair + 1] = jnp.where(low8, other, value)

    for pair in range(blocks // 2):
        spread(pair, v_ref[pair])
    for group, ref in enumerate(ghosts):
        for tile in range(half // 2):
            both = ref[half + tile].astype(F32)
            for side in range(2):
                pair = blocks // 2 + group * half + 2 * tile + side
                spread(pair, both[8 * side : 8 * side + 8])

    own = (sub < 4) == low8
    nothing = jnp.zeros((8, LANES), F32)
    low = low_half((16, LANES))
    columns = jnp.concatenate([columns_ref[...], columns_ref[...]], axis=0)
    sub16 = lax.broadcasted_iota(jnp.int32, (16, LANES), 0)
    for group, ref in enumerate((o0, o1, o2, o3)):
        slots = [jnp.maximum(send_ref[0, group, slot], 0) for slot in range(capacity)]
        for four in range(capacity // QUAD):
            lhs = []
            rhs = []
            for block in slots[four * QUAD : (four + 1) * QUAD]:
                a0, a1, a2, a3 = (vector_ref[cols_ref[k, block]] for k in range(4))
                left = jnp.where(own, jnp.where(sub < 4, a0, a1), nothing)
                right = jnp.where(own, jnp.where(sub < 4, a2, a3), nothing)
                lhs.append(
                    jnp.concatenate(
                        [
                            jnp.concatenate([left, nothing], axis=0),
                            jnp.concatenate([nothing, right], axis=0),
                        ],
                        axis=1,
                    ).astype(BF16)
                )
                rhs.append(m_ref[block])
            out = lax.dot_general(
                jnp.concatenate(lhs, axis=0),
                jnp.concatenate(rhs, axis=0),
                (((1,), (1,)), ((), ())),
                preferred_element_type=F32,
            )
            for side, value in enumerate(own_pairs(out, 16, low)):
                ref[2 * four + side] = value.astype(BF16)
        digits = jnp.zeros((16, LANES), F32)
        for tile in range(2):
            places = jnp.zeros((8, LANES), jnp.int32)
            for slot in range(half):
                places = jnp.where(lane // 16 == slot, slots[tile * half + slot], places)
            taken = jnp.take_along_axis(columns, places, axis=1).astype(F32)
            mine = jnp.sum(
                jnp.where(sub == (lane % 16) // 4, taken, 0.0), axis=0, keepdims=True
            )
            mine = jnp.broadcast_to(mine, (8, LANES)).astype(jnp.int32)
            taken = jnp.where(
                mine < LANES,
                jnp.take_along_axis(here, jnp.minimum(mine, LANES - 1), axis=1),
                jnp.take_along_axis(there, jnp.maximum(mine - LANES, 0), axis=1),
            )
            patch = jnp.sum(jnp.where(sub == lane % 4, taken, 0.0), axis=0, keepdims=True)
            patch = patch.astype(jnp.int32)
            digits = jnp.where(
                sub16 == 2 * tile,
                (patch // RADIX).astype(F32),
                jnp.where(sub16 == 2 * tile + 1, (patch % RADIX).astype(F32), digits),
            )
        ref[half] = digits.astype(BF16)

    def one(part, _):
        write_hot(hot_ref, rows, part)
        return 0

    lax.fori_loop(0, hot_ref.shape[0] // LANES, one, 0, unroll=2)


def last_kernel(
    z_ref, y_ref, v_ref, v0, v1, v2, v3, x0, x1, x2, x3,
    hot_ref, terms_ref, got_ref, out_ref,
):
    pert = z_ref.shape[1]
    local_pairs = v_ref.shape[0]
    half = (z_ref.shape[0] - local_pairs) // 4
    parts = got_ref.shape[0]
    low8 = low_half((8, LANES))
    low = low_half((16, LANES))
    sub = lax.broadcasted_iota(jnp.int32, (8, LANES), 0)
    own = (sub < 4) == low8
    nothing = jnp.zeros((8, LANES), F32)
    zero = jnp.zeros((16, LANES), F32)

    def wide(left, right):
        return jnp.concatenate([left, right], axis=1)

    def product(lhs, rhs):
        return lax.dot_general(
            lhs, rhs.astype(BF16), (((1,), (1,)), ((), ())), preferred_element_type=F32
        )

    def first_level(first, second):
        return jnp.concatenate(
            [
                wide(jnp.where(own, first, nothing), nothing),
                wide(nothing, jnp.where(own, second, nothing)),
            ],
            axis=0,
        )

    def second_level(first, second):
        return jnp.concatenate(
            [
                wide(jnp.where(low, first, zero), zero),
                wide(jnp.where(low, zero, first), zero),
                wide(zero, jnp.where(low, second, zero)),
                wide(zero, jnp.where(low, zero, second)),
            ],
            axis=0,
        )

    pieces = [terms_ref[...]]
    for pair in range(0, local_pairs, 2):
        lhs = wide(z_ref[pair], z_ref[pair + 1])
        pieces.append(product(lhs, first_level(v_ref[pair], v_ref[pair + 1])))
    for group, ref in enumerate((v0, v1, v2, v3)):
        for tile in range(half // 2):
            both = ref[half + tile].astype(F32)
            pair = local_pairs + group * half + 2 * tile
            lhs = wide(z_ref[pair], z_ref[pair + 1])
            pieces.append(product(lhs, first_level(both[:8], both[8:])))
    rows = []
    for group, ref in enumerate((x0, x1, x2, x3)):
        for tile in range(half // 2):
            pair = group * half + 2 * tile
            lhs = wide(y_ref[pair], y_ref[pair + 1])
            first, second = (ref[2 * tile + side].astype(F32) for side in range(2))
            pieces.append(product(lhs, second_level(first, second)))
        digits = ref[half].astype(F32)
        for tile in range(2):
            rows.append(
                digits[2 * tile : 2 * tile + 1] * RADIX + digits[2 * tile + 1 : 2 * tile + 2]
            )
    terms = jnp.concatenate(pieces, axis=1)
    top = terms.astype(BF16)
    rest = (terms - top.astype(F32)).astype(BF16)
    both = jnp.concatenate([top, rest], axis=0)
    near = hot_ref.shape[1]
    perts = out_ref.shape[0] // parts
    first_names = lax.broadcasted_iota(jnp.int32, (LANES, LANES), 0).astype(F32)
    for part in range(parts):
        hot = jnp.concatenate(
            [hot_ref[part * LANES : (part + 1) * LANES, :]]
            + [
                jnp.where(first_names == row - part * LANES, 1.0, 0.0).astype(BF16)
                for row in rows
            ],
            axis=1,
        )
        out = lax.dot_general(both, hot, (((1,), (1,)), ((), ())), preferred_element_type=F32)
        value = out[:pert] + out[pert:]
        curve = jnp.sum(value * got_ref[part, :pert], axis=0, keepdims=True)
        top = curve.astype(BF16).astype(F32)
        extra = jnp.where(sub == 0, top, jnp.where(sub == 1, curve - top, 0.0))
        for place in range(perts):
            out_ref[part * perts + place, :pert] = value.astype(BF16)
            out_ref[part * perts + place, pert:] = extra.astype(BF16)


def owner_kernel(terms_ref, hessian_ref, curve_ref, *, parts, scale):
    pert = hessian_ref.shape[0]
    perts = terms_ref.shape[0] // parts
    mine = lax.axis_index("pert")
    total = jnp.zeros(hessian_ref.shape, F32)
    for part in range(parts):
        total = total + terms_ref[part * perts + mine, :pert].astype(F32)
    hessian_ref[...] = total
    curve = jnp.zeros((8, LANES), F32)
    for place in range(terms_ref.shape[0]):
        curve = curve + terms_ref[place, pert:].astype(F32)
    curve_ref[...] = (curve[0:1] + curve[1:2]) * scale


def call(body, outs, spaces, scratch=(), name=None, flops=0, moved=1 << 20, limit=12):
    return pl.pallas_call(
        body,
        out_shape=outs,
        in_specs=[{"s": SMEM, "v": VMEM, "h": HBM}[s] for s in spaces],
        out_specs=jax.tree.map(lambda _: VMEM, outs),
        scratch_shapes=list(scratch),
        compiler_params=pltpu.CompilerParams(vmem_limit_bytes=limit * MIB),
        name=name,
        cost_estimate=pl.CostEstimate(flops=flops, transcendentals=0, bytes_accessed=moved),
    )


def shards(
    probes, melt_shape, obs_weight, diag_inverse, coupling, columns, send_list, patch_of_block
):
    pert = probes.shape[0]
    blocks = coupling.shape[0]
    capacity = send_list.shape[2]
    parts = lax.axis_size("dom")
    pairs = blocks // 2
    shape = jax.ShapeDtypeStruct
    msgs = [shape((capacity // 2, pert, LANES), BF16)] * 4
    pair_array = shape((pairs, pert, LANES), F32)
    block_array = shape((blocks, pert, LANES), BF16)
    ext = pltpu.VMEM((blocks + 4 * capacity, pert, LANES), BF16)
    accs = [pltpu.VMEM((blocks + 4 * capacity, pert, LANES), F32)] * 4
    held = pltpu.VMEM((pairs, pert, LANES), F32)
    melt = melt_shape.reshape(pairs, LANES)
    weight = obs_weight.reshape(pairs, LANES)
    patch = patch_of_block.reshape(1, blocks)

    perts = lax.axis_size("pert")
    columns = columns.T
    w, outgoing = call(
        functools.partial(melt_kernel, parts=parts),
        [shape((pairs, LANES), F32), shape((parts, pert + capacity + 8, LANES), F32)],
        "hhhhh",
        [
            pltpu.SMEM(send_list.shape, jnp.int32),
            pltpu.VMEM((pairs, LANES), F32),
            pltpu.VMEM((1, blocks), jnp.int32),
            pltpu.VMEM(probes.shape, F32),
            pltpu.VMEM((HALF, HALF, blocks), BF16),
            pltpu.SemaphoreType.DMA((5,)),
        ],
        name="melt",
        limit=60,
    )(send_list, melt, patch, probes, jnp.transpose(diag_inverse, (1, 2, 0)))
    got = lax.all_to_all(outgoing, "dom", 0, 0, tiled=True)
    wide = [shape((capacity // 2 + capacity // 4 + 1, pert, LANES), BF16)] * 4
    m, v, names, patches, t1, state, *out = call(
        first_kernel,
        [
            shape(coupling.shape, BF16),
            shape((pairs, 8, LANES), F32),
            shape((8, LANES), F32),
            shape((8, LANES), F32),
            pair_array,
            block_array,
        ]
        + wide,
        "ssvvvhvh",
        [
            ext,
            pltpu.VMEM((blocks + 4 * capacity, LANES), F32),
            pltpu.VMEM((pairs, LANES), F32),
            pltpu.VMEM(coupling.shape, BF16),
            pltpu.SemaphoreType.DMA,
            pltpu.SemaphoreType.DMA((8,)),
        ],
        name="first",
        limit=46,
    )(columns, send_list, patch, columns, got, w, diag_inverse, coupling)
    carried = [rotated(x, o) for x, o in zip(out, OFFSET_LIST)]
    state, *out = call(
        sweep_kernel, [block_array] + msgs, "ssvvvvvvv", [ext], name="sweep"
    )(columns, send_list, t1, state, *carried, m)
    ghosts = [rotated(v, o) for v, o in zip(out, OFFSET_LIST)]
    hot, *far = call(
        window_kernel,
        [shape((parts * LANES, 7 * LANES), BF16)]
        + [shape((capacity // 2 + 1, pert, LANES), BF16)] * 4,
        "ss" + "v" * 10,
        [pltpu.VMEM((blocks + 4 * capacity, 8, LANES), F32)],
        name="window",
        moved=4 << 20,
    )(columns, send_list, columns, patch, names, patches, *carried, v, m)
    far, ghosts = lax.optimization_barrier((far, ghosts))
    far = [rotated(x, o) for x, o in zip(far, OFFSET_LIST)]
    tangent, terms, z, y = call(
        turn_kernel,
        [
            shape((pert, blocks * HALF), F32),
            shape((pert, LANES), F32),
            shape((pairs + 2 * capacity, pert, LANES), BF16),
            shape((2 * capacity, pert, LANES), BF16),
        ],
        "s" + "v" * 9,
        [ext, held, held] + accs,
        name="turn",
        moved=16 << 20,
    )(columns, t1, state, *ghosts, m, weight, w)
    terms = call(
        last_kernel, shape((parts * perts, pert + 8, LANES), BF16), "v" * 14, name="last"
    )(z, y, v, *carried, *far, hot, terms, got)
    terms = lax.all_to_all(terms, ("dom", "pert"), 0, 0, tiled=True)
    hessian_probe, curvature = call(
        functools.partial(owner_kernel, parts=parts, scale=1.0 / (pert * perts)),
        [shape(probes.shape, F32), shape((1, LANES), F32)],
        "v",
        name="owner",
    )(terms)
    return tangent, hessian_probe, curvature.reshape(-1)


def solution(mesh):
    in_specs = (
        P("pert", "dom"),
        P("dom"),
        P("dom"),
        P("dom", None, None),
        P("dom", None, None),
        P("dom", None),
        P("dom", None, None),
        P("dom"),
    )
    out_specs = (P("pert", "dom"), P("pert", "dom"), P("dom"))
    return jax.shard_map(shards, mesh=mesh, in_specs=in_specs, out_specs=out_specs, check_vma=False)
```

```python
import functools

import jax
import jax.numpy as jnp
from jax import lax
from jax.experimental import pallas as pl
from jax.experimental.pallas import tpu as pltpu
from jax.sharding import PartitionSpec as P

OFFSET_LIST = (-2, -1, 1, 2)
F32 = jnp.float32
BF16 = jnp.bfloat16
LANES = 128
HALF = 64
QUAD = 4
RADIX = 64

VMEM = pl.BlockSpec(memory_space=pltpu.VMEM)
SMEM = pl.BlockSpec(memory_space=pltpu.SMEM)
HBM = pl.BlockSpec(memory_space=pltpu.HBM)
MIB = 1024 * 1024


def low_half(shape):
    return lax.broadcasted_iota(jnp.int32, shape, len(shape) - 1) < HALF


def swap_halves(value):
    return pltpu.roll(value, HALF, 1)


def rotated(value, by):
    peers = lax.axis_size("dom")
    return lax.ppermute(value, "dom", [(i, (i + by) % peers) for i in range(peers)])


def neighbours(parts):
    me = lax.axis_index("dom")
    return [lax.rem(me - offset + parts, parts) for offset in OFFSET_LIST]


def melt_kernel(
    send_hbm, melt_hbm, patch_hbm, probe_hbm, diag_hbm, w_ref, out_ref,
    send_ref, melt_ref, patch_ref, probe_ref, diag_ref, sems, *, parts,
):
    copies = [
        pltpu.make_async_copy(source, target, sems.at[number])
        for number, (source, target) in enumerate(
            (
                (diag_hbm, diag_ref),
                (melt_hbm, melt_ref),
                (patch_hbm, patch_ref),
                (probe_hbm, probe_ref),
                (send_hbm, send_ref),
            )
        )
    ]
    for copy in copies:
        copy.start()
    for copy in copies:
        copy.wait()
    pairs = melt_ref.shape[0]
    pert = probe_ref.shape[0]
    capacity = send_ref.shape[2]
    low = low_half((1, LANES))
    lane = lax.broadcasted_iota(jnp.int32, (HALF, LANES), 1)
    turned = jnp.transpose(jnp.concatenate([melt_ref[...], jnp.zeros((LANES - pairs, LANES), F32)], axis=0))
    even = jnp.take_along_axis(turned[:HALF], lane // 2, axis=1)
    odd = jnp.take_along_axis(turned[HALF:], lane // 2, axis=1)
    melt = jnp.where(lane % 2 == 0, even, odd)
    sums = [
        jnp.sum(diag_ref[i].astype(F32) * melt, axis=0, keepdims=True)
        for i in range(diag_ref.shape[0])
    ]
    sums = jnp.concatenate(sums, axis=0)
    source = 2 * (lane % HALF)
    both = jnp.concatenate(
        [
            jnp.take_along_axis(sums, source, axis=1),
            jnp.take_along_axis(sums, source + 1, axis=1),
        ],
        axis=0,
    )
    w_ref[...] = jnp.transpose(both)[:pairs]
    patch_row = jnp.broadcast_to(patch_ref[...].astype(F32), (8, LANES))
    lane = lax.broadcasted_iota(jnp.int32, (8, LANES), 1)
    for part in range(parts):
        out_ref[part, :pert] = probe_ref[...]
    me = lax.axis_index("dom")
    for group, offset in enumerate(OFFSET_LIST):
        to = lax.rem(me + offset + parts, parts)
        ids = jnp.zeros((8, LANES), jnp.int32)
        for slot in range(capacity):
            block = jnp.maximum(send_ref[0, group, slot], 0)
            row = w_ref[pl.ds(block // 2, 1), :]
            out_ref[to, pert + slot : pert + slot + 1, :] = jnp.where(
                low == (block % 2 == 0), row, swap_halves(row)
            )
            ids = jnp.where(lane == group * capacity + slot, block, ids)
        mine = (lane >= group * capacity) & (lane < (group + 1) * capacity)
        out_ref[to, pert + capacity :, :] = jnp.where(
            mine, jnp.take_along_axis(patch_row, ids, axis=1), 0.0
        )


def gather_rows(quad, cols_ref, ext_ref, low):
    rows = []
    for place in range(QUAD):
        g = quad * QUAD + place
        tiles = [ext_ref[cols_ref[k, g]] for k in range(4)]
        rows.append(
            jnp.concatenate(
                [jnp.where(low, tiles[0], tiles[1]), jnp.where(low, tiles[2], tiles[3])], axis=1
            )
        )
    return rows


def coupled_rows(quad, rows, m_ref):
    rhs = m_ref[pl.ds(quad * QUAD, QUAD)].reshape(QUAD * HALF, 4 * HALF)
    return lax.dot_general(
        jnp.concatenate(rows, axis=0), rhs, (((1,), (1,)), ((), ())), preferred_element_type=F32
    )


def own_pairs(out, size, low):
    first = jnp.where(low, out[:size, :LANES], out[size : 2 * size, :LANES])
    second = jnp.where(low, out[2 * size : 3 * size, LANES:], out[3 * size : 4 * size, LANES:])
    return first, second


def gather_multiply(quad, cols_ref, ext_ref, m_ref, low):
    out = coupled_rows(quad, gather_rows(quad, cols_ref, ext_ref, low), m_ref)
    return own_pairs(out, out.shape[0] // QUAD, low)


def store_pair(ref, pair, value, low):
    value = value.astype(BF16)
    other = swap_halves(value.astype(F32)).astype(BF16)
    ref[2 * pair] = jnp.where(low, value, other)
    ref[2 * pair + 1] = jnp.where(low, other, value)


def fill_messages(send_ref, ref, msg_refs, low):
    for group, msg_ref in enumerate(msg_refs):
        for pair in range(send_ref.shape[2] // 2):
            even, odd = (
                ref[jnp.maximum(send_ref[0, group, 2 * pair + half], 0)] for half in range(2)
            )
            msg_ref[pair] = jnp.where(low, even, odd)


def patches_of_columns(columns_ref, ids):
    columns = jnp.concatenate([columns_ref[...], columns_ref[...]], axis=0)
    here = jnp.broadcast_to(ids[:, :LANES], columns.shape)
    there = jnp.broadcast_to(ids[:, LANES:], columns.shape)
    return jnp.where(
        columns < LANES,
        jnp.take_along_axis(here, jnp.minimum(columns, LANES - 1), axis=1),
        jnp.take_along_axis(there, jnp.maximum(columns - LANES, 0), axis=1),
    )


def first_kernel(
    cols_ref, send_ref, patch_ref, columns_ref, got_ref, w_hbm, diag_ref, coupling_hbm,
    m_ref, v_ref, names_ref, patches_ref, t1_ref, t2_ref, o0, o1, o2, o3,
    ext_ref, row_ref, w_ref, coupling_ref, w_sem, sems,
):
    w_copy = pltpu.make_async_copy(w_hbm, w_ref, w_sem)
    w_copy.start()
    chunks = sems.shape[0]
    size = diag_ref.shape[0] // chunks
    copies = [
        pltpu.make_async_copy(
            coupling_hbm.at[chunk * size : (chunk + 1) * size],
            coupling_ref.at[chunk * size : (chunk + 1) * size],
            sems.at[chunk],
        )
        for chunk in range(chunks)
    ]
    for copy in copies:
        copy.start()
    pert = t1_ref.shape[1]
    capacity = send_ref.shape[2]
    blocks = cols_ref.shape[1]
    parts = got_ref.shape[0]
    sources = neighbours(parts)
    low = low_half((pert, LANES))
    lane = lax.broadcasted_iota(jnp.int32, (1, LANES), 1)
    ghost_ids = sum(got_ref[source, pert + capacity : pert + capacity + 1, :] for source in sources)
    ghost_ids = jnp.where(lane < 4 * capacity, ghost_ids, -1.0)
    ids = jnp.concatenate([patch_ref[...].astype(F32), ghost_ids], axis=1)
    total = jnp.zeros((3 * pert, 2 * LANES), F32)
    for part in range(parts):
        names = (
            lax.broadcasted_iota(jnp.int32, (LANES, 2 * LANES), 0) + part * LANES
        ).astype(F32)
        hot = jnp.where(names == ids, 1.0, 0.0).astype(BF16)
        value = got_ref[part, :pert]
        top = value.astype(BF16)
        rest = value - top.astype(F32)
        mid = rest.astype(BF16)
        last = (rest - mid.astype(F32)).astype(BF16)
        total = total + jnp.dot(
            jnp.concatenate([top, mid, last], axis=0), hot, preferred_element_type=F32
        )
    picked = total[:pert] + total[pert : 2 * pert] + total[2 * pert :]
    local_picked = picked[:, :LANES]
    ghost_picked = picked[:, LANES:]
    full_low = low.astype(jnp.int32)
    column_patches = patches_of_columns(columns_ref, ids)
    patches_ref[...] = column_patches
    sub = lax.broadcasted_iota(jnp.int32, (8, LANES), 0)
    lane8 = lax.broadcasted_iota(jnp.int32, (8, LANES), 1)
    wanted = sub == lane8 % 4

    def listed(blocks_of_lanes):
        taken = jnp.take_along_axis(column_patches, blocks_of_lanes, axis=1)
        return jnp.sum(jnp.where(wanted, taken, 0.0), axis=0, keepdims=True)

    for tile in range(4 * blocks // LANES):
        names_ref[tile : tile + 1, :] = listed(tile * (LANES // 4) + lane8 // 4)
    w_copy.wait()
    w = w_ref[...]
    w_other = swap_halves(w)
    low_w = low_half(w.shape)
    row_ref[pl.ds(0, blocks // 2, stride=2), :] = jnp.where(low_w, w, w_other)
    row_ref[pl.ds(1, blocks // 2, stride=2), :] = jnp.where(low_w, w_other, w)
    for group, source in enumerate(sources):
        start = blocks + group * capacity
        row_ref[start : start + capacity, :] = got_ref[source, pert : pert + capacity, :]

    def seed(pair, _):
        index = 2 * pair + 1 - full_low
        spread = jnp.take_along_axis(local_picked, index, axis=1)
        value = spread * w_ref[pl.ds(pair, 1), :]
        t1_ref[pair] = value
        store_pair(ext_ref, pair, value, low)
        return 0

    lax.fori_loop(0, blocks // 2, seed, 0, unroll=16)
    for group, source in enumerate(sources):
        for slot in range(capacity):
            place = group * capacity + slot
            row = got_ref[source, pert + slot : pert + slot + 1, :]
            spread = jnp.broadcast_to(ghost_picked[:, place : place + 1], (pert, LANES))
            ext_ref[blocks + place] = (spread * row).astype(BF16)

    for chunk, copy in enumerate(copies):
        copy.wait()
        for block in range(chunk * size, (chunk + 1) * size):
            m_ref[block] = jnp.dot(
                diag_ref[block], coupling_ref[block], preferred_element_type=F32
            ).astype(BF16)

    low8 = low_half((8, LANES))
    masks = [(sub % 4 == k) & (low8 if k % 2 == 0 else ~low8) for k in range(4)]
    nothing = jnp.zeros((8, LANES), F32)

    def sweep(quad, _):
        rows = gather_rows(quad, cols_ref, ext_ref, low)
        tiles = ([], [])
        for place in range(QUAD):
            w_rows = [row_ref[pl.ds(cols_ref[k, quad * QUAD + place], 1), :] for k in range(4)]
            for side in range(2):
                tiles[side].append(
                    jnp.where(
                        masks[2 * side],
                        w_rows[2 * side],
                        jnp.where(masks[2 * side + 1], w_rows[2 * side + 1], nothing),
                    )
                )
        extra = jnp.concatenate([jnp.concatenate(side, axis=0) for side in tiles], axis=1)
        out = coupled_rows(quad, rows + [extra.astype(BF16)], m_ref)
        for place, value in enumerate(own_pairs(out, pert, low)):
            pair = 2 * quad + place
            store_pair(t2_ref, pair, t1_ref[pair] - value, low)
        for place, value in enumerate(own_pairs(out[QUAD * pert :], 8, low8)):
            v_ref[2 * quad + place] = value
        return 0

    lax.fori_loop(0, blocks // QUAD, sweep, 0, unroll=32)
    msgs = (o0, o1, o2, o3)
    fill_messages(send_ref, t2_ref, msgs, low)
    half = capacity // 2
    for group, ref in enumerate(msgs):
        places = jnp.zeros((8, LANES), jnp.int32)
        values = []
        for slot in range(capacity):
            block = jnp.maximum(send_ref[0, group, slot], 0)
            value = v_ref[block // 2]
            right = (slot - block) % 2 == 0
            values.append(jnp.where(right, value, swap_halves(value)))
            places = jnp.where(lane8 // 4 == slot, block, places)
        pairs = [
            jnp.where(low8, values[2 * pair], values[2 * pair + 1]) for pair in range(half)
        ]
        for tile in range(half // 2):
            ref[half + tile] = jnp.concatenate(pairs[2 * tile : 2 * tile + 2], axis=0).astype(BF16)
        patch = listed(places).astype(jnp.int32)
        ref[half + half // 2] = jnp.concatenate(
            [
                jnp.broadcast_to(patch // RADIX, (8, LANES)),
                jnp.broadcast_to(patch % RADIX, (8, LANES)),
            ],
            axis=0,
        ).astype(F32).astype(BF16)


def extend(ext_ref, local_ref, ghosts, low):
    blocks = local_ref.shape[0]
    count = (ext_ref.shape[0] - blocks) // 2 // len(ghosts)
    ext_ref[:blocks] = local_ref[...]
    for group, ref in enumerate(ghosts):
        for pair in range(count):
            store_pair(ext_ref, blocks // 2 + group * count + pair, ref[pair], low)


def sweep_kernel(
    cols_ref, send_ref, t1_ref, prev_ref, g0, g1, g2, g3, m_ref,
    next_ref, o0, o1, o2, o3, ext_ref,
):
    low = low_half(prev_ref.shape[1:])
    extend(ext_ref, prev_ref, (g0, g1, g2, g3), low)

    def sweep(quad, _):
        first, second = gather_multiply(quad, cols_ref, ext_ref, m_ref, low)
        store_pair(next_ref, 2 * quad, t1_ref[2 * quad] - first, low)
        store_pair(next_ref, 2 * quad + 1, t1_ref[2 * quad + 1] - second, low)
        return 0

    lax.fori_loop(0, cols_ref.shape[1] // QUAD, sweep, 0, unroll=32)
    fill_messages(send_ref, next_ref, (o0, o1, o2, o3), low)


def zero_rows(acc_refs, places):
    for ref in acc_refs:
        for place in places:
            ref[place] = jnp.zeros(ref.shape[1:], F32)


def multiply_scatter(quad, cols_ref, pairs, m_ref, acc_refs, low):
    zero = jnp.zeros(pairs[0].shape, F32)
    rows = []
    for place in range(QUAD):
        value = pairs[place // 2]
        kept = jnp.where(low, value, zero) if place % 2 == 0 else jnp.where(low, zero, value)
        tiles = [kept, zero] if place < 2 else [zero, kept]
        rows.append(jnp.concatenate(tiles, axis=1))
    lhs = jnp.concatenate(rows, axis=0).astype(BF16)
    rhs = m_ref[pl.ds(quad * QUAD, QUAD)].reshape(QUAD * HALF, 4 * HALF)
    out = jnp.dot(lhs, rhs, preferred_element_type=F32)
    p = pairs[0].shape[0]
    for place in range(QUAD):
        g = quad * QUAD + place
        for k in range(4):
            column = cols_ref[k, g]
            piece = out[place * p : (place + 1) * p, (k // 2) * LANES : (k // 2 + 1) * LANES]
            acc_refs[k][column] = acc_refs[k][column] + piece


def half_sums(acc_refs, place, low):
    return jnp.where(
        low, acc_refs[0][place] + acc_refs[2][place], acc_refs[1][place] + acc_refs[3][place]
    )


def pair_sum(acc_refs, pair, low):
    even = half_sums(acc_refs, 2 * pair, low)
    odd = half_sums(acc_refs, 2 * pair + 1, low)
    return jnp.where(low, even, odd) + swap_halves(jnp.where(low, odd, even))


def turn_kernel(
    cols_ref, t1_ref, prev_ref, g0, g1, g2, g3, m_ref, weight_ref, w_ref,
    tangent_hbm, terms_ref, z_ref, y_ref,
    ext_ref, tangent_ref, target_ref, u_ref, sem, *acc_refs,
):
    pert = prev_ref.shape[1]
    low = low_half(prev_ref.shape[1:])
    lane = lax.broadcasted_iota(jnp.int32, (pert, LANES), 1)
    blocks = cols_ref.shape[1]
    extend(ext_ref, prev_ref, (g0, g1, g2, g3), low)

    share = acc_refs[0].shape[0] // (blocks // QUAD)

    def sweep(quad, terms):
        zero_rows(acc_refs, [share * quad + i for i in range(share)])
        coupled = gather_multiply(quad, cols_ref, ext_ref, m_ref, low)
        for place in range(2):
            pair = 2 * quad + place
            value = t1_ref[pair] - coupled[place]
            start = pl.multiple_of(pair * LANES, LANES)
            tangent_ref[:, pl.ds(start, LANES)] = value
            target = value * weight_ref[pl.ds(pair, 1), :]
            target_ref[pair] = target
            product = target * w_ref[pl.ds(pair, 1), :]
            even = jnp.sum(jnp.where(low, product, 0.0), axis=1, keepdims=True)
            odd = jnp.sum(jnp.where(low, 0.0, product), axis=1, keepdims=True)
            terms = jnp.where(
                lane == 2 * pair, even, jnp.where(lane == 2 * pair + 1, odd, terms)
            )
        return terms

    terms_ref[...] = lax.fori_loop(
        0, blocks // QUAD, sweep, jnp.zeros((pert, LANES), F32), unroll=32
    )
    tangent_copy = pltpu.make_async_copy(tangent_ref, tangent_hbm, sem)
    tangent_copy.start()
    scatter_all(cols_ref, target_ref, m_ref, acc_refs, low)

    def own(pair, _):
        u_ref[pair] = target_ref[pair] - pair_sum(acc_refs, pair, low)
        zero_rows(acc_refs, (2 * pair, 2 * pair + 1))
        return 0

    lax.fori_loop(0, blocks // 2, own, 0, unroll=16)
    for pair in range(y_ref.shape[0]):
        y_ref[pair] = (-pair_sum(acc_refs, blocks // 2 + pair, low)).astype(BF16)
        zero_rows(acc_refs, (blocks + 2 * pair, blocks + 2 * pair + 1))
    scatter_all(cols_ref, u_ref, m_ref, acc_refs, low)

    def second(pair, _):
        z_ref[pair] = (pair_sum(acc_refs, pair, low) - target_ref[pair]).astype(BF16)
        return 0

    lax.fori_loop(0, blocks // 2, second, 0, unroll=16)
    for pair in range(blocks // 2, z_ref.shape[0]):
        z_ref[pair] = pair_sum(acc_refs, pair, low).astype(BF16)
    tangent_copy.wait()


def scatter_all(cols_ref, u_ref, m_ref, acc_refs, low):
    def sweep(quad, _):
        pairs = [u_ref[2 * quad], u_ref[2 * quad + 1]]
        multiply_scatter(quad, cols_ref, pairs, m_ref, acc_refs, low)
        return 0

    lax.fori_loop(0, cols_ref.shape[1] // QUAD, sweep, 0, unroll=32)


def write_hot(hot_ref, rows, part):
    start = pl.multiple_of(part * LANES, LANES)
    names = lax.broadcasted_iota(jnp.int32, (LANES, LANES), 0) + part * LANES
    names = names.astype(F32)
    for tile, row in enumerate(rows):
        hot_ref[pl.ds(start, LANES), tile * LANES : (tile + 1) * LANES] = jnp.where(
            names == row, 1.0, 0.0
        ).astype(BF16)


def window_kernel(
    cols_ref, send_ref, columns_ref, patch_ref, names_ref, patches_ref, g0, g1, g2, g3,
    v_ref, m_ref, hot_ref, o0, o1, o2, o3, vector_ref,
):
    ghosts = (g0, g1, g2, g3)
    capacity = send_ref.shape[2]
    half = capacity // 2
    blocks = cols_ref.shape[1]
    low8 = low_half((8, LANES))
    sub = lax.broadcasted_iota(jnp.int32, (8, LANES), 0)
    lane = lax.broadcasted_iota(jnp.int32, (8, LANES), 1)

    listed = []
    there = jnp.zeros((8, LANES), F32)
    for group, ref in enumerate(ghosts):
        digits = ref[ref.shape[0] - 1].astype(F32)
        listed.append(digits[0:1] * RADIX + digits[8:9])
        taken = jnp.take_along_axis(
            jnp.broadcast_to(listed[-1], (8, LANES)), (lane % capacity) * 4 + sub % 4, axis=1
        )
        there = jnp.where(lane // capacity == group, taken, there)
    here = patches_ref[...]
    rows = [patch_ref[...].astype(F32)] + [names_ref[tile : tile + 1] for tile in range(4)]
    for tile in range(2):
        rows.append(
            jnp.where(low8[:1], listed[2 * tile], swap_halves(listed[2 * tile + 1]))
        )

    def spread(pair, value):
        other = swap_halves(value)
        vector_ref[2 * pair] = jnp.where(low8, value, other)
        vector_ref[2 * pair + 1] = jnp.where(low8, other, value)

    for pair in range(blocks // 2):
        spread(pair, v_ref[pair])
    for group, ref in enumerate(ghosts):
        for tile in range(half // 2):
            both = ref[half + tile].astype(F32)
            for side in range(2):
                pair = blocks // 2 + group * half + 2 * tile + side
                spread(pair, both[8 * side : 8 * side + 8])

    own = (sub < 4) == low8
    nothing = jnp.zeros((8, LANES), F32)
    low = low_half((16, LANES))
    columns = jnp.concatenate([columns_ref[...], columns_ref[...]], axis=0)
    sub16 = lax.broadcasted_iota(jnp.int32, (16, LANES), 0)
    for group, ref in enumerate((o0, o1, o2, o3)):
        slots = [jnp.maximum(send_ref[0, group, slot], 0) for slot in range(capacity)]
        for four in range(capacity // QUAD):
            lhs = []
            rhs = []
            for block in slots[four * QUAD : (four + 1) * QUAD]:
                a0, a1, a2, a3 = (vector_ref[cols_ref[k, block]] for k in range(4))
                left = jnp.where(own, jnp.where(sub < 4, a0, a1), nothing)
                right = jnp.where(own, jnp.where(sub < 4, a2, a3), nothing)
                lhs.append(
                    jnp.concatenate(
                        [
                            jnp.concatenate([left, nothing], axis=0),
                            jnp.concatenate([nothing, right], axis=0),
                        ],
                        axis=1,
                    ).astype(BF16)
                )
                rhs.append(m_ref[block])
            out = lax.dot_general(
                jnp.concatenate(lhs, axis=0),
                jnp.concatenate(rhs, axis=0),
                (((1,), (1,)), ((), ())),
                preferred_element_type=F32,
            )
            for side, value in enumerate(own_pairs(out, 16, low)):
                ref[2 * four + side] = value.astype(BF16)
        digits = jnp.zeros((16, LANES), F32)
        for tile in range(2):
            places = jnp.zeros((8, LANES), jnp.int32)
            for slot in range(half):
                places = jnp.where(lane // 16 == slot, slots[tile * half + slot], places)
            taken = jnp.take_along_axis(columns, places, axis=1).astype(F32)
            mine = jnp.sum(
                jnp.where(sub == (lane % 16) // 4, taken, 0.0), axis=0, keepdims=True
            )
            mine = jnp.broadcast_to(mine, (8, LANES)).astype(jnp.int32)
            taken = jnp.where(
                mine < LANES,
                jnp.take_along_axis(here, jnp.minimum(mine, LANES - 1), axis=1),
                jnp.take_along_axis(there, jnp.maximum(mine - LANES, 0), axis=1),
            )
            patch = jnp.sum(jnp.where(sub == lane % 4, taken, 0.0), axis=0, keepdims=True)
            patch = patch.astype(jnp.int32)
            digits = jnp.where(
                sub16 == 2 * tile,
                (patch // RADIX).astype(F32),
                jnp.where(sub16 == 2 * tile + 1, (patch % RADIX).astype(F32), digits),
            )
        ref[half] = digits.astype(BF16)

    def one(part, _):
        write_hot(hot_ref, rows, part)
        return 0

    lax.fori_loop(0, hot_ref.shape[0] // LANES, one, 0, unroll=2)


def last_kernel(
    z_ref, y_ref, v_ref, v0, v1, v2, v3, x0, x1, x2, x3,
    hot_ref, terms_ref, got_ref, out_ref,
):
    pert = z_ref.shape[1]
    local_pairs = v_ref.shape[0]
    half = (z_ref.shape[0] - local_pairs) // 4
    parts = got_ref.shape[0]
    low8 = low_half((8, LANES))
    low = low_half((16, LANES))
    sub = lax.broadcasted_iota(jnp.int32, (8, LANES), 0)
    own = (sub < 4) == low8
    nothing = jnp.zeros((8, LANES), F32)
    zero = jnp.zeros((16, LANES), F32)

    def wide(left, right):
        return jnp.concatenate([left, right], axis=1)

    def product(lhs, rhs):
        return lax.dot_general(
            lhs, rhs.astype(BF16), (((1,), (1,)), ((), ())), preferred_element_type=F32
        )

    def first_level(first, second):
        return jnp.concatenate(
            [
                wide(jnp.where(own, first, nothing), nothing),
                wide(nothing, jnp.where(own, second, nothing)),
            ],
            axis=0,
        )

    def second_level(first, second):
        return jnp.concatenate(
            [
                wide(jnp.where(low, first, zero), zero),
                wide(jnp.where(low, zero, first), zero),
                wide(zero, jnp.where(low, second, zero)),
                wide(zero, jnp.where(low, zero, second)),
            ],
            axis=0,
        )

    pieces = [terms_ref[...]]
    for pair in range(0, local_pairs, 2):
        lhs = wide(z_ref[pair], z_ref[pair + 1])
        pieces.append(product(lhs, first_level(v_ref[pair], v_ref[pair + 1])))
    for group, ref in enumerate((v0, v1, v2, v3)):
        for tile in range(half // 2):
            both = ref[half + tile].astype(F32)
            pair = local_pairs + group * half + 2 * tile
            lhs = wide(z_ref[pair], z_ref[pair + 1])
            pieces.append(product(lhs, first_level(both[:8], both[8:])))
    rows = []
    for group, ref in enumerate((x0, x1, x2, x3)):
        for tile in range(half // 2):
            pair = group * half + 2 * tile
            lhs = wide(y_ref[pair], y_ref[pair + 1])
            first, second = (ref[2 * tile + side].astype(F32) for side in range(2))
            pieces.append(product(lhs, second_level(first, second)))
        digits = ref[half].astype(F32)
        for tile in range(2):
            rows.append(
                digits[2 * tile : 2 * tile + 1] * RADIX + digits[2 * tile + 1 : 2 * tile + 2]
            )
    terms = jnp.concatenate(pieces, axis=1)
    top = terms.astype(BF16)
    rest = (terms - top.astype(F32)).astype(BF16)
    both = jnp.concatenate([top, rest], axis=0)
    mine = lax.axis_index("pert")
    sub16 = lax.broadcasted_iota(jnp.int32, (pert, LANES), 0)
    perts = out_ref.shape[0] // parts
    first_names = lax.broadcasted_iota(jnp.int32, (LANES, LANES), 0).astype(F32)
    for part in range(parts):
        hot = jnp.concatenate(
            [hot_ref[part * LANES : (part + 1) * LANES, :]]
            + [
                jnp.where(first_names == row - part * LANES, 1.0, 0.0).astype(BF16)
                for row in rows
            ],
            axis=1,
        )
        out = lax.dot_general(both, hot, (((1,), (1,)), ((), ())), preferred_element_type=F32)
        value = out[:pert] + out[pert:]
        curve = jnp.sum(value * got_ref[part, :pert], axis=0, keepdims=True)
        top = curve.astype(BF16).astype(F32)
        extra = jnp.where(sub16 == 0, top, jnp.where(sub16 == 1, curve - top, 0.0))
        for place in range(perts):
            out_ref[part * perts + place] = jnp.where(place == mine, value, extra).astype(BF16)


def owner_kernel(terms_ref, probe_ref, hessian_ref, curve_ref, *, parts, scale):
    perts = terms_ref.shape[0] // parts
    mine = lax.axis_index("pert")
    total = jnp.zeros(hessian_ref.shape, F32)
    every = jnp.zeros(hessian_ref.shape, F32)
    for part in range(parts):
        total = total + terms_ref[part * perts + mine].astype(F32)
        for place in range(perts):
            value = terms_ref[part * perts + place].astype(F32)
            every = every + jnp.where(place == mine, 0.0, value)
    hessian_ref[...] = total
    own = jnp.sum(total * probe_ref[...], axis=0, keepdims=True)
    curve_ref[...] = (own + every[0:1] + every[1:2]) * scale


def call(body, outs, spaces, scratch=(), name=None, flops=0, moved=1 << 20, limit=12, out_specs=None):
    return pl.pallas_call(
        body,
        out_shape=outs,
        in_specs=[{"s": SMEM, "v": VMEM, "h": HBM}[s] for s in spaces],
        out_specs=out_specs or jax.tree.map(lambda _: VMEM, outs),
        scratch_shapes=list(scratch),
        compiler_params=pltpu.CompilerParams(vmem_limit_bytes=limit * MIB),
        name=name,
        cost_estimate=pl.CostEstimate(flops=flops, transcendentals=0, bytes_accessed=moved),
    )


def shards(
    probes, melt_shape, obs_weight, diag_inverse, coupling, columns, send_list, patch_of_block
):
    pert = probes.shape[0]
    blocks = coupling.shape[0]
    capacity = send_list.shape[2]
    parts = lax.axis_size("dom")
    pairs = blocks // 2
    shape = jax.ShapeDtypeStruct
    msgs = [shape((capacity // 2, pert, LANES), BF16)] * 4
    pair_array = shape((pairs, pert, LANES), F32)
    block_array = shape((blocks, pert, LANES), BF16)
    ext = pltpu.VMEM((blocks + 4 * capacity, pert, LANES), BF16)
    accs = [pltpu.VMEM((blocks + 4 * capacity, pert, LANES), F32)] * 4
    held = pltpu.VMEM((pairs, pert, LANES), F32)
    melt = melt_shape.reshape(pairs, LANES)
    weight = obs_weight.reshape(pairs, LANES)
    patch = patch_of_block.reshape(1, blocks)

    perts = lax.axis_size("pert")
    columns = columns.T
    w, outgoing = call(
        functools.partial(melt_kernel, parts=parts),
        [shape((pairs, LANES), F32), shape((parts, pert + capacity + 8, LANES), F32)],
        "hhhhh",
        [
            pltpu.SMEM(send_list.shape, jnp.int32),
            pltpu.VMEM((pairs, LANES), F32),
            pltpu.VMEM((1, blocks), jnp.int32),
            pltpu.VMEM(probes.shape, F32),
            pltpu.VMEM((HALF, HALF, blocks), BF16),
            pltpu.SemaphoreType.DMA((5,)),
        ],
        name="melt",
        limit=60,
    )(send_list, melt, patch, probes, jnp.transpose(diag_inverse, (1, 2, 0)))
    got = lax.all_to_all(outgoing, "dom", 0, 0, tiled=True)
    wide = [shape((capacity // 2 + capacity // 4 + 1, pert, LANES), BF16)] * 4
    m, v, names, patches, t1, state, *out = call(
        first_kernel,
        [
            shape(coupling.shape, BF16),
            shape((pairs, 8, LANES), F32),
            shape((8, LANES), F32),
            shape((8, LANES), F32),
            pair_array,
            block_array,
        ]
        + wide,
        "ssvvvhvh",
        [
            ext,
            pltpu.VMEM((blocks + 4 * capacity, LANES), F32),
            pltpu.VMEM((pairs, LANES), F32),
            pltpu.VMEM(coupling.shape, BF16),
            pltpu.SemaphoreType.DMA,
            pltpu.SemaphoreType.DMA((8,)),
        ],
        name="first",
        limit=46,
    )(columns, send_list, patch, columns, got, w, diag_inverse, coupling)
    carried = [rotated(x, o) for x, o in zip(out, OFFSET_LIST)]
    state, *out = call(
        sweep_kernel, [block_array] + msgs, "ssvvvvvvv", [ext], name="sweep"
    )(columns, send_list, t1, state, *carried, m)
    ghosts = [rotated(v, o) for v, o in zip(out, OFFSET_LIST)]
    hot, *far = call(
        window_kernel,
        [shape((parts * LANES, 7 * LANES), BF16)]
        + [shape((capacity // 2 + 1, pert, LANES), BF16)] * 4,
        "ss" + "v" * 10,
        [pltpu.VMEM((blocks + 4 * capacity, 8, LANES), F32)],
        name="window",
        moved=4 << 20,
    )(columns, send_list, columns, patch, names, patches, *carried, v, m)
    far, ghosts = lax.optimization_barrier((far, ghosts))
    far = [rotated(x, o) for x, o in zip(far, OFFSET_LIST)]
    tangent, terms, z, y = call(
        turn_kernel,
        [
            shape((pert, blocks * HALF), F32),
            shape((pert, LANES), F32),
            shape((pairs + 2 * capacity, pert, LANES), BF16),
            shape((2 * capacity, pert, LANES), BF16),
        ],
        "s" + "v" * 9,
        [
            ext,
            pltpu.VMEM((pert, blocks * HALF), F32),
            held,
            held,
            pltpu.SemaphoreType.DMA,
        ]
        + accs,
        name="turn",
        moved=16 << 20,
        out_specs=[HBM, VMEM, VMEM, VMEM],
    )(columns, t1, state, *ghosts, m, weight, w)
    terms = call(
        last_kernel, shape((parts * perts, pert, LANES), BF16), "v" * 14, name="last"
    )(z, y, v, *carried, *far, hot, terms, got)
    terms = lax.all_to_all(terms, ("dom", "pert"), 0, 0, tiled=True)
    hessian_probe, curvature = call(
        functools.partial(owner_kernel, parts=parts, scale=1.0 / (pert * perts)),
        [shape(probes.shape, F32), shape((1, LANES), F32)],
        "vv",
        name="owner",
    )(terms, probes)
    return tangent, hessian_probe, curvature.reshape(-1)


def solution(mesh):
    in_specs = (
        P("pert", "dom"),
        P("dom"),
        P("dom"),
        P("dom", None, None),
        P("dom", None, None),
        P("dom", None),
        P("dom", None, None),
        P("dom"),
    )
    out_specs = (P("pert", "dom"), P("pert", "dom"), P("dom"))
    return jax.shard_map(shards, mesh=mesh, in_specs=in_specs, out_specs=out_specs, check_vma=False)
```

```python
import functools

import jax
import jax.numpy as jnp
from jax import lax
from jax.experimental import pallas as pl
from jax.experimental.pallas import tpu as pltpu
from jax.sharding import PartitionSpec as P

OFFSET_LIST = (-2, -1, 1, 2)
F32 = jnp.float32
BF16 = jnp.bfloat16
LANES = 128
HALF = 64
QUAD = 4
RADIX = 64
EARLY = 32

VMEM = pl.BlockSpec(memory_space=pltpu.VMEM)
SMEM = pl.BlockSpec(memory_space=pltpu.SMEM)
HBM = pl.BlockSpec(memory_space=pltpu.HBM)
MIB = 1024 * 1024


def low_half(shape):
    return lax.broadcasted_iota(jnp.int32, shape, len(shape) - 1) < HALF


def swap_halves(value):
    return pltpu.roll(value, HALF, 1)


def rotated(value, by):
    peers = lax.axis_size("dom")
    return lax.ppermute(value, "dom", [(i, (i + by) % peers) for i in range(peers)])


def neighbours(parts):
    me = lax.axis_index("dom")
    return [lax.rem(me - offset + parts, parts) for offset in OFFSET_LIST]


def melt_kernel(
    send_hbm, melt_hbm, patch_hbm, probe_hbm, diag_hbm, w_ref, out_ref,
    send_ref, melt_ref, patch_ref, probe_ref, diag_ref, sems, *, parts,
):
    copies = [
        pltpu.make_async_copy(source, target, sems.at[number])
        for number, (source, target) in enumerate(
            (
                (diag_hbm, diag_ref),
                (melt_hbm, melt_ref),
                (patch_hbm, patch_ref),
                (probe_hbm, probe_ref),
                (send_hbm, send_ref),
            )
        )
    ]
    for copy in copies:
        copy.start()
    for copy in copies:
        copy.wait()
    pairs = melt_ref.shape[0]
    pert = probe_ref.shape[0]
    capacity = send_ref.shape[2]
    low = low_half((1, LANES))
    lane = lax.broadcasted_iota(jnp.int32, (HALF, LANES), 1)
    turned = jnp.transpose(jnp.concatenate([melt_ref[...], jnp.zeros((LANES - pairs, LANES), F32)], axis=0))
    even = jnp.take_along_axis(turned[:HALF], lane // 2, axis=1)
    odd = jnp.take_along_axis(turned[HALF:], lane // 2, axis=1)
    melt = jnp.where(lane % 2 == 0, even, odd)
    sums = [
        jnp.sum(diag_ref[i].astype(F32) * melt, axis=0, keepdims=True)
        for i in range(diag_ref.shape[0])
    ]
    sums = jnp.concatenate(sums, axis=0)
    source = 2 * (lane % HALF)
    both = jnp.concatenate(
        [
            jnp.take_along_axis(sums, source, axis=1),
            jnp.take_along_axis(sums, source + 1, axis=1),
        ],
        axis=0,
    )
    w_ref[...] = jnp.transpose(both)[:pairs]
    patch_row = jnp.broadcast_to(patch_ref[...].astype(F32), (8, LANES))
    lane = lax.broadcasted_iota(jnp.int32, (8, LANES), 1)
    for part in range(parts):
        out_ref[part, :pert] = probe_ref[...]
    me = lax.axis_index("dom")
    for group, offset in enumerate(OFFSET_LIST):
        to = lax.rem(me + offset + parts, parts)
        ids = jnp.zeros((8, LANES), jnp.int32)
        for slot in range(capacity):
            block = jnp.maximum(send_ref[0, group, slot], 0)
            row = w_ref[pl.ds(block // 2, 1), :]
            out_ref[to, pert + slot : pert + slot + 1, :] = jnp.where(
                low == (block % 2 == 0), row, swap_halves(row)
            )
            ids = jnp.where(lane == group * capacity + slot, block, ids)
        mine = (lane >= group * capacity) & (lane < (group + 1) * capacity)
        out_ref[to, pert + capacity :, :] = jnp.where(
            mine, jnp.take_along_axis(patch_row, ids, axis=1), 0.0
        )


def gather_rows(quad, cols_ref, ext_ref, low):
    rows = []
    for place in range(QUAD):
        g = quad * QUAD + place
        tiles = [ext_ref[cols_ref[k, g]] for k in range(4)]
        rows.append(
            jnp.concatenate(
                [jnp.where(low, tiles[0], tiles[1]), jnp.where(low, tiles[2], tiles[3])], axis=1
            )
        )
    return rows


def coupled_rows(quad, rows, m_ref):
    rhs = m_ref[pl.ds(quad * QUAD, QUAD)].reshape(QUAD * HALF, 4 * HALF)
    return lax.dot_general(
        jnp.concatenate(rows, axis=0), rhs, (((1,), (1,)), ((), ())), preferred_element_type=F32
    )


def own_pairs(out, size, low):
    first = jnp.where(low, out[:size, :LANES], out[size : 2 * size, :LANES])
    second = jnp.where(low, out[2 * size : 3 * size, LANES:], out[3 * size : 4 * size, LANES:])
    return first, second


def gather_multiply(quad, cols_ref, ext_ref, m_ref, low):
    out = coupled_rows(quad, gather_rows(quad, cols_ref, ext_ref, low), m_ref)
    return own_pairs(out, out.shape[0] // QUAD, low)


def store_pair(ref, pair, value, low):
    value = value.astype(BF16)
    other = swap_halves(value.astype(F32)).astype(BF16)
    ref[2 * pair] = jnp.where(low, value, other)
    ref[2 * pair + 1] = jnp.where(low, other, value)


def fill_messages(send_ref, ref, msg_refs, low):
    for group, msg_ref in enumerate(msg_refs):
        for pair in range(send_ref.shape[2] // 2):
            even, odd = (
                ref[jnp.maximum(send_ref[0, group, 2 * pair + half], 0)] for half in range(2)
            )
            msg_ref[pair] = jnp.where(low, even, odd)


def start_streams(coupling_hbm, coupling_ref, sems, first):
    size = coupling_ref.shape[0] // sems.shape[0]
    copies = [
        pltpu.make_async_copy(
            coupling_hbm.at[pl.ds(first + chunk * size, size)],
            coupling_ref.at[pl.ds(chunk * size, size)],
            sems.at[chunk],
        )
        for chunk in range(sems.shape[0])
    ]
    for copy in copies:
        copy.start()
    return copies


def multiply_streams(copies, diag_ref, coupling_ref, m_ref, first):
    size = coupling_ref.shape[0] // len(copies)
    for chunk, copy in enumerate(copies):
        copy.wait()
        for block in range(chunk * size, (chunk + 1) * size):
            m_ref[first + block] = jnp.dot(
                diag_ref[first + block], coupling_ref[block], preferred_element_type=F32
            ).astype(BF16)


def settle_kernel(w_hbm, diag_ref, coupling_hbm, w_ref, m_ref, coupling_ref, w_sem, sems):
    w_copy = pltpu.make_async_copy(w_hbm, w_ref, w_sem)
    w_copy.start()
    copies = start_streams(coupling_hbm, coupling_ref, sems, 0)
    multiply_streams(copies, diag_ref, coupling_ref, m_ref, 0)
    w_copy.wait()


def patches_of_columns(columns_ref, ids):
    columns = jnp.concatenate([columns_ref[...], columns_ref[...]], axis=0)
    here = jnp.broadcast_to(ids[:, :LANES], columns.shape)
    there = jnp.broadcast_to(ids[:, LANES:], columns.shape)
    return jnp.where(
        columns < LANES,
        jnp.take_along_axis(here, jnp.minimum(columns, LANES - 1), axis=1),
        jnp.take_along_axis(there, jnp.maximum(columns - LANES, 0), axis=1),
    )


def first_kernel(
    cols_ref, send_ref, patch_ref, columns_ref, got_ref, w_ref, diag_ref, coupling_hbm, early_ref,
    m_ref, v_ref, names_ref, patches_ref, t1_ref, t2_ref, o0, o1, o2, o3,
    ext_ref, row_ref, coupling_ref, sems,
):
    copies = start_streams(coupling_hbm, coupling_ref, sems, EARLY)
    pert = t1_ref.shape[1]
    capacity = send_ref.shape[2]
    blocks = cols_ref.shape[1]
    parts = got_ref.shape[0]
    sources = neighbours(parts)
    low = low_half((pert, LANES))
    lane = lax.broadcasted_iota(jnp.int32, (1, LANES), 1)
    ghost_ids = sum(got_ref[source, pert + capacity : pert + capacity + 1, :] for source in sources)
    ghost_ids = jnp.where(lane < 4 * capacity, ghost_ids, -1.0)
    ids = jnp.concatenate([patch_ref[...].astype(F32), ghost_ids], axis=1)
    total = jnp.zeros((3 * pert, 2 * LANES), F32)
    for part in range(parts):
        names = (
            lax.broadcasted_iota(jnp.int32, (LANES, 2 * LANES), 0) + part * LANES
        ).astype(F32)
        hot = jnp.where(names == ids, 1.0, 0.0).astype(BF16)
        value = got_ref[part, :pert]
        top = value.astype(BF16)
        rest = value - top.astype(F32)
        mid = rest.astype(BF16)
        last = (rest - mid.astype(F32)).astype(BF16)
        total = total + jnp.dot(
            jnp.concatenate([top, mid, last], axis=0), hot, preferred_element_type=F32
        )
    picked = total[:pert] + total[pert : 2 * pert] + total[2 * pert :]
    local_picked = picked[:, :LANES]
    ghost_picked = picked[:, LANES:]
    full_low = low.astype(jnp.int32)
    column_patches = patches_of_columns(columns_ref, ids)
    patches_ref[...] = column_patches
    sub = lax.broadcasted_iota(jnp.int32, (8, LANES), 0)
    lane8 = lax.broadcasted_iota(jnp.int32, (8, LANES), 1)
    wanted = sub == lane8 % 4

    def listed(blocks_of_lanes):
        taken = jnp.take_along_axis(column_patches, blocks_of_lanes, axis=1)
        return jnp.sum(jnp.where(wanted, taken, 0.0), axis=0, keepdims=True)

    for tile in range(4 * blocks // LANES):
        names_ref[tile : tile + 1, :] = listed(tile * (LANES // 4) + lane8 // 4)
    w = w_ref[...]
    w_other = swap_halves(w)
    low_w = low_half(w.shape)
    row_ref[pl.ds(0, blocks // 2, stride=2), :] = jnp.where(low_w, w, w_other)
    row_ref[pl.ds(1, blocks // 2, stride=2), :] = jnp.where(low_w, w_other, w)
    for group, source in enumerate(sources):
        start = blocks + group * capacity
        row_ref[start : start + capacity, :] = got_ref[source, pert : pert + capacity, :]

    def seed(pair, _):
        index = 2 * pair + 1 - full_low
        spread = jnp.take_along_axis(local_picked, index, axis=1)
        value = spread * w_ref[pl.ds(pair, 1), :]
        t1_ref[pair] = value
        store_pair(ext_ref, pair, value, low)
        return 0

    lax.fori_loop(0, blocks // 2, seed, 0, unroll=16)
    for group, source in enumerate(sources):
        for slot in range(capacity):
            place = group * capacity + slot
            row = got_ref[source, pert + slot : pert + slot + 1, :]
            spread = jnp.broadcast_to(ghost_picked[:, place : place + 1], (pert, LANES))
            ext_ref[blocks + place] = (spread * row).astype(BF16)

    multiply_streams(copies, diag_ref, coupling_ref, m_ref, EARLY)
    m_ref[:EARLY] = early_ref[...]
    low8 = low_half((8, LANES))
    masks = [(sub % 4 == k) & (low8 if k % 2 == 0 else ~low8) for k in range(4)]
    nothing = jnp.zeros((8, LANES), F32)

    def sweep(quad, _):
        rows = gather_rows(quad, cols_ref, ext_ref, low)
        tiles = ([], [])
        for place in range(QUAD):
            w_rows = [row_ref[pl.ds(cols_ref[k, quad * QUAD + place], 1), :] for k in range(4)]
            for side in range(2):
                tiles[side].append(
                    jnp.where(
                        masks[2 * side],
                        w_rows[2 * side],
                        jnp.where(masks[2 * side + 1], w_rows[2 * side + 1], nothing),
                    )
                )
        extra = jnp.concatenate([jnp.concatenate(side, axis=0) for side in tiles], axis=1)
        out = coupled_rows(quad, rows + [extra.astype(BF16)], m_ref)
        for place, value in enumerate(own_pairs(out, pert, low)):
            pair = 2 * quad + place
            store_pair(t2_ref, pair, t1_ref[pair] - value, low)
        for place, value in enumerate(own_pairs(out[QUAD * pert :], 8, low8)):
            v_ref[2 * quad + place] = value
        return 0

    lax.fori_loop(0, blocks // QUAD, sweep, 0, unroll=32)
    msgs = (o0, o1, o2, o3)
    fill_messages(send_ref, t2_ref, msgs, low)
    half = capacity // 2
    for group, ref in enumerate(msgs):
        places = jnp.zeros((8, LANES), jnp.int32)
        values = []
        for slot in range(capacity):
            block = jnp.maximum(send_ref[0, group, slot], 0)
            value = v_ref[block // 2]
            right = (slot - block) % 2 == 0
            values.append(jnp.where(right, value, swap_halves(value)))
            places = jnp.where(lane8 // 4 == slot, block, places)
        pairs = [
            jnp.where(low8, values[2 * pair], values[2 * pair + 1]) for pair in range(half)
        ]
        for tile in range(half // 2):
            ref[half + tile] = jnp.concatenate(pairs[2 * tile : 2 * tile + 2], axis=0).astype(BF16)
        patch = listed(places).astype(jnp.int32)
        ref[half + half // 2] = jnp.concatenate(
            [
                jnp.broadcast_to(patch // RADIX, (8, LANES)),
                jnp.broadcast_to(patch % RADIX, (8, LANES)),
            ],
            axis=0,
        ).astype(F32).astype(BF16)


def extend(ext_ref, local_ref, ghosts, low):
    blocks = local_ref.shape[0]
    count = (ext_ref.shape[0] - blocks) // 2 // len(ghosts)
    ext_ref[:blocks] = local_ref[...]
    for group, ref in enumerate(ghosts):
        for pair in range(count):
            store_pair(ext_ref, blocks // 2 + group * count + pair, ref[pair], low)


def sweep_kernel(
    cols_ref, send_ref, t1_ref, prev_ref, g0, g1, g2, g3, m_ref,
    next_ref, o0, o1, o2, o3, ext_ref,
):
    low = low_half(prev_ref.shape[1:])
    extend(ext_ref, prev_ref, (g0, g1, g2, g3), low)

    def sweep(quad, _):
        first, second = gather_multiply(quad, cols_ref, ext_ref, m_ref, low)
        store_pair(next_ref, 2 * quad, t1_ref[2 * quad] - first, low)
        store_pair(next_ref, 2 * quad + 1, t1_ref[2 * quad + 1] - second, low)
        return 0

    lax.fori_loop(0, cols_ref.shape[1] // QUAD, sweep, 0, unroll=32)
    fill_messages(send_ref, next_ref, (o0, o1, o2, o3), low)


def zero_rows(acc_refs, places):
    for ref in acc_refs:
        for place in places:
            ref[place] = jnp.zeros(ref.shape[1:], F32)


def multiply_scatter(quad, cols_ref, pairs, m_ref, acc_refs, low):
    zero = jnp.zeros(pairs[0].shape, F32)
    rows = []
    for place in range(QUAD):
        value = pairs[place // 2]
        kept = jnp.where(low, value, zero) if place % 2 == 0 else jnp.where(low, zero, value)
        tiles = [kept, zero] if place < 2 else [zero, kept]
        rows.append(jnp.concatenate(tiles, axis=1))
    lhs = jnp.concatenate(rows, axis=0).astype(BF16)
    rhs = m_ref[pl.ds(quad * QUAD, QUAD)].reshape(QUAD * HALF, 4 * HALF)
    out = jnp.dot(lhs, rhs, preferred_element_type=F32)
    p = pairs[0].shape[0]
    for place in range(QUAD):
        g = quad * QUAD + place
        for k in range(4):
            column = cols_ref[k, g]
            piece = out[place * p : (place + 1) * p, (k // 2) * LANES : (k // 2 + 1) * LANES]
            acc_refs[k][column] = acc_refs[k][column] + piece


def half_sums(acc_refs, place, low):
    return jnp.where(
        low, acc_refs[0][place] + acc_refs[2][place], acc_refs[1][place] + acc_refs[3][place]
    )


def pair_sum(acc_refs, pair, low):
    even = half_sums(acc_refs, 2 * pair, low)
    odd = half_sums(acc_refs, 2 * pair + 1, low)
    return jnp.where(low, even, odd) + swap_halves(jnp.where(low, odd, even))


def turn_kernel(
    cols_ref, t1_ref, prev_ref, g0, g1, g2, g3, m_ref, weight_ref, w_ref,
    tangent_hbm, terms_ref, z_ref, y_ref,
    ext_ref, tangent_ref, target_ref, u_ref, sem, *acc_refs,
):
    pert = prev_ref.shape[1]
    low = low_half(prev_ref.shape[1:])
    lane = lax.broadcasted_iota(jnp.int32, (pert, LANES), 1)
    blocks = cols_ref.shape[1]
    extend(ext_ref, prev_ref, (g0, g1, g2, g3), low)

    share = acc_refs[0].shape[0] // (blocks // QUAD)

    def sweep(quad, terms):
        zero_rows(acc_refs, [share * quad + i for i in range(share)])
        coupled = gather_multiply(quad, cols_ref, ext_ref, m_ref, low)
        for place in range(2):
            pair = 2 * quad + place
            value = t1_ref[pair] - coupled[place]
            start = pl.multiple_of(pair * LANES, LANES)
            tangent_ref[:, pl.ds(start, LANES)] = value
            target = value * weight_ref[pl.ds(pair, 1), :]
            target_ref[pair] = target
            product = target * w_ref[pl.ds(pair, 1), :]
            even = jnp.sum(jnp.where(low, product, 0.0), axis=1, keepdims=True)
            odd = jnp.sum(jnp.where(low, 0.0, product), axis=1, keepdims=True)
            terms = jnp.where(
                lane == 2 * pair, even, jnp.where(lane == 2 * pair + 1, odd, terms)
            )
        return terms

    terms_ref[...] = lax.fori_loop(
        0, blocks // QUAD, sweep, jnp.zeros((pert, LANES), F32), unroll=32
    )
    tangent_copy = pltpu.make_async_copy(tangent_ref, tangent_hbm, sem)
    tangent_copy.start()
    scatter_all(cols_ref, target_ref, m_ref, acc_refs, low)

    def own(pair, _):
        u_ref[pair] = target_ref[pair] - pair_sum(acc_refs, pair, low)
        zero_rows(acc_refs, (2 * pair, 2 * pair + 1))
        return 0

    lax.fori_loop(0, blocks // 2, own, 0, unroll=16)
    for pair in range(y_ref.shape[0]):
        y_ref[pair] = (-pair_sum(acc_refs, blocks // 2 + pair, low)).astype(BF16)
        zero_rows(acc_refs, (blocks + 2 * pair, blocks + 2 * pair + 1))
    scatter_all(cols_ref, u_ref, m_ref, acc_refs, low)

    def second(pair, _):
        z_ref[pair] = (pair_sum(acc_refs, pair, low) - target_ref[pair]).astype(BF16)
        return 0

    lax.fori_loop(0, blocks // 2, second, 0, unroll=16)
    for pair in range(blocks // 2, z_ref.shape[0]):
        z_ref[pair] = pair_sum(acc_refs, pair, low).astype(BF16)
    tangent_copy.wait()


def scatter_all(cols_ref, u_ref, m_ref, acc_refs, low):
    def sweep(quad, _):
        pairs = [u_ref[2 * quad], u_ref[2 * quad + 1]]
        multiply_scatter(quad, cols_ref, pairs, m_ref, acc_refs, low)
        return 0

    lax.fori_loop(0, cols_ref.shape[1] // QUAD, sweep, 0, unroll=32)


def write_hot(hot_ref, rows, part):
    start = pl.multiple_of(part * LANES, LANES)
    names = lax.broadcasted_iota(jnp.int32, (LANES, LANES), 0) + part * LANES
    names = names.astype(F32)
    for tile, row in enumerate(rows):
        hot_ref[pl.ds(start, LANES), tile * LANES : (tile + 1) * LANES] = jnp.where(
            names == row, 1.0, 0.0
        ).astype(BF16)


def window_kernel(
    cols_ref, send_ref, columns_ref, patch_ref, names_ref, patches_ref, g0, g1, g2, g3,
    v_ref, m_ref, hot_ref, o0, o1, o2, o3, vector_ref,
):
    ghosts = (g0, g1, g2, g3)
    capacity = send_ref.shape[2]
    half = capacity // 2
    blocks = cols_ref.shape[1]
    low8 = low_half((8, LANES))
    sub = lax.broadcasted_iota(jnp.int32, (8, LANES), 0)
    lane = lax.broadcasted_iota(jnp.int32, (8, LANES), 1)

    listed = []
    there = jnp.zeros((8, LANES), F32)
    for group, ref in enumerate(ghosts):
        digits = ref[ref.shape[0] - 1].astype(F32)
        listed.append(digits[0:1] * RADIX + digits[8:9])
        taken = jnp.take_along_axis(
            jnp.broadcast_to(listed[-1], (8, LANES)), (lane % capacity) * 4 + sub % 4, axis=1
        )
        there = jnp.where(lane // capacity == group, taken, there)
    here = patches_ref[...]
    rows = [patch_ref[...].astype(F32)] + [names_ref[tile : tile + 1] for tile in range(4)]
    for tile in range(2):
        rows.append(
            jnp.where(low8[:1], listed[2 * tile], swap_halves(listed[2 * tile + 1]))
        )

    def spread(pair, value):
        other = swap_halves(value)
        vector_ref[2 * pair] = jnp.where(low8, value, other)
        vector_ref[2 * pair + 1] = jnp.where(low8, other, value)

    for pair in range(blocks // 2):
        spread(pair, v_ref[pair])
    for group, ref in enumerate(ghosts):
        for tile in range(half // 2):
            both = ref[half + tile].astype(F32)
            for side in range(2):
                pair = blocks // 2 + group * half + 2 * tile + side
                spread(pair, both[8 * side : 8 * side + 8])

    own = (sub < 4) == low8
    nothing = jnp.zeros((8, LANES), F32)
    low = low_half((16, LANES))
    columns = jnp.concatenate([columns_ref[...], columns_ref[...]], axis=0)
    sub16 = lax.broadcasted_iota(jnp.int32, (16, LANES), 0)
    for group, ref in enumerate((o0, o1, o2, o3)):
        slots = [jnp.maximum(send_ref[0, group, slot], 0) for slot in range(capacity)]
        for four in range(capacity // QUAD):
            lhs = []
            rhs = []
            for block in slots[four * QUAD : (four + 1) * QUAD]:
                a0, a1, a2, a3 = (vector_ref[cols_ref[k, block]] for k in range(4))
                left = jnp.where(own, jnp.where(sub < 4, a0, a1), nothing)
                right = jnp.where(own, jnp.where(sub < 4, a2, a3), nothing)
                lhs.append(
                    jnp.concatenate(
                        [
                            jnp.concatenate([left, nothing], axis=0),
                            jnp.concatenate([nothing, right], axis=0),
                        ],
                        axis=1,
                    ).astype(BF16)
                )
                rhs.append(m_ref[block])
            out = lax.dot_general(
                jnp.concatenate(lhs, axis=0),
                jnp.concatenate(rhs, axis=0),
                (((1,), (1,)), ((), ())),
                preferred_element_type=F32,
            )
            for side, value in enumerate(own_pairs(out, 16, low)):
                ref[2 * four + side] = value.astype(BF16)
        digits = jnp.zeros((16, LANES), F32)
        for tile in range(2):
            places = jnp.zeros((8, LANES), jnp.int32)
            for slot in range(half):
                places = jnp.where(lane // 16 == slot, slots[tile * half + slot], places)
            taken = jnp.take_along_axis(columns, places, axis=1).astype(F32)
            mine = jnp.sum(
                jnp.where(sub == (lane % 16) // 4, taken, 0.0), axis=0, keepdims=True
            )
            mine = jnp.broadcast_to(mine, (8, LANES)).astype(jnp.int32)
            taken = jnp.where(
                mine < LANES,
                jnp.take_along_axis(here, jnp.minimum(mine, LANES - 1), axis=1),
                jnp.take_along_axis(there, jnp.maximum(mine - LANES, 0), axis=1),
            )
            patch = jnp.sum(jnp.where(sub == lane % 4, taken, 0.0), axis=0, keepdims=True)
            patch = patch.astype(jnp.int32)
            digits = jnp.where(
                sub16 == 2 * tile,
                (patch // RADIX).astype(F32),
                jnp.where(sub16 == 2 * tile + 1, (patch % RADIX).astype(F32), digits),
            )
        ref[half] = digits.astype(BF16)

    def one(part, _):
        write_hot(hot_ref, rows, part)
        return 0

    lax.fori_loop(0, hot_ref.shape[0] // LANES, one, 0, unroll=2)


def last_kernel(
    z_ref, y_ref, v_ref, v0, v1, v2, v3, x0, x1, x2, x3,
    hot_ref, terms_ref, got_ref, out_ref,
):
    pert = z_ref.shape[1]
    local_pairs = v_ref.shape[0]
    half = (z_ref.shape[0] - local_pairs) // 4
    parts = got_ref.shape[0]
    low8 = low_half((8, LANES))
    low = low_half((16, LANES))
    sub = lax.broadcasted_iota(jnp.int32, (8, LANES), 0)
    own = (sub < 4) == low8
    nothing = jnp.zeros((8, LANES), F32)
    zero = jnp.zeros((16, LANES), F32)

    def wide(left, right):
        return jnp.concatenate([left, right], axis=1)

    def product(lhs, rhs):
        return lax.dot_general(
            lhs, rhs.astype(BF16), (((1,), (1,)), ((), ())), preferred_element_type=F32
        )

    def first_level(first, second):
        return jnp.concatenate(
            [
                wide(jnp.where(own, first, nothing), nothing),
                wide(nothing, jnp.where(own, second, nothing)),
            ],
            axis=0,
        )

    def second_level(first, second):
        return jnp.concatenate(
            [
                wide(jnp.where(low, first, zero), zero),
                wide(jnp.where(low, zero, first), zero),
                wide(zero, jnp.where(low, second, zero)),
                wide(zero, jnp.where(low, zero, second)),
            ],
            axis=0,
        )

    pieces = [terms_ref[...]]
    for pair in range(0, local_pairs, 2):
        lhs = wide(z_ref[pair], z_ref[pair + 1])
        pieces.append(product(lhs, first_level(v_ref[pair], v_ref[pair + 1])))
    for group, ref in enumerate((v0, v1, v2, v3)):
        for tile in range(half // 2):
            both = ref[half + tile].astype(F32)
            pair = local_pairs + group * half + 2 * tile
            lhs = wide(z_ref[pair], z_ref[pair + 1])
            pieces.append(product(lhs, first_level(both[:8], both[8:])))
    rows = []
    for group, ref in enumerate((x0, x1, x2, x3)):
        for tile in range(half // 2):
            pair = group * half + 2 * tile
            lhs = wide(y_ref[pair], y_ref[pair + 1])
            first, second = (ref[2 * tile + side].astype(F32) for side in range(2))
            pieces.append(product(lhs, second_level(first, second)))
        digits = ref[half].astype(F32)
        for tile in range(2):
            rows.append(
                digits[2 * tile : 2 * tile + 1] * RADIX + digits[2 * tile + 1 : 2 * tile + 2]
            )
    terms = jnp.concatenate(pieces, axis=1)
    top = terms.astype(BF16)
    rest = (terms - top.astype(F32)).astype(BF16)
    both = jnp.concatenate([top, rest], axis=0)
    mine = lax.axis_index("pert")
    sub16 = lax.broadcasted_iota(jnp.int32, (pert, LANES), 0)
    perts = out_ref.shape[0] // parts
    first_names = lax.broadcasted_iota(jnp.int32, (LANES, LANES), 0).astype(F32)
    for part in range(parts):
        hot = jnp.concatenate(
            [hot_ref[part * LANES : (part + 1) * LANES, :]]
            + [
                jnp.where(first_names == row - part * LANES, 1.0, 0.0).astype(BF16)
                for row in rows
            ],
            axis=1,
        )
        out = lax.dot_general(both, hot, (((1,), (1,)), ((), ())), preferred_element_type=F32)
        value = out[:pert] + out[pert:]
        curve = jnp.sum(value * got_ref[part, :pert], axis=0, keepdims=True)
        top = curve.astype(BF16).astype(F32)
        extra = jnp.where(sub16 == 0, top, jnp.where(sub16 == 1, curve - top, 0.0))
        for place in range(perts):
            out_ref[part * perts + place] = jnp.where(place == mine, value, extra).astype(BF16)


def owner_kernel(terms_ref, probe_ref, hessian_ref, curve_ref, *, parts, scale):
    perts = terms_ref.shape[0] // parts
    mine = lax.axis_index("pert")
    total = jnp.zeros(hessian_ref.shape, F32)
    every = jnp.zeros(hessian_ref.shape, F32)
    for part in range(parts):
        total = total + terms_ref[part * perts + mine].astype(F32)
        for place in range(perts):
            value = terms_ref[part * perts + place].astype(F32)
            every = every + jnp.where(place == mine, 0.0, value)
    hessian_ref[...] = total
    own = jnp.sum(total * probe_ref[...], axis=0, keepdims=True)
    curve_ref[...] = (own + every[0:1] + every[1:2]) * scale


def call(body, outs, spaces, scratch=(), name=None, flops=0, moved=1 << 20, limit=12, out_specs=None):
    return pl.pallas_call(
        body,
        out_shape=outs,
        in_specs=[{"s": SMEM, "v": VMEM, "h": HBM}[s] for s in spaces],
        out_specs=out_specs or jax.tree.map(lambda _: VMEM, outs),
        scratch_shapes=list(scratch),
        compiler_params=pltpu.CompilerParams(vmem_limit_bytes=limit * MIB),
        name=name,
        cost_estimate=pl.CostEstimate(flops=flops, transcendentals=0, bytes_accessed=moved),
    )


def shards(
    probes, melt_shape, obs_weight, diag_inverse, coupling, columns, send_list, patch_of_block
):
    pert = probes.shape[0]
    blocks = coupling.shape[0]
    capacity = send_list.shape[2]
    parts = lax.axis_size("dom")
    pairs = blocks // 2
    shape = jax.ShapeDtypeStruct
    msgs = [shape((capacity // 2, pert, LANES), BF16)] * 4
    pair_array = shape((pairs, pert, LANES), F32)
    block_array = shape((blocks, pert, LANES), BF16)
    ext = pltpu.VMEM((blocks + 4 * capacity, pert, LANES), BF16)
    accs = [pltpu.VMEM((blocks + 4 * capacity, pert, LANES), F32)] * 4
    held = pltpu.VMEM((pairs, pert, LANES), F32)
    melt = melt_shape.reshape(pairs, LANES)
    weight = obs_weight.reshape(pairs, LANES)
    patch = patch_of_block.reshape(1, blocks)

    perts = lax.axis_size("pert")
    columns = columns.T
    w, outgoing = call(
        functools.partial(melt_kernel, parts=parts),
        [shape((pairs, LANES), F32), shape((parts, pert + capacity + 8, LANES), F32)],
        "hhhhh",
        [
            pltpu.SMEM(send_list.shape, jnp.int32),
            pltpu.VMEM((pairs, LANES), F32),
            pltpu.VMEM((1, blocks), jnp.int32),
            pltpu.VMEM(probes.shape, F32),
            pltpu.VMEM((HALF, HALF, blocks), BF16),
            pltpu.SemaphoreType.DMA((5,)),
        ],
        name="melt",
        limit=60,
    )(send_list, melt, patch, probes, jnp.transpose(diag_inverse, (1, 2, 0)))
    got = lax.all_to_all(outgoing, "dom", 0, 0, tiled=True)
    wide = [shape((capacity // 2 + capacity // 4 + 1, pert, LANES), BF16)] * 4
    w, early = call(
        settle_kernel,
        [shape(w.shape, F32), shape((EARLY,) + coupling.shape[1:], BF16)],
        "hvh",
        [
            pltpu.VMEM((EARLY,) + coupling.shape[1:], BF16),
            pltpu.SemaphoreType.DMA,
            pltpu.SemaphoreType.DMA((2,)),
        ],
        name="settle",
        moved=4 << 20,
        limit=49,
    )(w, diag_inverse, coupling)
    m, v, names, patches, t1, state, *out = call(
        first_kernel,
        [
            shape(coupling.shape, BF16),
            shape((pairs, 8, LANES), F32),
            shape((8, LANES), F32),
            shape((8, LANES), F32),
            pair_array,
            block_array,
        ]
        + wide,
        "ssvvvvvhv",
        [
            ext,
            pltpu.VMEM((blocks + 4 * capacity, LANES), F32),
            pltpu.VMEM((blocks - EARLY,) + coupling.shape[1:], BF16),
            pltpu.SemaphoreType.DMA((6,)),
        ],
        name="first",
        limit=44,
    )(columns, send_list, patch, columns, got, w, diag_inverse, coupling, early)
    carried = [rotated(x, o) for x, o in zip(out, OFFSET_LIST)]
    state, *out = call(
        sweep_kernel, [block_array] + msgs, "ssvvvvvvv", [ext], name="sweep"
    )(columns, send_list, t1, state, *carried, m)
    ghosts = [rotated(v, o) for v, o in zip(out, OFFSET_LIST)]
    hot, *far = call(
        window_kernel,
        [shape((parts * LANES, 7 * LANES), BF16)]
        + [shape((capacity // 2 + 1, pert, LANES), BF16)] * 4,
        "ss" + "v" * 10,
        [pltpu.VMEM((blocks + 4 * capacity, 8, LANES), F32)],
        name="window",
        moved=4 << 20,
    )(columns, send_list, columns, patch, names, patches, *carried, v, m)
    far, ghosts = lax.optimization_barrier((far, ghosts))
    far = [rotated(x, o) for x, o in zip(far, OFFSET_LIST)]
    tangent, terms, z, y = call(
        turn_kernel,
        [
            shape((pert, blocks * HALF), F32),
            shape((pert, LANES), F32),
            shape((pairs + 2 * capacity, pert, LANES), BF16),
            shape((2 * capacity, pert, LANES), BF16),
        ],
        "s" + "v" * 9,
        [
            ext,
            pltpu.VMEM((pert, blocks * HALF), F32),
            held,
            held,
            pltpu.SemaphoreType.DMA,
        ]
        + accs,
        name="turn",
        moved=16 << 20,
        out_specs=[HBM, VMEM, VMEM, VMEM],
    )(columns, t1, state, *ghosts, m, weight, w)
    terms = call(
        last_kernel, shape((parts * perts, pert, LANES), BF16), "v" * 14, name="last"
    )(z, y, v, *carried, *far, hot, terms, got)
    terms = lax.all_to_all(terms, ("dom", "pert"), 0, 0, tiled=True)
    hessian_probe, curvature = call(
        functools.partial(owner_kernel, parts=parts, scale=1.0 / (pert * perts)),
        [shape(probes.shape, F32), shape((1, LANES), F32)],
        "vv",
        name="owner",
    )(terms, probes)
    return tangent, hessian_probe, curvature.reshape(-1)


def solution(mesh):
    in_specs = (
        P("pert", "dom"),
        P("dom"),
        P("dom"),
        P("dom", None, None),
        P("dom", None, None),
        P("dom", None),
        P("dom", None, None),
        P("dom"),
    )
    out_specs = (P("pert", "dom"), P("pert", "dom"), P("dom"))
    return jax.shard_map(shards, mesh=mesh, in_specs=in_specs, out_specs=out_specs, check_vma=False)
```

```python
import functools

import jax
import jax.numpy as jnp
from jax import lax
from jax.experimental import pallas as pl
from jax.experimental.pallas import tpu as pltpu
from jax.sharding import PartitionSpec as P

OFFSET_LIST = (-2, -1, 1, 2)
F32 = jnp.float32
BF16 = jnp.bfloat16
LANES = 128
HALF = 64
QUAD = 4
RADIX = 64
PITCH = 136

VMEM = pl.BlockSpec(memory_space=pltpu.VMEM)
SMEM = pl.BlockSpec(memory_space=pltpu.SMEM)
HBM = pl.BlockSpec(memory_space=pltpu.HBM)
MIB = 1024 * 1024


def low_half(shape):
    return lax.broadcasted_iota(jnp.int32, shape, len(shape) - 1) < HALF


def swap_halves(value):
    return pltpu.roll(value, HALF, 1)


def rotated(value, by):
    peers = lax.axis_size("dom")
    return lax.ppermute(value, "dom", [(i, (i + by) % peers) for i in range(peers)])


def neighbours(parts):
    me = lax.axis_index("dom")
    return [lax.rem(me - offset + parts, parts) for offset in OFFSET_LIST]


def melt_kernel(
    send_hbm, melt_hbm, patch_hbm, probe_hbm, diag_hbm, w_ref, out_ref,
    send_ref, melt_ref, patch_ref, probe_ref, diag_ref, sems, *, parts,
):
    copies = [
        pltpu.make_async_copy(source, target, sems.at[number])
        for number, (source, target) in enumerate(
            (
                (diag_hbm, diag_ref),
                (melt_hbm, melt_ref),
                (patch_hbm, patch_ref),
                (probe_hbm, probe_ref),
                (send_hbm, send_ref),
            )
        )
    ]
    for copy in copies:
        copy.start()
    for copy in copies:
        copy.wait()
    pairs = melt_ref.shape[0]
    pert = probe_ref.shape[0]
    capacity = send_ref.shape[2]
    low = low_half((1, LANES))
    lane = lax.broadcasted_iota(jnp.int32, (HALF, LANES), 1)
    turned = jnp.transpose(jnp.concatenate([melt_ref[...], jnp.zeros((LANES - pairs, LANES), F32)], axis=0))
    even = jnp.take_along_axis(turned[:HALF], lane // 2, axis=1)
    odd = jnp.take_along_axis(turned[HALF:], lane // 2, axis=1)
    melt = jnp.where(lane % 2 == 0, even, odd)
    sums = [
        jnp.sum(diag_ref[i].astype(F32) * melt, axis=0, keepdims=True)
        for i in range(diag_ref.shape[0])
    ]
    sums = jnp.concatenate(sums, axis=0)
    source = 2 * (lane % HALF)
    both = jnp.concatenate(
        [
            jnp.take_along_axis(sums, source, axis=1),
            jnp.take_along_axis(sums, source + 1, axis=1),
        ],
        axis=0,
    )
    w_ref[...] = jnp.transpose(both)[:pairs]
    patch_row = jnp.broadcast_to(patch_ref[...].astype(F32), (8, LANES))
    lane = lax.broadcasted_iota(jnp.int32, (8, LANES), 1)
    for part in range(parts):
        out_ref[part, :pert] = probe_ref[...]
    me = lax.axis_index("dom")
    for group, offset in enumerate(OFFSET_LIST):
        to = lax.rem(me + offset + parts, parts)
        ids = jnp.zeros((8, LANES), jnp.int32)
        for slot in range(capacity):
            block = jnp.maximum(send_ref[0, group, slot], 0)
            row = w_ref[pl.ds(block // 2, 1), :]
            out_ref[to, pert + slot : pert + slot + 1, :] = jnp.where(
                low == (block % 2 == 0), row, swap_halves(row)
            )
            ids = jnp.where(lane == group * capacity + slot, block, ids)
        mine = (lane >= group * capacity) & (lane < (group + 1) * capacity)
        out_ref[to, pert + capacity :, :] = jnp.where(
            mine, jnp.take_along_axis(patch_row, ids, axis=1), 0.0
        )


def gather_rows(quad, cols_ref, ext_ref, low):
    rows = []
    for place in range(QUAD):
        g = quad * QUAD + place
        tiles = [ext_ref[cols_ref[k, g]] for k in range(4)]
        rows.append(
            jnp.concatenate(
                [jnp.where(low, tiles[0], tiles[1]), jnp.where(low, tiles[2], tiles[3])], axis=1
            )
        )
    return rows


def coupled_rows(quad, rows, m_ref):
    rhs = m_ref[pl.ds(quad * QUAD, QUAD)].reshape(QUAD * HALF, 4 * HALF)
    return lax.dot_general(
        jnp.concatenate(rows, axis=0), rhs, (((1,), (1,)), ((), ())), preferred_element_type=F32
    )


def own_pairs(out, size, low):
    first = jnp.where(low, out[:size, :LANES], out[size : 2 * size, :LANES])
    second = jnp.where(low, out[2 * size : 3 * size, LANES:], out[3 * size : 4 * size, LANES:])
    return first, second


def gather_multiply(quad, cols_ref, ext_ref, m_ref, low):
    out = coupled_rows(quad, gather_rows(quad, cols_ref, ext_ref, low), m_ref)
    return own_pairs(out, out.shape[0] // QUAD, low)


def store_pair(ref, pair, value, low):
    value = value.astype(BF16)
    other = swap_halves(value.astype(F32)).astype(BF16)
    ref[2 * pair] = jnp.where(low, value, other)
    ref[2 * pair + 1] = jnp.where(low, other, value)


def fill_messages(send_ref, ref, msg_refs, low):
    for group, msg_ref in enumerate(msg_refs):
        for pair in range(send_ref.shape[2] // 2):
            even, odd = (
                ref[jnp.maximum(send_ref[0, group, 2 * pair + half], 0)] for half in range(2)
            )
            msg_ref[pair] = jnp.where(low, even, odd)


def patches_of_columns(columns_ref, ids):
    columns = jnp.concatenate([columns_ref[...], columns_ref[...]], axis=0)
    here = jnp.broadcast_to(ids[:, :LANES], columns.shape)
    there = jnp.broadcast_to(ids[:, LANES:], columns.shape)
    return jnp.where(
        columns < LANES,
        jnp.take_along_axis(here, jnp.minimum(columns, LANES - 1), axis=1),
        jnp.take_along_axis(there, jnp.maximum(columns - LANES, 0), axis=1),
    )


def first_kernel(
    cols_ref, send_ref, patch_ref, columns_ref, got_ref, w_hbm, diag_hbm, coupling_hbm,
    m_ref, v_ref, names_ref, patches_ref, t1_ref, t2_ref, o0, o1, o2, o3,
    ext_ref, row_ref, w_ref, coupling_ref, diag_ref, turned_ref, w_sem, diag_sem, sems,
):
    w_copy = pltpu.make_async_copy(w_hbm, w_ref, w_sem)
    w_copy.start()
    diag_copy = pltpu.make_async_copy(diag_hbm, diag_ref, diag_sem)
    diag_copy.start()
    chunks = sems.shape[0]
    size = m_ref.shape[0] // chunks
    copies = [
        pltpu.make_async_copy(
            coupling_hbm.at[chunk * size : (chunk + 1) * size],
            coupling_ref.at[chunk * size : (chunk + 1) * size],
            sems.at[chunk],
        )
        for chunk in range(chunks)
    ]
    for copy in copies:
        copy.start()
    pert = t1_ref.shape[1]
    capacity = send_ref.shape[2]
    blocks = cols_ref.shape[1]
    parts = got_ref.shape[0]
    sources = neighbours(parts)
    low = low_half((pert, LANES))
    lane = lax.broadcasted_iota(jnp.int32, (1, LANES), 1)
    ghost_ids = sum(got_ref[source, pert + capacity : pert + capacity + 1, :] for source in sources)
    ghost_ids = jnp.where(lane < 4 * capacity, ghost_ids, -1.0)
    ids = jnp.concatenate([patch_ref[...].astype(F32), ghost_ids], axis=1)
    total = jnp.zeros((3 * pert, 2 * LANES), F32)
    for part in range(parts):
        names = (
            lax.broadcasted_iota(jnp.int32, (LANES, 2 * LANES), 0) + part * LANES
        ).astype(F32)
        hot = jnp.where(names == ids, 1.0, 0.0).astype(BF16)
        value = got_ref[part, :pert]
        top = value.astype(BF16)
        rest = value - top.astype(F32)
        mid = rest.astype(BF16)
        last = (rest - mid.astype(F32)).astype(BF16)
        total = total + jnp.dot(
            jnp.concatenate([top, mid, last], axis=0), hot, preferred_element_type=F32
        )
    picked = total[:pert] + total[pert : 2 * pert] + total[2 * pert :]
    local_picked = picked[:, :LANES]
    ghost_picked = picked[:, LANES:]
    full_low = low.astype(jnp.int32)
    column_patches = patches_of_columns(columns_ref, ids)
    patches_ref[...] = column_patches
    sub = lax.broadcasted_iota(jnp.int32, (8, LANES), 0)
    lane8 = lax.broadcasted_iota(jnp.int32, (8, LANES), 1)
    wanted = sub == lane8 % 4

    def listed(blocks_of_lanes):
        taken = jnp.take_along_axis(column_patches, blocks_of_lanes, axis=1)
        return jnp.sum(jnp.where(wanted, taken, 0.0), axis=0, keepdims=True)

    for tile in range(4 * blocks // LANES):
        names_ref[tile : tile + 1, :] = listed(tile * (LANES // 4) + lane8 // 4)
    w_copy.wait()
    w = w_ref[...]
    w_other = swap_halves(w)
    low_w = low_half(w.shape)
    row_ref[pl.ds(0, blocks // 2, stride=2), :] = jnp.where(low_w, w, w_other)
    row_ref[pl.ds(1, blocks // 2, stride=2), :] = jnp.where(low_w, w_other, w)
    for group, source in enumerate(sources):
        start = blocks + group * capacity
        row_ref[start : start + capacity, :] = got_ref[source, pert : pert + capacity, :]

    def seed(pair, _):
        index = 2 * pair + 1 - full_low
        spread = jnp.take_along_axis(local_picked, index, axis=1)
        value = spread * w_ref[pl.ds(pair, 1), :]
        t1_ref[pair] = value
        store_pair(ext_ref, pair, value, low)
        return 0

    lax.fori_loop(0, blocks // 2, seed, 0, unroll=16)
    for group, source in enumerate(sources):
        for slot in range(capacity):
            place = group * capacity + slot
            row = got_ref[source, pert + slot : pert + slot + 1, :]
            spread = jnp.broadcast_to(ghost_picked[:, place : place + 1], (pert, LANES))
            ext_ref[blocks + place] = (spread * row).astype(BF16)

    diag_copy.wait()
    for i in range(HALF // 2):
        both = jnp.concatenate(
            [diag_ref[i].astype(F32), diag_ref[i + HALF // 2].astype(F32)], axis=0
        )
        turned_ref[i * PITCH : i * PITCH + LANES, :] = jnp.transpose(both)
    for chunk, copy in enumerate(copies):
        copy.wait()
        for block in range(chunk * size, (chunk + 1) * size):
            rows = turned_ref[pl.ds(block, HALF // 2, stride=PITCH), :]
            diag = jnp.concatenate([rows, swap_halves(rows)], axis=0)[:, :HALF]
            m_ref[block] = jnp.dot(
                diag.astype(BF16), coupling_ref[block], preferred_element_type=F32
            ).astype(BF16)

    low8 = low_half((8, LANES))
    masks = [(sub % 4 == k) & (low8 if k % 2 == 0 else ~low8) for k in range(4)]
    nothing = jnp.zeros((8, LANES), F32)

    def sweep(quad, _):
        rows = gather_rows(quad, cols_ref, ext_ref, low)
        tiles = ([], [])
        for place in range(QUAD):
            w_rows = [row_ref[pl.ds(cols_ref[k, quad * QUAD + place], 1), :] for k in range(4)]
            for side in range(2):
                tiles[side].append(
                    jnp.where(
                        masks[2 * side],
                        w_rows[2 * side],
                        jnp.where(masks[2 * side + 1], w_rows[2 * side + 1], nothing),
                    )
                )
        extra = jnp.concatenate([jnp.concatenate(side, axis=0) for side in tiles], axis=1)
        out = coupled_rows(quad, rows + [extra.astype(BF16)], m_ref)
        for place, value in enumerate(own_pairs(out, pert, low)):
            pair = 2 * quad + place
            store_pair(t2_ref, pair, t1_ref[pair] - value, low)
        for place, value in enumerate(own_pairs(out[QUAD * pert :], 8, low8)):
            v_ref[2 * quad + place] = value
        return 0

    lax.fori_loop(0, blocks // QUAD, sweep, 0, unroll=32)
    msgs = (o0, o1, o2, o3)
    fill_messages(send_ref, t2_ref, msgs, low)
    half = capacity // 2
    for group, ref in enumerate(msgs):
        places = jnp.zeros((8, LANES), jnp.int32)
        values = []
        for slot in range(capacity):
            block = jnp.maximum(send_ref[0, group, slot], 0)
            value = v_ref[block // 2]
            right = (slot - block) % 2 == 0
            values.append(jnp.where(right, value, swap_halves(value)))
            places = jnp.where(lane8 // 4 == slot, block, places)
        pairs = [
            jnp.where(low8, values[2 * pair], values[2 * pair + 1]) for pair in range(half)
        ]
        for tile in range(half // 2):
            ref[half + tile] = jnp.concatenate(pairs[2 * tile : 2 * tile + 2], axis=0).astype(BF16)
        patch = listed(places).astype(jnp.int32)
        ref[half + half // 2] = jnp.concatenate(
            [
                jnp.broadcast_to(patch // RADIX, (8, LANES)),
                jnp.broadcast_to(patch % RADIX, (8, LANES)),
            ],
            axis=0,
        ).astype(F32).astype(BF16)


def extend(ext_ref, local_ref, ghosts, low):
    blocks = local_ref.shape[0]
    count = (ext_ref.shape[0] - blocks) // 2 // len(ghosts)
    ext_ref[:blocks] = local_ref[...]
    for group, ref in enumerate(ghosts):
        for pair in range(count):
            store_pair(ext_ref, blocks // 2 + group * count + pair, ref[pair], low)


def sweep_kernel(
    cols_ref, send_ref, t1_ref, prev_ref, g0, g1, g2, g3, m_ref,
    next_ref, o0, o1, o2, o3, ext_ref,
):
    low = low_half(prev_ref.shape[1:])
    extend(ext_ref, prev_ref, (g0, g1, g2, g3), low)

    def sweep(quad, _):
        first, second = gather_multiply(quad, cols_ref, ext_ref, m_ref, low)
        store_pair(next_ref, 2 * quad, t1_ref[2 * quad] - first, low)
        store_pair(next_ref, 2 * quad + 1, t1_ref[2 * quad + 1] - second, low)
        return 0

    lax.fori_loop(0, cols_ref.shape[1] // QUAD, sweep, 0, unroll=32)
    fill_messages(send_ref, next_ref, (o0, o1, o2, o3), low)


def zero_rows(acc_refs, places):
    for ref in acc_refs:
        for place in places:
            ref[place] = jnp.zeros(ref.shape[1:], F32)


def multiply_scatter(quad, cols_ref, pairs, m_ref, acc_refs, low):
    zero = jnp.zeros(pairs[0].shape, F32)
    rows = []
    for place in range(QUAD):
        value = pairs[place // 2]
        kept = jnp.where(low, value, zero) if place % 2 == 0 else jnp.where(low, zero, value)
        tiles = [kept, zero] if place < 2 else [zero, kept]
        rows.append(jnp.concatenate(tiles, axis=1))
    lhs = jnp.concatenate(rows, axis=0).astype(BF16)
    rhs = m_ref[pl.ds(quad * QUAD, QUAD)].reshape(QUAD * HALF, 4 * HALF)
    out = jnp.dot(lhs, rhs, preferred_element_type=F32)
    p = pairs[0].shape[0]
    for place in range(QUAD):
        g = quad * QUAD + place
        for k in range(4):
            column = cols_ref[k, g]
            piece = out[place * p : (place + 1) * p, (k // 2) * LANES : (k // 2 + 1) * LANES]
            acc_refs[k][column] = acc_refs[k][column] + piece


def half_sums(acc_refs, place, low):
    return jnp.where(
        low, acc_refs[0][place] + acc_refs[2][place], acc_refs[1][place] + acc_refs[3][place]
    )


def pair_sum(acc_refs, pair, low):
    even = half_sums(acc_refs, 2 * pair, low)
    odd = half_sums(acc_refs, 2 * pair + 1, low)
    return jnp.where(low, even, odd) + swap_halves(jnp.where(low, odd, even))


def turn_kernel(
    cols_ref, t1_ref, prev_ref, g0, g1, g2, g3, m_ref, weight_ref, w_ref,
    tangent_hbm, terms_ref, z_ref, y_ref,
    ext_ref, tangent_ref, target_ref, u_ref, sem, *acc_refs,
):
    pert = prev_ref.shape[1]
    low = low_half(prev_ref.shape[1:])
    lane = lax.broadcasted_iota(jnp.int32, (pert, LANES), 1)
    blocks = cols_ref.shape[1]
    extend(ext_ref, prev_ref, (g0, g1, g2, g3), low)

    share = acc_refs[0].shape[0] // (blocks // QUAD)

    def sweep(quad, terms):
        zero_rows(acc_refs, [share * quad + i for i in range(share)])
        coupled = gather_multiply(quad, cols_ref, ext_ref, m_ref, low)
        for place in range(2):
            pair = 2 * quad + place
            value = t1_ref[pair] - coupled[place]
            start = pl.multiple_of(pair * LANES, LANES)
            tangent_ref[:, pl.ds(start, LANES)] = value
            target = value * weight_ref[pl.ds(pair, 1), :]
            target_ref[pair] = target
            product = target * w_ref[pl.ds(pair, 1), :]
            even = jnp.sum(jnp.where(low, product, 0.0), axis=1, keepdims=True)
            odd = jnp.sum(jnp.where(low, 0.0, product), axis=1, keepdims=True)
            terms = jnp.where(
                lane == 2 * pair, even, jnp.where(lane == 2 * pair + 1, odd, terms)
            )
        return terms

    terms_ref[...] = lax.fori_loop(
        0, blocks // QUAD, sweep, jnp.zeros((pert, LANES), F32), unroll=32
    )
    tangent_copy = pltpu.make_async_copy(tangent_ref, tangent_hbm, sem)
    tangent_copy.start()
    scatter_all(cols_ref, target_ref, m_ref, acc_refs, low)

    def own(pair, _):
        u_ref[pair] = target_ref[pair] - pair_sum(acc_refs, pair, low)
        zero_rows(acc_refs, (2 * pair, 2 * pair + 1))
        return 0

    lax.fori_loop(0, blocks // 2, own, 0, unroll=16)
    for pair in range(y_ref.shape[0]):
        y_ref[pair] = (-pair_sum(acc_refs, blocks // 2 + pair, low)).astype(BF16)
        zero_rows(acc_refs, (blocks + 2 * pair, blocks + 2 * pair + 1))
    scatter_all(cols_ref, u_ref, m_ref, acc_refs, low)

    def second(pair, _):
        z_ref[pair] = (pair_sum(acc_refs, pair, low) - target_ref[pair]).astype(BF16)
        return 0

    lax.fori_loop(0, blocks // 2, second, 0, unroll=16)
    for pair in range(blocks // 2, z_ref.shape[0]):
        z_ref[pair] = pair_sum(acc_refs, pair, low).astype(BF16)
    tangent_copy.wait()


def scatter_all(cols_ref, u_ref, m_ref, acc_refs, low):
    def sweep(quad, _):
        pairs = [u_ref[2 * quad], u_ref[2 * quad + 1]]
        multiply_scatter(quad, cols_ref, pairs, m_ref, acc_refs, low)
        return 0

    lax.fori_loop(0, cols_ref.shape[1] // QUAD, sweep, 0, unroll=32)


def write_hot(hot_ref, rows, part):
    start = pl.multiple_of(part * LANES, LANES)
    names = lax.broadcasted_iota(jnp.int32, (LANES, LANES), 0) + part * LANES
    names = names.astype(F32)
    for tile, row in enumerate(rows):
        hot_ref[pl.ds(start, LANES), tile * LANES : (tile + 1) * LANES] = jnp.where(
            names == row, 1.0, 0.0
        ).astype(BF16)


def window_kernel(
    cols_ref, send_ref, columns_ref, patch_ref, names_ref, patches_ref, g0, g1, g2, g3,
    v_ref, m_ref, hot_ref, o0, o1, o2, o3, vector_ref,
):
    ghosts = (g0, g1, g2, g3)
    capacity = send_ref.shape[2]
    half = capacity // 2
    blocks = cols_ref.shape[1]
    low8 = low_half((8, LANES))
    sub = lax.broadcasted_iota(jnp.int32, (8, LANES), 0)
    lane = lax.broadcasted_iota(jnp.int32, (8, LANES), 1)

    listed = []
    there = jnp.zeros((8, LANES), F32)
    for group, ref in enumerate(ghosts):
        digits = ref[ref.shape[0] - 1].astype(F32)
        listed.append(digits[0:1] * RADIX + digits[8:9])
        taken = jnp.take_along_axis(
            jnp.broadcast_to(listed[-1], (8, LANES)), (lane % capacity) * 4 + sub % 4, axis=1
        )
        there = jnp.where(lane // capacity == group, taken, there)
    here = patches_ref[...]
    rows = [patch_ref[...].astype(F32)] + [names_ref[tile : tile + 1] for tile in range(4)]
    for tile in range(2):
        rows.append(
            jnp.where(low8[:1], listed[2 * tile], swap_halves(listed[2 * tile + 1]))
        )

    def spread(pair, value):
        other = swap_halves(value)
        vector_ref[2 * pair] = jnp.where(low8, value, other)
        vector_ref[2 * pair + 1] = jnp.where(low8, other, value)

    for pair in range(blocks // 2):
        spread(pair, v_ref[pair])
    for group, ref in enumerate(ghosts):
        for tile in range(half // 2):
            both = ref[half + tile].astype(F32)
            for side in range(2):
                pair = blocks // 2 + group * half + 2 * tile + side
                spread(pair, both[8 * side : 8 * side + 8])

    own = (sub < 4) == low8
    nothing = jnp.zeros((8, LANES), F32)
    low = low_half((16, LANES))
    columns = jnp.concatenate([columns_ref[...], columns_ref[...]], axis=0)
    sub16 = lax.broadcasted_iota(jnp.int32, (16, LANES), 0)
    for group, ref in enumerate((o0, o1, o2, o3)):
        slots = [jnp.maximum(send_ref[0, group, slot], 0) for slot in range(capacity)]
        for four in range(capacity // QUAD):
            lhs = []
            rhs = []
            for block in slots[four * QUAD : (four + 1) * QUAD]:
                a0, a1, a2, a3 = (vector_ref[cols_ref[k, block]] for k in range(4))
                left = jnp.where(own, jnp.where(sub < 4, a0, a1), nothing)
                right = jnp.where(own, jnp.where(sub < 4, a2, a3), nothing)
                lhs.append(
                    jnp.concatenate(
                        [
                            jnp.concatenate([left, nothing], axis=0),
                            jnp.concatenate([nothing, right], axis=0),
                        ],
                        axis=1,
                    ).astype(BF16)
                )
                rhs.append(m_ref[block])
            out = lax.dot_general(
                jnp.concatenate(lhs, axis=0),
                jnp.concatenate(rhs, axis=0),
                (((1,), (1,)), ((), ())),
                preferred_element_type=F32,
            )
            for side, value in enumerate(own_pairs(out, 16, low)):
                ref[2 * four + side] = value.astype(BF16)
        digits = jnp.zeros((16, LANES), F32)
        for tile in range(2):
            places = jnp.zeros((8, LANES), jnp.int32)
            for slot in range(half):
                places = jnp.where(lane // 16 == slot, slots[tile * half + slot], places)
            taken = jnp.take_along_axis(columns, places, axis=1).astype(F32)
            mine = jnp.sum(
                jnp.where(sub == (lane % 16) // 4, taken, 0.0), axis=0, keepdims=True
            )
            mine = jnp.broadcast_to(mine, (8, LANES)).astype(jnp.int32)
            taken = jnp.where(
                mine < LANES,
                jnp.take_along_axis(here, jnp.minimum(mine, LANES - 1), axis=1),
                jnp.take_along_axis(there, jnp.maximum(mine - LANES, 0), axis=1),
            )
            patch = jnp.sum(jnp.where(sub == lane % 4, taken, 0.0), axis=0, keepdims=True)
            patch = patch.astype(jnp.int32)
            digits = jnp.where(
                sub16 == 2 * tile,
                (patch // RADIX).astype(F32),
                jnp.where(sub16 == 2 * tile + 1, (patch % RADIX).astype(F32), digits),
            )
        ref[half] = digits.astype(BF16)

    def one(part, _):
        write_hot(hot_ref, rows, part)
        return 0

    lax.fori_loop(0, hot_ref.shape[0] // LANES, one, 0, unroll=2)


def last_kernel(
    z_ref, y_ref, v_ref, v0, v1, v2, v3, x0, x1, x2, x3,
    hot_ref, terms_ref, got_ref, out_ref,
):
    pert = z_ref.shape[1]
    local_pairs = v_ref.shape[0]
    half = (z_ref.shape[0] - local_pairs) // 4
    parts = got_ref.shape[0]
    low8 = low_half((8, LANES))
    low = low_half((16, LANES))
    sub = lax.broadcasted_iota(jnp.int32, (8, LANES), 0)
    own = (sub < 4) == low8
    nothing = jnp.zeros((8, LANES), F32)
    zero = jnp.zeros((16, LANES), F32)

    def wide(left, right):
        return jnp.concatenate([left, right], axis=1)

    def product(lhs, rhs):
        return lax.dot_general(
            lhs, rhs.astype(BF16), (((1,), (1,)), ((), ())), preferred_element_type=F32
        )

    def first_level(first, second):
        return jnp.concatenate(
            [
                wide(jnp.where(own, first, nothing), nothing),
                wide(nothing, jnp.where(own, second, nothing)),
            ],
            axis=0,
        )

    def second_level(first, second):
        return jnp.concatenate(
            [
                wide(jnp.where(low, first, zero), zero),
                wide(jnp.where(low, zero, first), zero),
                wide(zero, jnp.where(low, second, zero)),
                wide(zero, jnp.where(low, zero, second)),
            ],
            axis=0,
        )

    pieces = [terms_ref[...]]
    for pair in range(0, local_pairs, 2):
        lhs = wide(z_ref[pair], z_ref[pair + 1])
        pieces.append(product(lhs, first_level(v_ref[pair], v_ref[pair + 1])))
    for group, ref in enumerate((v0, v1, v2, v3)):
        for tile in range(half // 2):
            both = ref[half + tile].astype(F32)
            pair = local_pairs + group * half + 2 * tile
            lhs = wide(z_ref[pair], z_ref[pair + 1])
            pieces.append(product(lhs, first_level(both[:8], both[8:])))
    rows = []
    for group, ref in enumerate((x0, x1, x2, x3)):
        for tile in range(half // 2):
            pair = group * half + 2 * tile
            lhs = wide(y_ref[pair], y_ref[pair + 1])
            first, second = (ref[2 * tile + side].astype(F32) for side in range(2))
            pieces.append(product(lhs, second_level(first, second)))
        digits = ref[half].astype(F32)
        for tile in range(2):
            rows.append(
                digits[2 * tile : 2 * tile + 1] * RADIX + digits[2 * tile + 1 : 2 * tile + 2]
            )
    terms = jnp.concatenate(pieces, axis=1)
    top = terms.astype(BF16)
    rest = (terms - top.astype(F32)).astype(BF16)
    both = jnp.concatenate([top, rest], axis=0)
    mine = lax.axis_index("pert")
    sub16 = lax.broadcasted_iota(jnp.int32, (pert, LANES), 0)
    perts = out_ref.shape[0] // parts
    first_names = lax.broadcasted_iota(jnp.int32, (LANES, LANES), 0).astype(F32)
    for part in range(parts):
        hot = jnp.concatenate(
            [hot_ref[part * LANES : (part + 1) * LANES, :]]
            + [
                jnp.where(first_names == row - part * LANES, 1.0, 0.0).astype(BF16)
                for row in rows
            ],
            axis=1,
        )
        out = lax.dot_general(both, hot, (((1,), (1,)), ((), ())), preferred_element_type=F32)
        value = out[:pert] + out[pert:]
        curve = jnp.sum(value * got_ref[part, :pert], axis=0, keepdims=True)
        top = curve.astype(BF16).astype(F32)
        extra = jnp.where(sub16 == 0, top, jnp.where(sub16 == 1, curve - top, 0.0))
        for place in range(perts):
            out_ref[part * perts + place] = jnp.where(place == mine, value, extra).astype(BF16)


def owner_kernel(terms_ref, probe_ref, hessian_ref, curve_ref, *, parts, scale):
    perts = terms_ref.shape[0] // parts
    mine = lax.axis_index("pert")
    total = jnp.zeros(hessian_ref.shape, F32)
    every = jnp.zeros(hessian_ref.shape, F32)
    for part in range(parts):
        total = total + terms_ref[part * perts + mine].astype(F32)
        for place in range(perts):
            value = terms_ref[part * perts + place].astype(F32)
            every = every + jnp.where(place == mine, 0.0, value)
    hessian_ref[...] = total
    own = jnp.sum(total * probe_ref[...], axis=0, keepdims=True)
    curve_ref[...] = (own + every[0:1] + every[1:2]) * scale


def call(body, outs, spaces, scratch=(), name=None, flops=0, moved=1 << 20, limit=12, out_specs=None):
    return pl.pallas_call(
        body,
        out_shape=outs,
        in_specs=[{"s": SMEM, "v": VMEM, "h": HBM}[s] for s in spaces],
        out_specs=out_specs or jax.tree.map(lambda _: VMEM, outs),
        scratch_shapes=list(scratch),
        compiler_params=pltpu.CompilerParams(vmem_limit_bytes=limit * MIB),
        name=name,
        cost_estimate=pl.CostEstimate(flops=flops, transcendentals=0, bytes_accessed=moved),
    )


def shards(
    probes, melt_shape, obs_weight, diag_inverse, coupling, columns, send_list, patch_of_block
):
    pert = probes.shape[0]
    blocks = coupling.shape[0]
    capacity = send_list.shape[2]
    parts = lax.axis_size("dom")
    pairs = blocks // 2
    shape = jax.ShapeDtypeStruct
    msgs = [shape((capacity // 2, pert, LANES), BF16)] * 4
    pair_array = shape((pairs, pert, LANES), F32)
    block_array = shape((blocks, pert, LANES), BF16)
    ext = pltpu.VMEM((blocks + 4 * capacity, pert, LANES), BF16)
    accs = [pltpu.VMEM((blocks + 4 * capacity, pert, LANES), F32)] * 4
    held = pltpu.VMEM((pairs, pert, LANES), F32)
    melt = melt_shape.reshape(pairs, LANES)
    weight = obs_weight.reshape(pairs, LANES)
    patch = patch_of_block.reshape(1, blocks)

    perts = lax.axis_size("pert")
    columns = columns.T
    diag_turned = jnp.transpose(diag_inverse, (1, 2, 0))
    w, outgoing = call(
        functools.partial(melt_kernel, parts=parts),
        [shape((pairs, LANES), F32), shape((parts, pert + capacity + 8, LANES), F32)],
        "hhhhh",
        [
            pltpu.SMEM(send_list.shape, jnp.int32),
            pltpu.VMEM((pairs, LANES), F32),
            pltpu.VMEM((1, blocks), jnp.int32),
            pltpu.VMEM(probes.shape, F32),
            pltpu.VMEM((HALF, HALF, blocks), BF16),
            pltpu.SemaphoreType.DMA((5,)),
        ],
        name="melt",
        limit=60,
    )(send_list, melt, patch, probes, diag_turned)
    got = lax.all_to_all(outgoing, "dom", 0, 0, tiled=True)
    wide = [shape((capacity // 2 + capacity // 4 + 1, pert, LANES), BF16)] * 4
    m, v, names, patches, t1, state, *out = call(
        first_kernel,
        [
            shape(coupling.shape, BF16),
            shape((pairs, 8, LANES), F32),
            shape((8, LANES), F32),
            shape((8, LANES), F32),
            pair_array,
            block_array,
        ]
        + wide,
        "ssvvvhhh",
        [
            ext,
            pltpu.VMEM((blocks + 4 * capacity, LANES), F32),
            pltpu.VMEM((pairs, LANES), F32),
            pltpu.VMEM(coupling.shape, BF16),
            pltpu.VMEM((HALF, HALF, blocks), BF16),
            pltpu.VMEM((HALF // 2 * PITCH, LANES), F32),
            pltpu.SemaphoreType.DMA,
            pltpu.SemaphoreType.DMA,
            pltpu.SemaphoreType.DMA((8,)),
        ],
        name="first",
        limit=46,
    )(columns, send_list, patch, columns, got, w, diag_turned, coupling)
    carried = [rotated(x, o) for x, o in zip(out, OFFSET_LIST)]
    state, *out = call(
        sweep_kernel, [block_array] + msgs, "ssvvvvvvv", [ext], name="sweep"
    )(columns, send_list, t1, state, *carried, m)
    ghosts = [rotated(v, o) for v, o in zip(out, OFFSET_LIST)]
    hot, *far = call(
        window_kernel,
        [shape((parts * LANES, 7 * LANES), BF16)]
        + [shape((capacity // 2 + 1, pert, LANES), BF16)] * 4,
        "ss" + "v" * 10,
        [pltpu.VMEM((blocks + 4 * capacity, 8, LANES), F32)],
        name="window",
        moved=4 << 20,
    )(columns, send_list, columns, patch, names, patches, *carried, v, m)
    far, ghosts = lax.optimization_barrier((far, ghosts))
    far = [rotated(x, o) for x, o in zip(far, OFFSET_LIST)]
    tangent, terms, z, y = call(
        turn_kernel,
        [
            shape((pert, blocks * HALF), F32),
            shape((pert, LANES), F32),
            shape((pairs + 2 * capacity, pert, LANES), BF16),
            shape((2 * capacity, pert, LANES), BF16),
        ],
        "s" + "v" * 9,
        [
            ext,
            pltpu.VMEM((pert, blocks * HALF), F32),
            held,
            held,
            pltpu.SemaphoreType.DMA,
        ]
        + accs,
        name="turn",
        moved=16 << 20,
        out_specs=[HBM, VMEM, VMEM, VMEM],
    )(columns, t1, state, *ghosts, m, weight, w)
    terms = call(
        last_kernel, shape((parts * perts, pert, LANES), BF16), "v" * 14, name="last"
    )(z, y, v, *carried, *far, hot, terms, got)
    terms = lax.all_to_all(terms, ("dom", "pert"), 0, 0, tiled=True)
    hessian_probe, curvature = call(
        functools.partial(owner_kernel, parts=parts, scale=1.0 / (pert * perts)),
        [shape(probes.shape, F32), shape((1, LANES), F32)],
        "vv",
        name="owner",
    )(terms, probes)
    return tangent, hessian_probe, curvature.reshape(-1)


def solution(mesh):
    in_specs = (
        P("pert", "dom"),
        P("dom"),
        P("dom"),
        P("dom", None, None),
        P("dom", None, None),
        P("dom", None),
        P("dom", None, None),
        P("dom"),
    )
    out_specs = (P("pert", "dom"), P("pert", "dom"), P("dom"))
    return jax.shard_map(shards, mesh=mesh, in_specs=in_specs, out_specs=out_specs, check_vma=False)
```

```python
import functools

import jax
import jax.numpy as jnp
from jax import lax
from jax.experimental import pallas as pl
from jax.experimental.pallas import tpu as pltpu
from jax.sharding import PartitionSpec as P

OFFSET_LIST = (-2, -1, 1, 2)
F32 = jnp.float32
BF16 = jnp.bfloat16
LANES = 128
HALF = 64
QUAD = 4
RADIX = 64
W_ROWS = 24576

VMEM = pl.BlockSpec(memory_space=pltpu.VMEM)
SMEM = pl.BlockSpec(memory_space=pltpu.SMEM)
HBM = pl.BlockSpec(memory_space=pltpu.HBM)
MIB = 1024 * 1024


def low_half(shape):
    return lax.broadcasted_iota(jnp.int32, shape, len(shape) - 1) < HALF


def swap_halves(value):
    return pltpu.roll(value, HALF, 1)


def rotated(value, by):
    peers = lax.axis_size("dom")
    return lax.ppermute(value, "dom", [(i, (i + by) % peers) for i in range(peers)])


def neighbours(parts):
    me = lax.axis_index("dom")
    return [lax.rem(me - offset + parts, parts) for offset in OFFSET_LIST]


def melt_kernel(
    send_hbm, melt_hbm, patch_hbm, probe_hbm, diag_hbm, w_hbm, out_ref,
    send_ref, melt_ref, patch_ref, probe_ref, diag_ref, w_ref, sems, w_sem, *, parts,
):
    copies = [
        pltpu.make_async_copy(source, target, sems.at[number])
        for number, (source, target) in enumerate(
            (
                (diag_hbm, diag_ref),
                (melt_hbm, melt_ref),
                (patch_hbm, patch_ref),
                (probe_hbm, probe_ref),
                (send_hbm, send_ref),
            )
        )
    ]
    for copy in copies:
        copy.start()
    for copy in copies:
        copy.wait()
    pairs = melt_ref.shape[0]
    pert = probe_ref.shape[0]
    capacity = send_ref.shape[2]
    low = low_half((1, LANES))
    lane = lax.broadcasted_iota(jnp.int32, (HALF, LANES), 1)
    turned = jnp.transpose(jnp.concatenate([melt_ref[...], jnp.zeros((LANES - pairs, LANES), F32)], axis=0))
    even = jnp.take_along_axis(turned[:HALF], lane // 2, axis=1)
    odd = jnp.take_along_axis(turned[HALF:], lane // 2, axis=1)
    melt = jnp.where(lane % 2 == 0, even, odd)
    sums = [
        jnp.sum(diag_ref[i].astype(F32) * melt, axis=0, keepdims=True)
        for i in range(diag_ref.shape[0])
    ]
    sums = jnp.concatenate(sums, axis=0)
    source = 2 * (lane % HALF)
    both = jnp.concatenate(
        [
            jnp.take_along_axis(sums, source, axis=1),
            jnp.take_along_axis(sums, source + 1, axis=1),
        ],
        axis=0,
    )
    w_ref[...] = jnp.transpose(both)[:pairs]
    w_copy = pltpu.make_async_copy(w_ref, w_hbm.at[pl.ds(0, pairs)], w_sem)
    w_copy.start()
    patch_row = jnp.broadcast_to(patch_ref[...].astype(F32), (8, LANES))
    lane = lax.broadcasted_iota(jnp.int32, (8, LANES), 1)
    for part in range(parts):
        out_ref[part, :pert] = probe_ref[...]
    me = lax.axis_index("dom")
    for group, offset in enumerate(OFFSET_LIST):
        to = lax.rem(me + offset + parts, parts)
        ids = jnp.zeros((8, LANES), jnp.int32)
        for slot in range(capacity):
            block = jnp.maximum(send_ref[0, group, slot], 0)
            row = w_ref[pl.ds(block // 2, 1), :]
            out_ref[to, pert + slot : pert + slot + 1, :] = jnp.where(
                low == (block % 2 == 0), row, swap_halves(row)
            )
            ids = jnp.where(lane == group * capacity + slot, block, ids)
        mine = (lane >= group * capacity) & (lane < (group + 1) * capacity)
        out_ref[to, pert + capacity :, :] = jnp.where(
            mine, jnp.take_along_axis(patch_row, ids, axis=1), 0.0
        )
    w_copy.wait()


def gather_rows(quad, cols_ref, ext_ref, low):
    rows = []
    for place in range(QUAD):
        g = quad * QUAD + place
        tiles = [ext_ref[cols_ref[k, g]] for k in range(4)]
        rows.append(
            jnp.concatenate(
                [jnp.where(low, tiles[0], tiles[1]), jnp.where(low, tiles[2], tiles[3])], axis=1
            )
        )
    return rows


def coupled_rows(quad, rows, m_ref):
    rhs = m_ref[pl.ds(quad * QUAD, QUAD)].reshape(QUAD * HALF, 4 * HALF)
    return lax.dot_general(
        jnp.concatenate(rows, axis=0), rhs, (((1,), (1,)), ((), ())), preferred_element_type=F32
    )


def own_pairs(out, size, low):
    first = jnp.where(low, out[:size, :LANES], out[size : 2 * size, :LANES])
    second = jnp.where(low, out[2 * size : 3 * size, LANES:], out[3 * size : 4 * size, LANES:])
    return first, second


def gather_multiply(quad, cols_ref, ext_ref, m_ref, low):
    out = coupled_rows(quad, gather_rows(quad, cols_ref, ext_ref, low), m_ref)
    return own_pairs(out, out.shape[0] // QUAD, low)


def store_pair(ref, pair, value, low):
    value = value.astype(BF16)
    other = swap_halves(value.astype(F32)).astype(BF16)
    ref[2 * pair] = jnp.where(low, value, other)
    ref[2 * pair + 1] = jnp.where(low, other, value)


def fill_messages(send_ref, ref, msg_refs, low):
    for group, msg_ref in enumerate(msg_refs):
        for pair in range(send_ref.shape[2] // 2):
            even, odd = (
                ref[jnp.maximum(send_ref[0, group, 2 * pair + half], 0)] for half in range(2)
            )
            msg_ref[pair] = jnp.where(low, even, odd)


def patches_of_columns(columns_ref, ids):
    columns = jnp.concatenate([columns_ref[...], columns_ref[...]], axis=0)
    here = jnp.broadcast_to(ids[:, :LANES], columns.shape)
    there = jnp.broadcast_to(ids[:, LANES:], columns.shape)
    return jnp.where(
        columns < LANES,
        jnp.take_along_axis(here, jnp.minimum(columns, LANES - 1), axis=1),
        jnp.take_along_axis(there, jnp.maximum(columns - LANES, 0), axis=1),
    )


def first_kernel(
    cols_ref, send_ref, patch_ref, columns_ref, got_ref, w_hbm, diag_ref, coupling_hbm,
    m_ref, w_ref, v_ref, names_ref, patches_ref, t1_ref, t2_ref, o0, o1, o2, o3,
    ext_ref, row_ref, coupling_ref, w_sem, sems,
):
    w_copy = pltpu.make_async_copy(w_hbm.at[pl.ds(0, w_ref.shape[0])], w_ref, w_sem)
    w_copy.start()
    chunks = sems.shape[0]
    size = diag_ref.shape[0] // chunks
    copies = [
        pltpu.make_async_copy(
            coupling_hbm.at[chunk * size : (chunk + 1) * size],
            coupling_ref.at[chunk * size : (chunk + 1) * size],
            sems.at[chunk],
        )
        for chunk in range(chunks)
    ]
    for copy in copies:
        copy.start()
    pert = t1_ref.shape[1]
    capacity = send_ref.shape[2]
    blocks = cols_ref.shape[1]
    parts = got_ref.shape[0]
    sources = neighbours(parts)
    low = low_half((pert, LANES))
    lane = lax.broadcasted_iota(jnp.int32, (1, LANES), 1)
    ghost_ids = sum(got_ref[source, pert + capacity : pert + capacity + 1, :] for source in sources)
    ghost_ids = jnp.where(lane < 4 * capacity, ghost_ids, -1.0)
    ids = jnp.concatenate([patch_ref[...].astype(F32), ghost_ids], axis=1)
    total = jnp.zeros((3 * pert, 2 * LANES), F32)
    for part in range(parts):
        names = (
            lax.broadcasted_iota(jnp.int32, (LANES, 2 * LANES), 0) + part * LANES
        ).astype(F32)
        hot = jnp.where(names == ids, 1.0, 0.0).astype(BF16)
        value = got_ref[part, :pert]
        top = value.astype(BF16)
        rest = value - top.astype(F32)
        mid = rest.astype(BF16)
        last = (rest - mid.astype(F32)).astype(BF16)
        total = total + jnp.dot(
            jnp.concatenate([top, mid, last], axis=0), hot, preferred_element_type=F32
        )
    picked = total[:pert] + total[pert : 2 * pert] + total[2 * pert :]
    local_picked = picked[:, :LANES]
    ghost_picked = picked[:, LANES:]
    full_low = low.astype(jnp.int32)
    column_patches = patches_of_columns(columns_ref, ids)
    patches_ref[...] = column_patches
    sub = lax.broadcasted_iota(jnp.int32, (8, LANES), 0)
    lane8 = lax.broadcasted_iota(jnp.int32, (8, LANES), 1)
    wanted = sub == lane8 % 4

    def listed(blocks_of_lanes):
        taken = jnp.take_along_axis(column_patches, blocks_of_lanes, axis=1)
        return jnp.sum(jnp.where(wanted, taken, 0.0), axis=0, keepdims=True)

    for tile in range(4 * blocks // LANES):
        names_ref[tile : tile + 1, :] = listed(tile * (LANES // 4) + lane8 // 4)
    w_copy.wait()
    w = w_ref[...]
    w_other = swap_halves(w)
    low_w = low_half(w.shape)
    row_ref[pl.ds(0, blocks // 2, stride=2), :] = jnp.where(low_w, w, w_other)
    row_ref[pl.ds(1, blocks // 2, stride=2), :] = jnp.where(low_w, w_other, w)
    for group, source in enumerate(sources):
        start = blocks + group * capacity
        row_ref[start : start + capacity, :] = got_ref[source, pert : pert + capacity, :]

    def seed(pair, _):
        index = 2 * pair + 1 - full_low
        spread = jnp.take_along_axis(local_picked, index, axis=1)
        value = spread * w_ref[pl.ds(pair, 1), :]
        t1_ref[pair] = value
        store_pair(ext_ref, pair, value, low)
        return 0

    lax.fori_loop(0, blocks // 2, seed, 0, unroll=16)
    for group, source in enumerate(sources):
        for slot in range(capacity):
            place = group * capacity + slot
            row = got_ref[source, pert + slot : pert + slot + 1, :]
            spread = jnp.broadcast_to(ghost_picked[:, place : place + 1], (pert, LANES))
            ext_ref[blocks + place] = (spread * row).astype(BF16)

    for chunk, copy in enumerate(copies):
        copy.wait()
        for block in range(chunk * size, (chunk + 1) * size):
            m_ref[block] = jnp.dot(
                diag_ref[block], coupling_ref[block], preferred_element_type=F32
            ).astype(BF16)

    low8 = low_half((8, LANES))
    masks = [(sub % 4 == k) & (low8 if k % 2 == 0 else ~low8) for k in range(4)]
    nothing = jnp.zeros((8, LANES), F32)

    def sweep(quad, _):
        rows = gather_rows(quad, cols_ref, ext_ref, low)
        tiles = ([], [])
        for place in range(QUAD):
            w_rows = [row_ref[pl.ds(cols_ref[k, quad * QUAD + place], 1), :] for k in range(4)]
            for side in range(2):
                tiles[side].append(
                    jnp.where(
                        masks[2 * side],
                        w_rows[2 * side],
                        jnp.where(masks[2 * side + 1], w_rows[2 * side + 1], nothing),
                    )
                )
        extra = jnp.concatenate([jnp.concatenate(side, axis=0) for side in tiles], axis=1)
        out = coupled_rows(quad, rows + [extra.astype(BF16)], m_ref)
        for place, value in enumerate(own_pairs(out, pert, low)):
            pair = 2 * quad + place
            store_pair(t2_ref, pair, t1_ref[pair] - value, low)
        for place, value in enumerate(own_pairs(out[QUAD * pert :], 8, low8)):
            v_ref[2 * quad + place] = value
        return 0

    lax.fori_loop(0, blocks // QUAD, sweep, 0, unroll=32)
    msgs = (o0, o1, o2, o3)
    fill_messages(send_ref, t2_ref, msgs, low)
    half = capacity // 2
    for group, ref in enumerate(msgs):
        places = jnp.zeros((8, LANES), jnp.int32)
        values = []
        for slot in range(capacity):
            block = jnp.maximum(send_ref[0, group, slot], 0)
            value = v_ref[block // 2]
            right = (slot - block) % 2 == 0
            values.append(jnp.where(right, value, swap_halves(value)))
            places = jnp.where(lane8 // 4 == slot, block, places)
        pairs = [
            jnp.where(low8, values[2 * pair], values[2 * pair + 1]) for pair in range(half)
        ]
        for tile in range(half // 2):
            ref[half + tile] = jnp.concatenate(pairs[2 * tile : 2 * tile + 2], axis=0).astype(BF16)
        patch = listed(places).astype(jnp.int32)
        ref[half + half // 2] = jnp.concatenate(
            [
                jnp.broadcast_to(patch // RADIX, (8, LANES)),
                jnp.broadcast_to(patch % RADIX, (8, LANES)),
            ],
            axis=0,
        ).astype(F32).astype(BF16)


def extend(ext_ref, local_ref, ghosts, low):
    blocks = local_ref.shape[0]
    count = (ext_ref.shape[0] - blocks) // 2 // len(ghosts)
    ext_ref[:blocks] = local_ref[...]
    for group, ref in enumerate(ghosts):
        for pair in range(count):
            store_pair(ext_ref, blocks // 2 + group * count + pair, ref[pair], low)


def sweep_kernel(
    cols_ref, send_ref, t1_ref, prev_ref, g0, g1, g2, g3, m_ref,
    next_ref, o0, o1, o2, o3, ext_ref,
):
    low = low_half(prev_ref.shape[1:])
    extend(ext_ref, prev_ref, (g0, g1, g2, g3), low)

    def sweep(quad, _):
        first, second = gather_multiply(quad, cols_ref, ext_ref, m_ref, low)
        store_pair(next_ref, 2 * quad, t1_ref[2 * quad] - first, low)
        store_pair(next_ref, 2 * quad + 1, t1_ref[2 * quad + 1] - second, low)
        return 0

    lax.fori_loop(0, cols_ref.shape[1] // QUAD, sweep, 0, unroll=32)
    fill_messages(send_ref, next_ref, (o0, o1, o2, o3), low)


def zero_rows(acc_refs, places):
    for ref in acc_refs:
        for place in places:
            ref[place] = jnp.zeros(ref.shape[1:], F32)


def multiply_scatter(quad, cols_ref, pairs, m_ref, acc_refs, low):
    zero = jnp.zeros(pairs[0].shape, F32)
    rows = []
    for place in range(QUAD):
        value = pairs[place // 2]
        kept = jnp.where(low, value, zero) if place % 2 == 0 else jnp.where(low, zero, value)
        tiles = [kept, zero] if place < 2 else [zero, kept]
        rows.append(jnp.concatenate(tiles, axis=1))
    lhs = jnp.concatenate(rows, axis=0).astype(BF16)
    rhs = m_ref[pl.ds(quad * QUAD, QUAD)].reshape(QUAD * HALF, 4 * HALF)
    out = jnp.dot(lhs, rhs, preferred_element_type=F32)
    p = pairs[0].shape[0]
    for place in range(QUAD):
        g = quad * QUAD + place
        for k in range(4):
            column = cols_ref[k, g]
            piece = out[place * p : (place + 1) * p, (k // 2) * LANES : (k // 2 + 1) * LANES]
            acc_refs[k][column] = acc_refs[k][column] + piece


def half_sums(acc_refs, place, low):
    return jnp.where(
        low, acc_refs[0][place] + acc_refs[2][place], acc_refs[1][place] + acc_refs[3][place]
    )


def pair_sum(acc_refs, pair, low):
    even = half_sums(acc_refs, 2 * pair, low)
    odd = half_sums(acc_refs, 2 * pair + 1, low)
    return jnp.where(low, even, odd) + swap_halves(jnp.where(low, odd, even))


def turn_kernel(
    cols_ref, t1_ref, prev_ref, g0, g1, g2, g3, m_ref, weight_ref, w_ref,
    tangent_hbm, terms_ref, z_ref, y_ref,
    ext_ref, tangent_ref, target_ref, u_ref, sem, *acc_refs,
):
    pert = prev_ref.shape[1]
    low = low_half(prev_ref.shape[1:])
    lane = lax.broadcasted_iota(jnp.int32, (pert, LANES), 1)
    blocks = cols_ref.shape[1]
    extend(ext_ref, prev_ref, (g0, g1, g2, g3), low)

    share = acc_refs[0].shape[0] // (blocks // QUAD)

    def sweep(quad, terms):
        zero_rows(acc_refs, [share * quad + i for i in range(share)])
        coupled = gather_multiply(quad, cols_ref, ext_ref, m_ref, low)
        for place in range(2):
            pair = 2 * quad + place
            value = t1_ref[pair] - coupled[place]
            start = pl.multiple_of(pair * LANES, LANES)
            tangent_ref[:, pl.ds(start, LANES)] = value
            target = value * weight_ref[pl.ds(pair, 1), :]
            target_ref[pair] = target
            product = target * w_ref[pl.ds(pair, 1), :]
            even = jnp.sum(jnp.where(low, product, 0.0), axis=1, keepdims=True)
            odd = jnp.sum(jnp.where(low, 0.0, product), axis=1, keepdims=True)
            terms = jnp.where(
                lane == 2 * pair, even, jnp.where(lane == 2 * pair + 1, odd, terms)
            )
        return terms

    terms_ref[...] = lax.fori_loop(
        0, blocks // QUAD, sweep, jnp.zeros((pert, LANES), F32), unroll=32
    )
    tangent_copy = pltpu.make_async_copy(tangent_ref, tangent_hbm, sem)
    tangent_copy.start()
    scatter_all(cols_ref, target_ref, m_ref, acc_refs, low)

    def own(pair, _):
        u_ref[pair] = target_ref[pair] - pair_sum(acc_refs, pair, low)
        zero_rows(acc_refs, (2 * pair, 2 * pair + 1))
        return 0

    lax.fori_loop(0, blocks // 2, own, 0, unroll=16)
    for pair in range(y_ref.shape[0]):
        y_ref[pair] = (-pair_sum(acc_refs, blocks // 2 + pair, low)).astype(BF16)
        zero_rows(acc_refs, (blocks + 2 * pair, blocks + 2 * pair + 1))
    scatter_all(cols_ref, u_ref, m_ref, acc_refs, low)

    def second(pair, _):
        z_ref[pair] = (pair_sum(acc_refs, pair, low) - target_ref[pair]).astype(BF16)
        return 0

    lax.fori_loop(0, blocks // 2, second, 0, unroll=16)
    for pair in range(blocks // 2, z_ref.shape[0]):
        z_ref[pair] = pair_sum(acc_refs, pair, low).astype(BF16)
    tangent_copy.wait()


def scatter_all(cols_ref, u_ref, m_ref, acc_refs, low):
    def sweep(quad, _):
        pairs = [u_ref[2 * quad], u_ref[2 * quad + 1]]
        multiply_scatter(quad, cols_ref, pairs, m_ref, acc_refs, low)
        return 0

    lax.fori_loop(0, cols_ref.shape[1] // QUAD, sweep, 0, unroll=32)


def write_hot(hot_ref, rows, part):
    start = pl.multiple_of(part * LANES, LANES)
    names = lax.broadcasted_iota(jnp.int32, (LANES, LANES), 0) + part * LANES
    names = names.astype(F32)
    for tile, row in enumerate(rows):
        hot_ref[pl.ds(start, LANES), tile * LANES : (tile + 1) * LANES] = jnp.where(
            names == row, 1.0, 0.0
        ).astype(BF16)


def window_kernel(
    cols_ref, send_ref, columns_ref, patch_ref, names_ref, patches_ref, g0, g1, g2, g3,
    v_ref, m_ref, hot_ref, o0, o1, o2, o3, vector_ref,
):
    ghosts = (g0, g1, g2, g3)
    capacity = send_ref.shape[2]
    half = capacity // 2
    blocks = cols_ref.shape[1]
    low8 = low_half((8, LANES))
    sub = lax.broadcasted_iota(jnp.int32, (8, LANES), 0)
    lane = lax.broadcasted_iota(jnp.int32, (8, LANES), 1)

    listed = []
    there = jnp.zeros((8, LANES), F32)
    for group, ref in enumerate(ghosts):
        digits = ref[ref.shape[0] - 1].astype(F32)
        listed.append(digits[0:1] * RADIX + digits[8:9])
        taken = jnp.take_along_axis(
            jnp.broadcast_to(listed[-1], (8, LANES)), (lane % capacity) * 4 + sub % 4, axis=1
        )
        there = jnp.where(lane // capacity == group, taken, there)
    here = patches_ref[...]
    rows = [patch_ref[...].astype(F32)] + [names_ref[tile : tile + 1] for tile in range(4)]
    for tile in range(2):
        rows.append(
            jnp.where(low8[:1], listed[2 * tile], swap_halves(listed[2 * tile + 1]))
        )

    def spread(pair, value):
        other = swap_halves(value)
        vector_ref[2 * pair] = jnp.where(low8, value, other)
        vector_ref[2 * pair + 1] = jnp.where(low8, other, value)

    for pair in range(blocks // 2):
        spread(pair, v_ref[pair])
    for group, ref in enumerate(ghosts):
        for tile in range(half // 2):
            both = ref[half + tile].astype(F32)
            for side in range(2):
                pair = blocks // 2 + group * half + 2 * tile + side
                spread(pair, both[8 * side : 8 * side + 8])

    own = (sub < 4) == low8
    nothing = jnp.zeros((8, LANES), F32)
    low = low_half((16, LANES))
    columns = jnp.concatenate([columns_ref[...], columns_ref[...]], axis=0)
    sub16 = lax.broadcasted_iota(jnp.int32, (16, LANES), 0)
    for group, ref in enumerate((o0, o1, o2, o3)):
        slots = [jnp.maximum(send_ref[0, group, slot], 0) for slot in range(capacity)]
        for four in range(capacity // QUAD):
            lhs = []
            rhs = []
            for block in slots[four * QUAD : (four + 1) * QUAD]:
                a0, a1, a2, a3 = (vector_ref[cols_ref[k, block]] for k in range(4))
                left = jnp.where(own, jnp.where(sub < 4, a0, a1), nothing)
                right = jnp.where(own, jnp.where(sub < 4, a2, a3), nothing)
                lhs.append(
                    jnp.concatenate(
                        [
                            jnp.concatenate([left, nothing], axis=0),
                            jnp.concatenate([nothing, right], axis=0),
                        ],
                        axis=1,
                    ).astype(BF16)
                )
                rhs.append(m_ref[block])
            out = lax.dot_general(
                jnp.concatenate(lhs, axis=0),
                jnp.concatenate(rhs, axis=0),
                (((1,), (1,)), ((), ())),
                preferred_element_type=F32,
            )
            for side, value in enumerate(own_pairs(out, 16, low)):
                ref[2 * four + side] = value.astype(BF16)
        digits = jnp.zeros((16, LANES), F32)
        for tile in range(2):
            places = jnp.zeros((8, LANES), jnp.int32)
            for slot in range(half):
                places = jnp.where(lane // 16 == slot, slots[tile * half + slot], places)
            taken = jnp.take_along_axis(columns, places, axis=1).astype(F32)
            mine = jnp.sum(
                jnp.where(sub == (lane % 16) // 4, taken, 0.0), axis=0, keepdims=True
            )
            mine = jnp.broadcast_to(mine, (8, LANES)).astype(jnp.int32)
            taken = jnp.where(
                mine < LANES,
                jnp.take_along_axis(here, jnp.minimum(mine, LANES - 1), axis=1),
                jnp.take_along_axis(there, jnp.maximum(mine - LANES, 0), axis=1),
            )
            patch = jnp.sum(jnp.where(sub == lane % 4, taken, 0.0), axis=0, keepdims=True)
            patch = patch.astype(jnp.int32)
            digits = jnp.where(
                sub16 == 2 * tile,
                (patch // RADIX).astype(F32),
                jnp.where(sub16 == 2 * tile + 1, (patch % RADIX).astype(F32), digits),
            )
        ref[half] = digits.astype(BF16)

    def one(part, _):
        write_hot(hot_ref, rows, part)
        return 0

    lax.fori_loop(0, hot_ref.shape[0] // LANES, one, 0, unroll=2)


def last_kernel(
    z_ref, y_ref, v_ref, v0, v1, v2, v3, x0, x1, x2, x3,
    hot_ref, terms_ref, got_ref, out_ref,
):
    pert = z_ref.shape[1]
    local_pairs = v_ref.shape[0]
    half = (z_ref.shape[0] - local_pairs) // 4
    parts = got_ref.shape[0]
    low8 = low_half((8, LANES))
    low = low_half((16, LANES))
    sub = lax.broadcasted_iota(jnp.int32, (8, LANES), 0)
    own = (sub < 4) == low8
    nothing = jnp.zeros((8, LANES), F32)
    zero = jnp.zeros((16, LANES), F32)

    def wide(left, right):
        return jnp.concatenate([left, right], axis=1)

    def product(lhs, rhs):
        return lax.dot_general(
            lhs, rhs.astype(BF16), (((1,), (1,)), ((), ())), preferred_element_type=F32
        )

    def first_level(first, second):
        return jnp.concatenate(
            [
                wide(jnp.where(own, first, nothing), nothing),
                wide(nothing, jnp.where(own, second, nothing)),
            ],
            axis=0,
        )

    def second_level(first, second):
        return jnp.concatenate(
            [
                wide(jnp.where(low, first, zero), zero),
                wide(jnp.where(low, zero, first), zero),
                wide(zero, jnp.where(low, second, zero)),
                wide(zero, jnp.where(low, zero, second)),
            ],
            axis=0,
        )

    pieces = [terms_ref[...]]
    for pair in range(0, local_pairs, 2):
        lhs = wide(z_ref[pair], z_ref[pair + 1])
        pieces.append(product(lhs, first_level(v_ref[pair], v_ref[pair + 1])))
    for group, ref in enumerate((v0, v1, v2, v3)):
        for tile in range(half // 2):
            both = ref[half + tile].astype(F32)
            pair = local_pairs + group * half + 2 * tile
            lhs = wide(z_ref[pair], z_ref[pair + 1])
            pieces.append(product(lhs, first_level(both[:8], both[8:])))
    rows = []
    for group, ref in enumerate((x0, x1, x2, x3)):
        for tile in range(half // 2):
            pair = group * half + 2 * tile
            lhs = wide(y_ref[pair], y_ref[pair + 1])
            first, second = (ref[2 * tile + side].astype(F32) for side in range(2))
            pieces.append(product(lhs, second_level(first, second)))
        digits = ref[half].astype(F32)
        for tile in range(2):
            rows.append(
                digits[2 * tile : 2 * tile + 1] * RADIX + digits[2 * tile + 1 : 2 * tile + 2]
            )
    terms = jnp.concatenate(pieces, axis=1)
    top = terms.astype(BF16)
    rest = (terms - top.astype(F32)).astype(BF16)
    both = jnp.concatenate([top, rest], axis=0)
    mine = lax.axis_index("pert")
    sub16 = lax.broadcasted_iota(jnp.int32, (pert, LANES), 0)
    perts = out_ref.shape[0] // parts
    first_names = lax.broadcasted_iota(jnp.int32, (LANES, LANES), 0).astype(F32)
    for part in range(parts):
        hot = jnp.concatenate(
            [hot_ref[part * LANES : (part + 1) * LANES, :]]
            + [
                jnp.where(first_names == row - part * LANES, 1.0, 0.0).astype(BF16)
                for row in rows
            ],
            axis=1,
        )
        out = lax.dot_general(both, hot, (((1,), (1,)), ((), ())), preferred_element_type=F32)
        value = out[:pert] + out[pert:]
        curve = jnp.sum(value * got_ref[part, :pert], axis=0, keepdims=True)
        top = curve.astype(BF16).astype(F32)
        extra = jnp.where(sub16 == 0, top, jnp.where(sub16 == 1, curve - top, 0.0))
        for place in range(perts):
            out_ref[part * perts + place] = jnp.where(place == mine, value, extra).astype(BF16)


def owner_kernel(terms_ref, probe_ref, hessian_ref, curve_ref, *, parts, scale):
    perts = terms_ref.shape[0] // parts
    mine = lax.axis_index("pert")
    total = jnp.zeros(hessian_ref.shape, F32)
    every = jnp.zeros(hessian_ref.shape, F32)
    for part in range(parts):
        total = total + terms_ref[part * perts + mine].astype(F32)
        for place in range(perts):
            value = terms_ref[part * perts + place].astype(F32)
            every = every + jnp.where(place == mine, 0.0, value)
    hessian_ref[...] = total
    own = jnp.sum(total * probe_ref[...], axis=0, keepdims=True)
    curve_ref[...] = (own + every[0:1] + every[1:2]) * scale


def call(body, outs, spaces, scratch=(), name=None, flops=0, moved=1 << 20, limit=12, out_specs=None):
    return pl.pallas_call(
        body,
        out_shape=outs,
        in_specs=[{"s": SMEM, "v": VMEM, "h": HBM}[s] for s in spaces],
        out_specs=out_specs or jax.tree.map(lambda _: VMEM, outs),
        scratch_shapes=list(scratch),
        compiler_params=pltpu.CompilerParams(vmem_limit_bytes=limit * MIB),
        name=name,
        cost_estimate=pl.CostEstimate(flops=flops, transcendentals=0, bytes_accessed=moved),
    )


def shards(
    probes, melt_shape, obs_weight, diag_inverse, coupling, columns, send_list, patch_of_block
):
    pert = probes.shape[0]
    blocks = coupling.shape[0]
    capacity = send_list.shape[2]
    parts = lax.axis_size("dom")
    pairs = blocks // 2
    shape = jax.ShapeDtypeStruct
    msgs = [shape((capacity // 2, pert, LANES), BF16)] * 4
    pair_array = shape((pairs, pert, LANES), F32)
    block_array = shape((blocks, pert, LANES), BF16)
    ext = pltpu.VMEM((blocks + 4 * capacity, pert, LANES), BF16)
    accs = [pltpu.VMEM((blocks + 4 * capacity, pert, LANES), F32)] * 4
    held = pltpu.VMEM((pairs, pert, LANES), F32)
    melt = melt_shape.reshape(pairs, LANES)
    weight = obs_weight.reshape(pairs, LANES)
    patch = patch_of_block.reshape(1, blocks)

    perts = lax.axis_size("pert")
    columns = columns.T
    w_far, outgoing = call(
        functools.partial(melt_kernel, parts=parts),
        [shape((W_ROWS, LANES), F32), shape((parts, pert + capacity + 8, LANES), F32)],
        "hhhhh",
        [
            pltpu.SMEM(send_list.shape, jnp.int32),
            pltpu.VMEM((pairs, LANES), F32),
            pltpu.VMEM((1, blocks), jnp.int32),
            pltpu.VMEM(probes.shape, F32),
            pltpu.VMEM((HALF, HALF, blocks), BF16),
            pltpu.VMEM((pairs, LANES), F32),
            pltpu.SemaphoreType.DMA((5,)),
            pltpu.SemaphoreType.DMA,
        ],
        name="melt",
        out_specs=[HBM, VMEM],
        limit=60,
    )(send_list, melt, patch, probes, jnp.transpose(diag_inverse, (1, 2, 0)))
    got = lax.all_to_all(outgoing, "dom", 0, 0, tiled=True)
    wide = [shape((capacity // 2 + capacity // 4 + 1, pert, LANES), BF16)] * 4
    m, w, v, names, patches, t1, state, *out = call(
        first_kernel,
        [
            shape(coupling.shape, BF16),
            shape((pairs, LANES), F32),
            shape((pairs, 8, LANES), F32),
            shape((8, LANES), F32),
            shape((8, LANES), F32),
            pair_array,
            block_array,
        ]
        + wide,
        "ssvvvhvh",
        [
            ext,
            pltpu.VMEM((blocks + 4 * capacity, LANES), F32),
            pltpu.VMEM(coupling.shape, BF16),
            pltpu.SemaphoreType.DMA,
            pltpu.SemaphoreType.DMA((8,)),
        ],
        name="first",
        limit=46,
    )(columns, send_list, patch, columns, got, w_far, diag_inverse, coupling)
    carried = [rotated(x, o) for x, o in zip(out, OFFSET_LIST)]
    state, *out = call(
        sweep_kernel, [block_array] + msgs, "ssvvvvvvv", [ext], name="sweep"
    )(columns, send_list, t1, state, *carried, m)
    ghosts = [rotated(v, o) for v, o in zip(out, OFFSET_LIST)]
    hot, *far = call(
        window_kernel,
        [shape((parts * LANES, 7 * LANES), BF16)]
        + [shape((capacity // 2 + 1, pert, LANES), BF16)] * 4,
        "ss" + "v" * 10,
        [pltpu.VMEM((blocks + 4 * capacity, 8, LANES), F32)],
        name="window",
        moved=4 << 20,
    )(columns, send_list, columns, patch, names, patches, *carried, v, m)
    far, ghosts = lax.optimization_barrier((far, ghosts))
    far = [rotated(x, o) for x, o in zip(far, OFFSET_LIST)]
    tangent, terms, z, y = call(
        turn_kernel,
        [
            shape((pert, blocks * HALF), F32),
            shape((pert, LANES), F32),
            shape((pairs + 2 * capacity, pert, LANES), BF16),
            shape((2 * capacity, pert, LANES), BF16),
        ],
        "s" + "v" * 9,
        [
            ext,
            pltpu.VMEM((pert, blocks * HALF), F32),
            held,
            held,
            pltpu.SemaphoreType.DMA,
        ]
        + accs,
        name="turn",
        moved=16 << 20,
        out_specs=[HBM, VMEM, VMEM, VMEM],
    )(columns, t1, state, *ghosts, m, weight, w)
    terms = call(
        last_kernel, shape((parts * perts, pert, LANES), BF16), "v" * 14, name="last"
    )(z, y, v, *carried, *far, hot, terms, got)
    terms = lax.all_to_all(terms, ("dom", "pert"), 0, 0, tiled=True)
    hessian_probe, curvature = call(
        functools.partial(owner_kernel, parts=parts, scale=1.0 / (pert * perts)),
        [shape(probes.shape, F32), shape((1, LANES), F32)],
        "vv",
        name="owner",
    )(terms, probes)
    return tangent, hessian_probe, curvature.reshape(-1)


def solution(mesh):
    in_specs = (
        P("pert", "dom"),
        P("dom"),
        P("dom"),
        P("dom", None, None),
        P("dom", None, None),
        P("dom", None),
        P("dom", None, None),
        P("dom"),
    )
    out_specs = (P("pert", "dom"), P("pert", "dom"), P("dom"))
    return jax.shard_map(shards, mesh=mesh, in_specs=in_specs, out_specs=out_specs, check_vma=False)
```

```python
import functools

import jax
import jax.numpy as jnp
from jax import lax
from jax.experimental import pallas as pl
from jax.experimental.pallas import tpu as pltpu
from jax.sharding import PartitionSpec as P

OFFSET_LIST = (-2, -1, 1, 2)
F32 = jnp.float32
BF16 = jnp.bfloat16
LANES = 128
HALF = 64
QUAD = 4
RADIX = 64

VMEM = pl.BlockSpec(memory_space=pltpu.VMEM)
SMEM = pl.BlockSpec(memory_space=pltpu.SMEM)
HBM = pl.BlockSpec(memory_space=pltpu.HBM)
MIB = 1024 * 1024


def low_half(shape):
    return lax.broadcasted_iota(jnp.int32, shape, len(shape) - 1) < HALF


def swap_halves(value):
    return pltpu.roll(value, HALF, 1)


def rotated(value, by):
    peers = lax.axis_size("dom")
    return lax.ppermute(value, "dom", [(i, (i + by) % peers) for i in range(peers)])


def neighbours(parts):
    me = lax.axis_index("dom")
    return [lax.rem(me - offset + parts, parts) for offset in OFFSET_LIST]


def melt_kernel(
    send_hbm, melt_hbm, patch_hbm, probe_hbm, diag_hbm, w_ref, out_ref,
    send_ref, melt_ref, patch_ref, probe_ref, diag_ref, sems, *, parts,
):
    copies = [
        pltpu.make_async_copy(source, target, sems.at[number])
        for number, (source, target) in enumerate(
            (
                (diag_hbm, diag_ref),
                (melt_hbm, melt_ref),
                (patch_hbm, patch_ref),
                (probe_hbm, probe_ref),
                (send_hbm, send_ref),
            )
        )
    ]
    for copy in copies:
        copy.start()
    for copy in copies:
        copy.wait()
    pairs = melt_ref.shape[0]
    pert = probe_ref.shape[0]
    capacity = send_ref.shape[2]
    low = low_half((1, LANES))
    lane = lax.broadcasted_iota(jnp.int32, (HALF, LANES), 1)
    turned = jnp.transpose(jnp.concatenate([melt_ref[...], jnp.zeros((LANES - pairs, LANES), F32)], axis=0))
    even = jnp.take_along_axis(turned[:HALF], lane // 2, axis=1)
    odd = jnp.take_along_axis(turned[HALF:], lane // 2, axis=1)
    melt = jnp.where(lane % 2 == 0, even, odd)
    sums = [
        jnp.sum(diag_ref[i].astype(F32) * melt, axis=0, keepdims=True)
        for i in range(diag_ref.shape[0])
    ]
    sums = jnp.concatenate(sums, axis=0)
    source = 2 * (lane % HALF)
    both = jnp.concatenate(
        [
            jnp.take_along_axis(sums, source, axis=1),
            jnp.take_along_axis(sums, source + 1, axis=1),
        ],
        axis=0,
    )
    w_ref[...] = jnp.transpose(both)[:pairs]
    patch_row = jnp.broadcast_to(patch_ref[...].astype(F32), (8, LANES))
    lane = lax.broadcasted_iota(jnp.int32, (8, LANES), 1)
    for part in range(parts):
        out_ref[part, :pert] = probe_ref[...]
    me = lax.axis_index("dom")
    for group, offset in enumerate(OFFSET_LIST):
        to = lax.rem(me + offset + parts, parts)
        ids = jnp.zeros((8, LANES), jnp.int32)
        for slot in range(capacity):
            block = jnp.maximum(send_ref[0, group, slot], 0)
            row = w_ref[pl.ds(block // 2, 1), :]
            row = jnp.where(low == (block % 2 == 0), row, swap_halves(row))
            if slot % 2 == 0:
                left = row
            else:
                place = pert + slot // 2
                out_ref[to, place : place + 1, :] = jnp.where(low, left, row)
            ids = jnp.where(lane == group * capacity + slot, block, ids)
        mine = (lane >= group * capacity) & (lane < (group + 1) * capacity)
        out_ref[to, pert + capacity // 2 :, :] = jnp.where(
            mine, jnp.take_along_axis(patch_row, ids, axis=1), 0.0
        )


def gather_rows(quad, cols_ref, ext_ref, low):
    rows = []
    for place in range(QUAD):
        g = quad * QUAD + place
        tiles = [ext_ref[cols_ref[k, g]] for k in range(4)]
        rows.append(
            jnp.concatenate(
                [jnp.where(low, tiles[0], tiles[1]), jnp.where(low, tiles[2], tiles[3])], axis=1
            )
        )
    return rows


def coupled_rows(quad, rows, m_ref):
    rhs = m_ref[pl.ds(quad * QUAD, QUAD)].reshape(QUAD * HALF, 4 * HALF)
    return lax.dot_general(
        jnp.concatenate(rows, axis=0), rhs, (((1,), (1,)), ((), ())), preferred_element_type=F32
    )


def own_pairs(out, size, low):
    first = jnp.where(low, out[:size, :LANES], out[size : 2 * size, :LANES])
    second = jnp.where(low, out[2 * size : 3 * size, LANES:], out[3 * size : 4 * size, LANES:])
    return first, second


def gather_multiply(quad, cols_ref, ext_ref, m_ref, low):
    out = coupled_rows(quad, gather_rows(quad, cols_ref, ext_ref, low), m_ref)
    return own_pairs(out, out.shape[0] // QUAD, low)


def store_pair(ref, pair, value, low):
    value = value.astype(BF16)
    other = swap_halves(value.astype(F32)).astype(BF16)
    ref[2 * pair] = jnp.where(low, value, other)
    ref[2 * pair + 1] = jnp.where(low, other, value)


def fill_messages(send_ref, ref, msg_refs, low):
    for group, msg_ref in enumerate(msg_refs):
        for pair in range(send_ref.shape[2] // 2):
            even, odd = (
                ref[jnp.maximum(send_ref[0, group, 2 * pair + half], 0)] for half in range(2)
            )
            msg_ref[pair] = jnp.where(low, even, odd)


def patches_of_columns(columns_ref, ids):
    columns = jnp.concatenate([columns_ref[...], columns_ref[...]], axis=0)
    here = jnp.broadcast_to(ids[:, :LANES], columns.shape)
    there = jnp.broadcast_to(ids[:, LANES:], columns.shape)
    return jnp.where(
        columns < LANES,
        jnp.take_along_axis(here, jnp.minimum(columns, LANES - 1), axis=1),
        jnp.take_along_axis(there, jnp.maximum(columns - LANES, 0), axis=1),
    )


def first_kernel(
    cols_ref, send_ref, patch_ref, columns_ref, got_ref, w_hbm, diag_ref, coupling_hbm,
    m_ref, v_ref, names_ref, patches_ref, t1_ref, t2_ref, o0, o1, o2, o3,
    ext_ref, row_ref, w_ref, coupling_ref, w_sem, sems,
):
    w_copy = pltpu.make_async_copy(w_hbm, w_ref, w_sem)
    w_copy.start()
    chunks = sems.shape[0]
    size = diag_ref.shape[0] // chunks
    copies = [
        pltpu.make_async_copy(
            coupling_hbm.at[chunk * size : (chunk + 1) * size],
            coupling_ref.at[chunk * size : (chunk + 1) * size],
            sems.at[chunk],
        )
        for chunk in range(chunks)
    ]
    for copy in copies:
        copy.start()
    pert = t1_ref.shape[1]
    capacity = send_ref.shape[2]
    blocks = cols_ref.shape[1]
    parts = got_ref.shape[0]
    sources = neighbours(parts)
    low = low_half((pert, LANES))
    lane = lax.broadcasted_iota(jnp.int32, (1, LANES), 1)
    names = pert + capacity // 2
    ghost_ids = sum(got_ref[source, names : names + 1, :] for source in sources)
    ghost_ids = jnp.where(lane < 4 * capacity, ghost_ids, -1.0)
    ids = jnp.concatenate([patch_ref[...].astype(F32), ghost_ids], axis=1)
    total = jnp.zeros((3 * pert, 2 * LANES), F32)
    for part in range(parts):
        names = (
            lax.broadcasted_iota(jnp.int32, (LANES, 2 * LANES), 0) + part * LANES
        ).astype(F32)
        hot = jnp.where(names == ids, 1.0, 0.0).astype(BF16)
        value = got_ref[part, :pert]
        top = value.astype(BF16)
        rest = value - top.astype(F32)
        mid = rest.astype(BF16)
        last = (rest - mid.astype(F32)).astype(BF16)
        total = total + jnp.dot(
            jnp.concatenate([top, mid, last], axis=0), hot, preferred_element_type=F32
        )
    picked = total[:pert] + total[pert : 2 * pert] + total[2 * pert :]
    local_picked = picked[:, :LANES]
    ghost_picked = picked[:, LANES:]
    full_low = low.astype(jnp.int32)
    column_patches = patches_of_columns(columns_ref, ids)
    patches_ref[...] = column_patches
    sub = lax.broadcasted_iota(jnp.int32, (8, LANES), 0)
    lane8 = lax.broadcasted_iota(jnp.int32, (8, LANES), 1)
    wanted = sub == lane8 % 4

    def listed(blocks_of_lanes):
        taken = jnp.take_along_axis(column_patches, blocks_of_lanes, axis=1)
        return jnp.sum(jnp.where(wanted, taken, 0.0), axis=0, keepdims=True)

    for tile in range(4 * blocks // LANES):
        names_ref[tile : tile + 1, :] = listed(tile * (LANES // 4) + lane8 // 4)
    w_copy.wait()
    w = w_ref[...]
    w_other = swap_halves(w)
    low_w = low_half(w.shape)
    row_ref[pl.ds(0, blocks // 2, stride=2), :] = jnp.where(low_w, w, w_other)
    row_ref[pl.ds(1, blocks // 2, stride=2), :] = jnp.where(low_w, w_other, w)
    for group, source in enumerate(sources):
        start = blocks + group * capacity
        both = got_ref[source, pert : pert + capacity // 2, :]
        other = swap_halves(both)
        low_both = low_half(both.shape)
        row_ref[pl.ds(start, capacity // 2, stride=2), :] = jnp.where(low_both, both, other)
        row_ref[pl.ds(start + 1, capacity // 2, stride=2), :] = jnp.where(low_both, other, both)

    def seed(pair, _):
        index = 2 * pair + 1 - full_low
        spread = jnp.take_along_axis(local_picked, index, axis=1)
        value = spread * w_ref[pl.ds(pair, 1), :]
        t1_ref[pair] = value
        store_pair(ext_ref, pair, value, low)
        return 0

    lax.fori_loop(0, blocks // 2, seed, 0, unroll=16)
    for group, source in enumerate(sources):
        for slot in range(capacity):
            place = group * capacity + slot
            row = row_ref[blocks + place : blocks + place + 1, :]
            spread = jnp.broadcast_to(ghost_picked[:, place : place + 1], (pert, LANES))
            ext_ref[blocks + place] = (spread * row).astype(BF16)

    for chunk, copy in enumerate(copies):
        copy.wait()
        for block in range(chunk * size, (chunk + 1) * size):
            m_ref[block] = jnp.dot(
                diag_ref[block], coupling_ref[block], preferred_element_type=F32
            ).astype(BF16)

    low8 = low_half((8, LANES))
    masks = [(sub % 4 == k) & (low8 if k % 2 == 0 else ~low8) for k in range(4)]
    nothing = jnp.zeros((8, LANES), F32)

    def sweep(quad, _):
        rows = gather_rows(quad, cols_ref, ext_ref, low)
        tiles = ([], [])
        for place in range(QUAD):
            w_rows = [row_ref[pl.ds(cols_ref[k, quad * QUAD + place], 1), :] for k in range(4)]
            for side in range(2):
                tiles[side].append(
                    jnp.where(
                        masks[2 * side],
                        w_rows[2 * side],
                        jnp.where(masks[2 * side + 1], w_rows[2 * side + 1], nothing),
                    )
                )
        extra = jnp.concatenate([jnp.concatenate(side, axis=0) for side in tiles], axis=1)
        out = coupled_rows(quad, rows + [extra.astype(BF16)], m_ref)
        for place, value in enumerate(own_pairs(out, pert, low)):
            pair = 2 * quad + place
            store_pair(t2_ref, pair, t1_ref[pair] - value, low)
        for place, value in enumerate(own_pairs(out[QUAD * pert :], 8, low8)):
            v_ref[2 * quad + place] = value
        return 0

    lax.fori_loop(0, blocks // QUAD, sweep, 0, unroll=32)
    msgs = (o0, o1, o2, o3)
    fill_messages(send_ref, t2_ref, msgs, low)
    half = capacity // 2
    for group, ref in enumerate(msgs):
        places = jnp.zeros((8, LANES), jnp.int32)
        values = []
        for slot in range(capacity):
            block = jnp.maximum(send_ref[0, group, slot], 0)
            value = v_ref[block // 2]
            right = (slot - block) % 2 == 0
            values.append(jnp.where(right, value, swap_halves(value)))
            places = jnp.where(lane8 // 4 == slot, block, places)
        pairs = [
            jnp.where(low8, values[2 * pair], values[2 * pair + 1]) for pair in range(half)
        ]
        for tile in range(half // 2):
            ref[half + tile] = jnp.concatenate(pairs[2 * tile : 2 * tile + 2], axis=0).astype(BF16)
        patch = listed(places).astype(jnp.int32)
        ref[half + half // 2] = jnp.concatenate(
            [
                jnp.broadcast_to(patch // RADIX, (8, LANES)),
                jnp.broadcast_to(patch % RADIX, (8, LANES)),
            ],
            axis=0,
        ).astype(F32).astype(BF16)


def extend(ext_ref, local_ref, ghosts, low):
    blocks = local_ref.shape[0]
    count = (ext_ref.shape[0] - blocks) // 2 // len(ghosts)
    ext_ref[:blocks] = local_ref[...]
    for group, ref in enumerate(ghosts):
        for pair in range(count):
            store_pair(ext_ref, blocks // 2 + group * count + pair, ref[pair], low)


def sweep_kernel(
    cols_ref, send_ref, t1_ref, prev_ref, g0, g1, g2, g3, m_ref,
    next_ref, o0, o1, o2, o3, ext_ref,
):
    low = low_half(prev_ref.shape[1:])
    extend(ext_ref, prev_ref, (g0, g1, g2, g3), low)

    def sweep(quad, _):
        first, second = gather_multiply(quad, cols_ref, ext_ref, m_ref, low)
        store_pair(next_ref, 2 * quad, t1_ref[2 * quad] - first, low)
        store_pair(next_ref, 2 * quad + 1, t1_ref[2 * quad + 1] - second, low)
        return 0

    lax.fori_loop(0, cols_ref.shape[1] // QUAD, sweep, 0, unroll=32)
    fill_messages(send_ref, next_ref, (o0, o1, o2, o3), low)


def zero_rows(acc_refs, places):
    for ref in acc_refs:
        for place in places:
            ref[place] = jnp.zeros(ref.shape[1:], F32)


def multiply_scatter(quad, cols_ref, pairs, m_ref, acc_refs, low):
    zero = jnp.zeros(pairs[0].shape, F32)
    rows = []
    for place in range(QUAD):
        value = pairs[place // 2]
        kept = jnp.where(low, value, zero) if place % 2 == 0 else jnp.where(low, zero, value)
        tiles = [kept, zero] if place < 2 else [zero, kept]
        rows.append(jnp.concatenate(tiles, axis=1))
    lhs = jnp.concatenate(rows, axis=0).astype(BF16)
    rhs = m_ref[pl.ds(quad * QUAD, QUAD)].reshape(QUAD * HALF, 4 * HALF)
    out = jnp.dot(lhs, rhs, preferred_element_type=F32)
    p = pairs[0].shape[0]
    for place in range(QUAD):
        g = quad * QUAD + place
        for k in range(4):
            column = cols_ref[k, g]
            piece = out[place * p : (place + 1) * p, (k // 2) * LANES : (k // 2 + 1) * LANES]
            acc_refs[k][column] = acc_refs[k][column] + piece


def half_sums(acc_refs, place, low):
    return jnp.where(
        low, acc_refs[0][place] + acc_refs[2][place], acc_refs[1][place] + acc_refs[3][place]
    )


def pair_sum(acc_refs, pair, low):
    even = half_sums(acc_refs, 2 * pair, low)
    odd = half_sums(acc_refs, 2 * pair + 1, low)
    return jnp.where(low, even, odd) + swap_halves(jnp.where(low, odd, even))


def turn_kernel(
    cols_ref, t1_ref, prev_ref, g0, g1, g2, g3, m_ref, weight_ref, w_ref,
    tangent_hbm, terms_ref, z_ref, y_ref,
    ext_ref, tangent_ref, target_ref, u_ref, sem, *acc_refs,
):
    pert = prev_ref.shape[1]
    low = low_half(prev_ref.shape[1:])
    lane = lax.broadcasted_iota(jnp.int32, (pert, LANES), 1)
    blocks = cols_ref.shape[1]
    extend(ext_ref, prev_ref, (g0, g1, g2, g3), low)

    share = acc_refs[0].shape[0] // (blocks // QUAD)

    def sweep(quad, terms):
        zero_rows(acc_refs, [share * quad + i for i in range(share)])
        coupled = gather_multiply(quad, cols_ref, ext_ref, m_ref, low)
        for place in range(2):
            pair = 2 * quad + place
            value = t1_ref[pair] - coupled[place]
            start = pl.multiple_of(pair * LANES, LANES)
            tangent_ref[:, pl.ds(start, LANES)] = value
            target = value * weight_ref[pl.ds(pair, 1), :]
            target_ref[pair] = target
            product = target * w_ref[pl.ds(pair, 1), :]
            even = jnp.sum(jnp.where(low, product, 0.0), axis=1, keepdims=True)
            odd = jnp.sum(jnp.where(low, 0.0, product), axis=1, keepdims=True)
            terms = jnp.where(
                lane == 2 * pair, even, jnp.where(lane == 2 * pair + 1, odd, terms)
            )
        return terms

    terms_ref[...] = lax.fori_loop(
        0, blocks // QUAD, sweep, jnp.zeros((pert, LANES), F32), unroll=32
    )
    tangent_copy = pltpu.make_async_copy(tangent_ref, tangent_hbm, sem)
    tangent_copy.start()
    scatter_all(cols_ref, target_ref, m_ref, acc_refs, low)

    def own(pair, _):
        u_ref[pair] = target_ref[pair] - pair_sum(acc_refs, pair, low)
        zero_rows(acc_refs, (2 * pair, 2 * pair + 1))
        return 0

    lax.fori_loop(0, blocks // 2, own, 0, unroll=16)
    for pair in range(y_ref.shape[0]):
        y_ref[pair] = (-pair_sum(acc_refs, blocks // 2 + pair, low)).astype(BF16)
        zero_rows(acc_refs, (blocks + 2 * pair, blocks + 2 * pair + 1))
    scatter_all(cols_ref, u_ref, m_ref, acc_refs, low)

    def second(pair, _):
        z_ref[pair] = (pair_sum(acc_refs, pair, low) - target_ref[pair]).astype(BF16)
        return 0

    lax.fori_loop(0, blocks // 2, second, 0, unroll=16)
    for pair in range(blocks // 2, z_ref.shape[0]):
        z_ref[pair] = pair_sum(acc_refs, pair, low).astype(BF16)
    tangent_copy.wait()


def scatter_all(cols_ref, u_ref, m_ref, acc_refs, low):
    def sweep(quad, _):
        pairs = [u_ref[2 * quad], u_ref[2 * quad + 1]]
        multiply_scatter(quad, cols_ref, pairs, m_ref, acc_refs, low)
        return 0

    lax.fori_loop(0, cols_ref.shape[1] // QUAD, sweep, 0, unroll=32)


def write_hot(hot_ref, rows, part):
    start = pl.multiple_of(part * LANES, LANES)
    names = lax.broadcasted_iota(jnp.int32, (LANES, LANES), 0) + part * LANES
    names = names.astype(F32)
    for tile, row in enumerate(rows):
        hot_ref[pl.ds(start, LANES), tile * LANES : (tile + 1) * LANES] = jnp.where(
            names == row, 1.0, 0.0
        ).astype(BF16)


def window_kernel(
    cols_ref, send_ref, columns_ref, patch_ref, names_ref, patches_ref, g0, g1, g2, g3,
    v_ref, m_ref, hot_ref, o0, o1, o2, o3, vector_ref,
):
    ghosts = (g0, g1, g2, g3)
    capacity = send_ref.shape[2]
    half = capacity // 2
    blocks = cols_ref.shape[1]
    low8 = low_half((8, LANES))
    sub = lax.broadcasted_iota(jnp.int32, (8, LANES), 0)
    lane = lax.broadcasted_iota(jnp.int32, (8, LANES), 1)

    listed = []
    there = jnp.zeros((8, LANES), F32)
    for group, ref in enumerate(ghosts):
        digits = ref[ref.shape[0] - 1].astype(F32)
        listed.append(digits[0:1] * RADIX + digits[8:9])
        taken = jnp.take_along_axis(
            jnp.broadcast_to(listed[-1], (8, LANES)), (lane % capacity) * 4 + sub % 4, axis=1
        )
        there = jnp.where(lane // capacity == group, taken, there)
    here = patches_ref[...]
    rows = [patch_ref[...].astype(F32)] + [names_ref[tile : tile + 1] for tile in range(4)]
    for tile in range(2):
        rows.append(
            jnp.where(low8[:1], listed[2 * tile], swap_halves(listed[2 * tile + 1]))
        )

    def spread(pair, value):
        other = swap_halves(value)
        vector_ref[2 * pair] = jnp.where(low8, value, other)
        vector_ref[2 * pair + 1] = jnp.where(low8, other, value)

    for pair in range(blocks // 2):
        spread(pair, v_ref[pair])
    for group, ref in enumerate(ghosts):
        for tile in range(half // 2):
            both = ref[half + tile].astype(F32)
            for side in range(2):
                pair = blocks // 2 + group * half + 2 * tile + side
                spread(pair, both[8 * side : 8 * side + 8])

    own = (sub < 4) == low8
    nothing = jnp.zeros((8, LANES), F32)
    low = low_half((16, LANES))
    columns = jnp.concatenate([columns_ref[...], columns_ref[...]], axis=0)
    sub16 = lax.broadcasted_iota(jnp.int32, (16, LANES), 0)
    for group, ref in enumerate((o0, o1, o2, o3)):
        slots = [jnp.maximum(send_ref[0, group, slot], 0) for slot in range(capacity)]
        for four in range(capacity // QUAD):
            lhs = []
            rhs = []
            for block in slots[four * QUAD : (four + 1) * QUAD]:
                a0, a1, a2, a3 = (vector_ref[cols_ref[k, block]] for k in range(4))
                left = jnp.where(own, jnp.where(sub < 4, a0, a1), nothing)
                right = jnp.where(own, jnp.where(sub < 4, a2, a3), nothing)
                lhs.append(
                    jnp.concatenate(
                        [
                            jnp.concatenate([left, nothing], axis=0),
                            jnp.concatenate([nothing, right], axis=0),
                        ],
                        axis=1,
                    ).astype(BF16)
                )
                rhs.append(m_ref[block])
            out = lax.dot_general(
                jnp.concatenate(lhs, axis=0),
                jnp.concatenate(rhs, axis=0),
                (((1,), (1,)), ((), ())),
                preferred_element_type=F32,
            )
            for side, value in enumerate(own_pairs(out, 16, low)):
                ref[2 * four + side] = value.astype(BF16)
        digits = jnp.zeros((16, LANES), F32)
        for tile in range(2):
            places = jnp.zeros((8, LANES), jnp.int32)
            for slot in range(half):
                places = jnp.where(lane // 16 == slot, slots[tile * half + slot], places)
            taken = jnp.take_along_axis(columns, places, axis=1).astype(F32)
            mine = jnp.sum(
                jnp.where(sub == (lane % 16) // 4, taken, 0.0), axis=0, keepdims=True
            )
            mine = jnp.broadcast_to(mine, (8, LANES)).astype(jnp.int32)
            taken = jnp.where(
                mine < LANES,
                jnp.take_along_axis(here, jnp.minimum(mine, LANES - 1), axis=1),
                jnp.take_along_axis(there, jnp.maximum(mine - LANES, 0), axis=1),
            )
            patch = jnp.sum(jnp.where(sub == lane % 4, taken, 0.0), axis=0, keepdims=True)
            patch = patch.astype(jnp.int32)
            digits = jnp.where(
                sub16 == 2 * tile,
                (patch // RADIX).astype(F32),
                jnp.where(sub16 == 2 * tile + 1, (patch % RADIX).astype(F32), digits),
            )
        ref[half] = digits.astype(BF16)

    def one(part, _):
        write_hot(hot_ref, rows, part)
        return 0

    lax.fori_loop(0, hot_ref.shape[0] // LANES, one, 0, unroll=2)


def last_kernel(
    z_ref, y_ref, v_ref, v0, v1, v2, v3, x0, x1, x2, x3,
    hot_ref, terms_ref, got_ref, out_ref,
):
    pert = z_ref.shape[1]
    local_pairs = v_ref.shape[0]
    half = (z_ref.shape[0] - local_pairs) // 4
    parts = got_ref.shape[0]
    low8 = low_half((8, LANES))
    low = low_half((16, LANES))
    sub = lax.broadcasted_iota(jnp.int32, (8, LANES), 0)
    own = (sub < 4) == low8
    nothing = jnp.zeros((8, LANES), F32)
    zero = jnp.zeros((16, LANES), F32)

    def wide(left, right):
        return jnp.concatenate([left, right], axis=1)

    def product(lhs, rhs):
        return lax.dot_general(
            lhs, rhs.astype(BF16), (((1,), (1,)), ((), ())), preferred_element_type=F32
        )

    def first_level(first, second):
        return jnp.concatenate(
            [
                wide(jnp.where(own, first, nothing), nothing),
                wide(nothing, jnp.where(own, second, nothing)),
            ],
            axis=0,
        )

    def second_level(first, second):
        return jnp.concatenate(
            [
                wide(jnp.where(low, first, zero), zero),
                wide(jnp.where(low, zero, first), zero),
                wide(zero, jnp.where(low, second, zero)),
                wide(zero, jnp.where(low, zero, second)),
            ],
            axis=0,
        )

    pieces = [terms_ref[...]]
    for pair in range(0, local_pairs, 2):
        lhs = wide(z_ref[pair], z_ref[pair + 1])
        pieces.append(product(lhs, first_level(v_ref[pair], v_ref[pair + 1])))
    for group, ref in enumerate((v0, v1, v2, v3)):
        for tile in range(half // 2):
            both = ref[half + tile].astype(F32)
            pair = local_pairs + group * half + 2 * tile
            lhs = wide(z_ref[pair], z_ref[pair + 1])
            pieces.append(product(lhs, first_level(both[:8], both[8:])))
    rows = []
    for group, ref in enumerate((x0, x1, x2, x3)):
        for tile in range(half // 2):
            pair = group * half + 2 * tile
            lhs = wide(y_ref[pair], y_ref[pair + 1])
            first, second = (ref[2 * tile + side].astype(F32) for side in range(2))
            pieces.append(product(lhs, second_level(first, second)))
        digits = ref[half].astype(F32)
        for tile in range(2):
            rows.append(
                digits[2 * tile : 2 * tile + 1] * RADIX + digits[2 * tile + 1 : 2 * tile + 2]
            )
    terms = jnp.concatenate(pieces, axis=1)
    top = terms.astype(BF16)
    rest = (terms - top.astype(F32)).astype(BF16)
    both = jnp.concatenate([top, rest], axis=0)
    mine = lax.axis_index("pert")
    sub16 = lax.broadcasted_iota(jnp.int32, (pert, LANES), 0)
    perts = out_ref.shape[0] // parts
    first_names = lax.broadcasted_iota(jnp.int32, (LANES, LANES), 0).astype(F32)
    for part in range(parts):
        hot = jnp.concatenate(
            [hot_ref[part * LANES : (part + 1) * LANES, :]]
            + [
                jnp.where(first_names == row - part * LANES, 1.0, 0.0).astype(BF16)
                for row in rows
            ],
            axis=1,
        )
        out = lax.dot_general(both, hot, (((1,), (1,)), ((), ())), preferred_element_type=F32)
        value = out[:pert] + out[pert:]
        curve = jnp.sum(value * got_ref[part, :pert], axis=0, keepdims=True)
        top = curve.astype(BF16).astype(F32)
        extra = jnp.where(sub16 == 0, top, jnp.where(sub16 == 1, curve - top, 0.0))
        for place in range(perts):
            out_ref[part * perts + place] = jnp.where(place == mine, value, extra).astype(BF16)


def owner_kernel(terms_ref, probe_ref, hessian_ref, curve_ref, *, parts, scale):
    perts = terms_ref.shape[0] // parts
    mine = lax.axis_index("pert")
    total = jnp.zeros(hessian_ref.shape, F32)
    every = jnp.zeros(hessian_ref.shape, F32)
    for part in range(parts):
        total = total + terms_ref[part * perts + mine].astype(F32)
        for place in range(perts):
            value = terms_ref[part * perts + place].astype(F32)
            every = every + jnp.where(place == mine, 0.0, value)
    hessian_ref[...] = total
    own = jnp.sum(total * probe_ref[...], axis=0, keepdims=True)
    curve_ref[...] = (own + every[0:1] + every[1:2]) * scale


def call(body, outs, spaces, scratch=(), name=None, flops=0, moved=1 << 20, limit=12, out_specs=None):
    return pl.pallas_call(
        body,
        out_shape=outs,
        in_specs=[{"s": SMEM, "v": VMEM, "h": HBM}[s] for s in spaces],
        out_specs=out_specs or jax.tree.map(lambda _: VMEM, outs),
        scratch_shapes=list(scratch),
        compiler_params=pltpu.CompilerParams(vmem_limit_bytes=limit * MIB),
        name=name,
        cost_estimate=pl.CostEstimate(flops=flops, transcendentals=0, bytes_accessed=moved),
    )


def shards(
    probes, melt_shape, obs_weight, diag_inverse, coupling, columns, send_list, patch_of_block
):
    pert = probes.shape[0]
    blocks = coupling.shape[0]
    capacity = send_list.shape[2]
    parts = lax.axis_size("dom")
    pairs = blocks // 2
    shape = jax.ShapeDtypeStruct
    msgs = [shape((capacity // 2, pert, LANES), BF16)] * 4
    pair_array = shape((pairs, pert, LANES), F32)
    block_array = shape((blocks, pert, LANES), BF16)
    ext = pltpu.VMEM((blocks + 4 * capacity, pert, LANES), BF16)
    accs = [pltpu.VMEM((blocks + 4 * capacity, pert, LANES), F32)] * 4
    held = pltpu.VMEM((pairs, pert, LANES), F32)
    melt = melt_shape.reshape(pairs, LANES)
    weight = obs_weight.reshape(pairs, LANES)
    patch = patch_of_block.reshape(1, blocks)

    perts = lax.axis_size("pert")
    columns = columns.T
    w, outgoing = call(
        functools.partial(melt_kernel, parts=parts),
        [shape((pairs, LANES), F32), shape((parts, pert + capacity // 2 + 8, LANES), F32)],
        "hhhhh",
        [
            pltpu.SMEM(send_list.shape, jnp.int32),
            pltpu.VMEM((pairs, LANES), F32),
            pltpu.VMEM((1, blocks), jnp.int32),
            pltpu.VMEM(probes.shape, F32),
            pltpu.VMEM((HALF, HALF, blocks), BF16),
            pltpu.SemaphoreType.DMA((5,)),
        ],
        name="melt",
        limit=60,
    )(send_list, melt, patch, probes, jnp.transpose(diag_inverse, (1, 2, 0)))
    got = lax.all_to_all(outgoing, "dom", 0, 0, tiled=True)
    wide = [shape((capacity // 2 + capacity // 4 + 1, pert, LANES), BF16)] * 4
    m, v, names, patches, t1, state, *out = call(
        first_kernel,
        [
            shape(coupling.shape, BF16),
            shape((pairs, 8, LANES), F32),
            shape((8, LANES), F32),
            shape((8, LANES), F32),
            pair_array,
            block_array,
        ]
        + wide,
        "ssvvvhvh",
        [
            ext,
            pltpu.VMEM((blocks + 4 * capacity, LANES), F32),
            pltpu.VMEM((pairs, LANES), F32),
            pltpu.VMEM(coupling.shape, BF16),
            pltpu.SemaphoreType.DMA,
            pltpu.SemaphoreType.DMA((8,)),
        ],
        name="first",
        limit=46,
    )(columns, send_list, patch, columns, got, w, diag_inverse, coupling)
    carried = [rotated(x, o) for x, o in zip(out, OFFSET_LIST)]
    state, *out = call(
        sweep_kernel, [block_array] + msgs, "ssvvvvvvv", [ext], name="sweep"
    )(columns, send_list, t1, state, *carried, m)
    ghosts = [rotated(v, o) for v, o in zip(out, OFFSET_LIST)]
    hot, *far = call(
        window_kernel,
        [shape((parts * LANES, 7 * LANES), BF16)]
        + [shape((capacity // 2 + 1, pert, LANES), BF16)] * 4,
        "ss" + "v" * 10,
        [pltpu.VMEM((blocks + 4 * capacity, 8, LANES), F32)],
        name="window",
        moved=4 << 20,
    )(columns, send_list, columns, patch, names, patches, *carried, v, m)
    far, ghosts = lax.optimization_barrier((far, ghosts))
    far = [rotated(x, o) for x, o in zip(far, OFFSET_LIST)]
    tangent, terms, z, y = call(
        turn_kernel,
        [
            shape((pert, blocks * HALF), F32),
            shape((pert, LANES), F32),
            shape((pairs + 2 * capacity, pert, LANES), BF16),
            shape((2 * capacity, pert, LANES), BF16),
        ],
        "s" + "v" * 9,
        [
            ext,
            pltpu.VMEM((pert, blocks * HALF), F32),
            held,
            held,
            pltpu.SemaphoreType.DMA,
        ]
        + accs,
        name="turn",
        moved=16 << 20,
        out_specs=[HBM, VMEM, VMEM, VMEM],
    )(columns, t1, state, *ghosts, m, weight, w)
    terms = call(
        last_kernel, shape((parts * perts, pert, LANES), BF16), "v" * 14, name="last"
    )(z, y, v, *carried, *far, hot, terms, got)
    terms = lax.all_to_all(terms, ("dom", "pert"), 0, 0, tiled=True)
    hessian_probe, curvature = call(
        functools.partial(owner_kernel, parts=parts, scale=1.0 / (pert * perts)),
        [shape(probes.shape, F32), shape((1, LANES), F32)],
        "vv",
        name="owner",
    )(terms, probes)
    return tangent, hessian_probe, curvature.reshape(-1)


def solution(mesh):
    in_specs = (
        P("pert", "dom"),
        P("dom"),
        P("dom"),
        P("dom", None, None),
        P("dom", None, None),
        P("dom", None),
        P("dom", None, None),
        P("dom"),
    )
    out_specs = (P("pert", "dom"), P("pert", "dom"), P("dom"))
    return jax.shard_map(shards, mesh=mesh, in_specs=in_specs, out_specs=out_specs, check_vma=False)
```
